32 devices in a mesh: rows: 4 (over y, core), chan: 8 (over z, x).
Axes of the slice: x: 2, y: 2, z: 4, core: 2. Of those that a mesh axis runs over, the one named last changes fastest.
Arguments:
- hidden_in: bfloat16 [4, 1024, 512], P('rows', 'chan'), may hold values from -6 to 6
- segments: int32 [4, 1024], P('rows'), may hold values from 0 to 3, never falling along the last dimension, each value on 1 to 512 neighbouring positions
- filters: bfloat16 [24, 1024], replicated, may hold values from -0.1875 to 0.1875
- gain_one: float32 [512], replicated, may hold values from 0.1 to 1.9
- mixing: bfloat16 [51, 512, 512], P(None, 'chan'), may hold values from -0.0390625 to 0.0390625
- gain_two: float32 [512], replicated, may hold values from 0.1 to 1.9
- w_gate: bfloat16 [512, 2048], replicated, may hold values from -0.25 to 0.25
- w_up: bfloat16 [512, 2048], replicated, may hold values from -0.25 to 0.25
- w_down: bfloat16 [2048, 512], replicated, may hold values from -0.125 to 0.125
- out_grad: bfloat16 [4, 1024, 512], P('rows', 'chan'), may hold values from -6 to 6
Outputs:
- output: bfloat16 [4, 1024, 512], P('rows', 'chan')
- input_grad: float32 [4, 1024, 512], P('rows', 'chan')
- mixing_grad: float32 [51, 512, 512], P(None, 'chan')
- gate_grad: float32 [512, 2048], P(None, 'chan')
- up_grad: float32 [512, 2048], P(None, 'chan')
- down_grad: float32 [2048, 512], P('chan')
- gain_one_grad: float32 [512], P('chan')
- gain_two_grad: float32 [512], P('chan')
The draws below stay inside these ranges and needn't reach their ends.
Inputs may be any that keep to these rules, and one draw needn't show every extreme that they name: `segments`: along each row the numbers never fall; each of the 4 numbers covers 1 to 512 consecutive positions, and one covers exactly 512.
All inputs are finite; a program needn't handle non-finite values.
Results may differ from the reference program's by a relative error of at most 0.025.
Values may be sent and summed in bfloat16 or wider, within the bound.
No kernel may reach another device: no remote copies, remote signals or barrier semaphores. Data moves between devices by JAX's collectives and lax.ppermute only.
A program may use at most 320 MiB of HBM per device.

```python
import math
import jax
import jax.numpy as jnp
import numpy as np
from jax import lax

D = 512
FF = 2048
K = 24
AR = 3
SEGS = 4
ROW = 1024
ROWS = 4


def raised(values, key, source, target, shards_of, factor):
    def block_of(dim):
        return (jnp.arange(values.shape[dim]) // (values.shape[dim] // shards_of)).reshape((-1,) + (1,) * (values.ndim - 1 - dim))

    near = jax.random.permutation(key, shards_of)[block_of(target)]
    other_side = (block_of(target) + shards_of // 2) % shards_of
    return jnp.where((block_of(source) == near) | (block_of(source) == other_side), factor * values, values)


def block_levels(rng, dims, shards, low, high):
    def one(position, parts):
        heights = jax.random.uniform(jax.random.fold_in(jax.random.fold_in(rng, 6), position), (parts,), jnp.float32, low / len(shards), high / len(shards))
        return jnp.repeat(jnp.exp(heights), dims[position] // parts).reshape((-1,) + (1,) * (len(dims) - position - 1))

    loudness = one(*shards[0])
    for cut in shards[1:]:
        loudness = loudness * one(*cut)
    return loudness


def split_up(count, total, bound, slope):
    weights = [(1 << 20) // math.isqrt(grade ** slope) + 1 for grade in range(2, count + 1)]
    rest, counts = total - bound - (count - 1), [1] * (count - 1)
    while rest > 0:
        candidates = [i for i in range(count - 1) if counts[i] < bound]
        pool, remaining = sum([weights[i] for i in candidates]), rest
        for i in candidates:
            more = min(bound - counts[i], max(1, remaining * weights[i] // pool), rest)
            counts[i] = counts[i] + more
            rest = rest - more
    return np.array([bound] + counts)


def ragged_sizes(own_key, number_of, total, bound, skew):
    if number_of == 2:
        one = jax.random.randint(own_key, (), max(1, total - bound), min(bound, total - 1) + 1)
        return jnp.stack([one, total - one])
    lengths = jnp.asarray(split_up(number_of, total, bound, skew), jnp.int32)
    couples = (number_of - 1) // 2
    source_of, receiver = lengths[1:1 + 2 * couples:2], lengths[2:2 + 2 * couples:2]
    room = jnp.minimum(source_of - 1, bound - receiver)
    passed = jax.random.randint(jax.random.fold_in(own_key, 1), (couples,), 0, 1 << 20) % (room + 1)
    lengths = lengths.at[1:1 + 2 * couples:2].set(source_of - passed).at[2:2 + 2 * couples:2].set(receiver + passed)
    return lengths[jax.random.permutation(jax.random.fold_in(own_key, 2), number_of)]


def scatter_about(rng, extent, deviation, most, shards=(), held_as=jnp.bfloat16):
    result = deviation * jax.random.normal(rng, extent, jnp.float32)
    if shards:
        result = result * block_levels(rng, extent, shards, -0.22, 0.18)
    return jnp.clip(result, -most, most).astype(held_as)


def gaussian_with(own_key, dims, scale, limit, pieces, heavy, kind=jnp.bfloat16):
    entries = scale * jax.random.normal(own_key, dims, jnp.float32)
    if pieces:
        entries = entries * block_levels(own_key, dims, pieces, -0.22, 0.18)
    return jnp.clip(raised(entries, jax.random.fold_in(own_key, 3), *heavy), -limit, limit).astype(kind)


def setup_inputs(seed: int = 0) -> dict:
    seeds = jax.random.split(jax.random.key(seed), 11)
    return {
        "hidden_in": scatter_about(seeds[0], (ROWS, ROW, D), 1.0, 6.0, ((0, 4), (1, 8))),
        "segments": jax.vmap(lambda own: jnp.searchsorted(jnp.cumsum(ragged_sizes(own, SEGS, ROW, ROW // 2, 0)), jnp.arange(ROW), side="right"))(jax.random.split(seeds[1], ROWS)).reshape((ROWS, ROW)).astype(jnp.int32),
        "filters": scatter_about(seeds[2], (K, ROW), ROW ** -0.5, 0.1875),
        "gain_one": jnp.clip(1.0 + 0.18 * jax.random.normal(seeds[3], (D,), jnp.float32), 0.1, 1.9),
        "mixing": scatter_about(seeds[4], (2 * K + AR, D, D), ((2 * K + AR) * D) ** -0.5, 0.0390625, ((1, 8),)),
        "gain_two": jnp.clip(1.0 + 0.18 * jax.random.normal(seeds[5], (D,), jnp.float32), 0.1, 1.9),
        "w_gate": scatter_about(seeds[6], (D, FF), D ** -0.5, 0.25),
        "w_up": scatter_about(seeds[7], (D, FF), D ** -0.5, 0.25),
        "w_down": scatter_about(seeds[8], (FF, D), FF ** -0.5, 0.125),
        "out_grad": gaussian_with(seeds[9], (ROWS, ROW, D), 1.0, 6.0, ((0, 4), (1, 8)), (1, 2, 8, 2.0)),
    }


@jax.custom_vjp
def low(v):
    return lax.optimization_barrier(v.astype(jnp.bfloat16)).astype(jnp.float32)

@jax.custom_vjp
def low_back(v):
    return v

def low_keep(v):
    return (low(v), None)

def low_pass(kept, grad):
    return (grad,)

def back_keep(v):
    return (v, None)

def back_low(kept, grad):
    return (low(grad),)
low.defvjp(low_keep, low_pass)
low_back.defvjp(back_keep, back_low)
eps_norm = 1e-05

def matmul(left, right):
    return jnp.dot(left, right, precision=lax.Precision.HIGHEST, preferred_element_type=jnp.float32)

def rms_scale(values, scales):
    return values * lax.rsqrt(lax.optimization_barrier(jnp.mean(values * values, axis=-1, keepdims=True)) + eps_norm) * scales

def row_forward(row_tokens, row_segments, gain_one, mixing, gain_two, w_gate, w_up, w_down, filters):
    length = row_tokens.shape[0]
    normed_in = low_back(low(rms_scale(row_tokens, gain_one)))
    parity = 1.0 - 2.0 * (jnp.arange(length) % 2).astype(jnp.float32)
    doubled = jnp.concatenate([normed_in, parity[:, None] * normed_in], axis=1)
    onehot = (row_segments[None, :] == jnp.arange(SEGS, dtype=jnp.int32)[:, None]).astype(jnp.float32)
    spectra = jnp.fft.rfft(onehot[:, :, None] * doubled[None], n=2 * length, axis=1)

    def per_filter(mixed_sum, filter_item):
        response_in, plus_weight, minus_weight = filter_item
        response = jnp.fft.rfft(response_in, n=2 * length)
        convolved = jnp.fft.irfft(spectra * response[None, :, None], n=2 * length, axis=1)[:, :length]
        filtered = lax.optimization_barrier(jnp.sum(onehot[:, :, None] * convolved, axis=0))
        plus_maps = low_back(low(filtered[:, :D]))
        minus_maps = low_back(low(parity[:, None] * filtered[:, D:]))
        return (mixed_sum + matmul(plus_maps, plus_weight) + matmul(minus_maps, minus_weight), None)
    start_sum = jnp.zeros((length, D), jnp.float32)
    mixed_sum, _ = lax.scan(jax.checkpoint(per_filter), start_sum, (filters, mixing[:K], mixing[K:2 * K]))
    for offset in range(AR):
        shifted = jnp.concatenate([jnp.zeros((offset, D), jnp.float32), normed_in[:length - offset]], axis=0)
        before = jnp.concatenate([jnp.full((offset,), -1, jnp.int32), row_segments[:length - offset]])
        same = (before == row_segments).astype(jnp.float32)
        mixed_sum = mixed_sum + matmul(shifted * same[:, None], mixing[2 * K + offset])
    mixed = low_back(mixed_sum)
    resid = row_tokens + mixed
    normed_two = low(rms_scale(resid, gain_two))
    gate_value = low_back(matmul(normed_two, w_gate))
    upper_value = low_back(matmul(normed_two, w_up))
    hidden = low(jax.nn.gelu(gate_value, approximate=True) * upper_value)
    return resid + matmul(hidden, w_down)

def reference(hidden_in, segments, filters, gain_one, mixing, gain_two, w_gate, w_up, w_down, out_grad):
    filter_values = filters.astype(jnp.float32)

    def forward(tokens, first_gain, mix_weights, second_gain, gate_weights, up_weights, down_weights):

        def one_row(row_pair):
            return row_forward(row_pair[0], row_pair[1], first_gain, mix_weights, second_gain, gate_weights, up_weights, down_weights, filter_values)
        return lax.map(jax.checkpoint(one_row), (tokens, segments))
    output, pull = jax.vjp(forward, hidden_in.astype(jnp.float32), gain_one, mixing.astype(jnp.float32), gain_two, w_gate.astype(jnp.float32), w_up.astype(jnp.float32), w_down.astype(jnp.float32))
    input_grad, gain_one_grad, mixing_grad, gain_two_grad, gate_grad, up_grad, down_grad = pull(out_grad.astype(jnp.float32))
    return (output.astype(jnp.bfloat16), input_grad, mixing_grad, gate_grad, up_grad, down_grad, gain_one_grad, gain_two_grad)
```

```python
import functools

import jax
import jax.numpy as jnp
from jax import lax
from jax.experimental import pallas as pl
from jax.experimental.pallas import tpu as pltpu
from jax.sharding import PartitionSpec as P

K = 24
AR = 3
TILE = 256
HALF = 128
PER_STEP = 4

eps_norm = 1e-05


def rms_scale(values, scales):
    return values * lax.rsqrt(jnp.mean(values * values, axis=-1, keepdims=True) + eps_norm) * scales


def gelu_product(gate_value, upper_value):
    return jax.nn.gelu(gate_value, approximate=True) * upper_value


def contract_first(left, right):
    return lax.dot_general(
        left, right, (((0,), (0,)), ((), ())), preferred_element_type=jnp.float32
    )


def contract_last(left, right):
    return lax.dot_general(
        left, right, (((1,), (1,)), ((), ())), preferred_element_type=jnp.float32
    )


def tile_pairs(length):
    blocks, reach = length // TILE, length // 2 // TILE
    return [(tb, sb) for tb in range(blocks) for sb in range(max(0, tb - reach), tb + 1)]


def parity_lanes(rows, lanes, dtype=jnp.float32):
    lane = lax.broadcasted_iota(jnp.int32, (rows, lanes), 1)
    return (1 - 2 * (lane % 2)).astype(dtype)


def build_masks(seg_row, seg_col, masks, length):
    for index, (tb, sb) in enumerate(tile_pairs(length)):
        targets = seg_row[:, tb * TILE : (tb + 1) * TILE]
        sources = seg_col[sb * TILE : (sb + 1) * TILE, :]
        same = sources == targets
        if tb == sb:
            row = lax.broadcasted_iota(jnp.int32, (TILE, TILE), 0)
            col = lax.broadcasted_iota(jnp.int32, (TILE, TILE), 1)
            same = same & (col >= row)
        masks[index] = jnp.where(same, 1.0, 0.0).astype(jnp.bfloat16)


def build_slab(filter_row, slab, width):
    wide = jnp.broadcast_to(filter_row.astype(jnp.float32), (HALF, width))
    rolled = pltpu.roll(wide, 0, 1, stride=1, stride_axis=0).astype(jnp.bfloat16)
    slab[:HALF, :] = rolled
    slab[HALF:, HALF:] = rolled[:, : width - HALF]
    slab[HALF:, :HALF] = rolled[:, :HALF]


def spectral_kernel(length, width, filters, doubled, seg_row, seg_col, maps, slabs, masks):
    channels = maps.shape[2]
    pairs = tile_pairs(length)

    @pl.when(pl.program_id(0) == 0)
    def _():
        build_masks(seg_row, seg_col, masks, length)

    parity = parity_lanes(channels, TILE)
    for k in range(PER_STEP):
        slab = slabs.at[k]
        build_slab(filters[k], slab, width)
        for tb in range(length // TILE):
            chosen = [(i, sb) for i, (t, sb) in enumerate(pairs) if t == tb]
            tiles = [
                slab[:, (tb - sb) * TILE : (tb - sb + 1) * TILE] * masks[i] for i, sb in chosen
            ]
            first = chosen[0][1]
            both = jnp.dot(
                doubled[:, first * TILE : (tb + 1) * TILE],
                jnp.concatenate(tiles, axis=0),
                preferred_element_type=jnp.float32,
            )
            maps[0, k, :, tb * TILE : (tb + 1) * TILE] = both[:channels].astype(jnp.bfloat16)
            maps[1, k, :, tb * TILE : (tb + 1) * TILE] = (both[channels:] * parity).astype(
                jnp.bfloat16
            )


def spectral_back_kernel(length, width, filters, grads, seg_row, seg_col, out, slabs, masks, acc):
    channels = grads.shape[2]
    pairs = tile_pairs(length)

    @pl.when(pl.program_id(0) == 0)
    def _():
        build_masks(seg_row, seg_col, masks, length)
        acc[...] = jnp.zeros_like(acc)

    parity = parity_lanes(channels, length, jnp.bfloat16)
    for k in range(PER_STEP):
        slab = slabs.at[k]
        build_slab(filters[k], slab, width)
        both = jnp.concatenate([grads[0, k], grads[1, k] * parity], axis=0)
        for sb in range(length // TILE):
            chosen = [(i, tb) for i, (tb, s) in enumerate(pairs) if s == sb]
            tiles = [
                slab[:, (tb - sb) * TILE : (tb - sb + 1) * TILE] * masks[i] for i, tb in chosen
            ]
            last = chosen[-1][1]
            acc[:, sb * TILE : (sb + 1) * TILE] += contract_last(
                both[:, sb * TILE : (last + 1) * TILE], jnp.concatenate(tiles, axis=1)
            )

    @pl.when(pl.program_id(0) == pl.num_programs(0) - 1)
    def _():
        out[...] = acc[:channels] + parity.astype(jnp.float32) * acc[channels:]


def slab_width(length):
    return length // 2 + TILE


def common_specs(filters, segment_ids):
    length = filters.shape[1]
    width = slab_width(length)
    specs = [
        pl.BlockSpec((PER_STEP, 1, width), lambda k: (k, 0, 0)),
    ]
    masks = pltpu.VMEM((len(tile_pairs(length)), TILE, TILE), jnp.bfloat16)
    slabs = pltpu.VMEM((PER_STEP, TILE, width), jnp.bfloat16)
    segs = [
        pl.BlockSpec((1, length), lambda k: (0, 0)),
        pl.BlockSpec((length, 1), lambda k: (0, 0)),
    ]
    return length, width, specs, segs, slabs, masks


def spectral_maps(doubled, filters, segment_ids):
    length, width, specs, segs, slabs, masks = common_specs(filters, segment_ids)
    channels = doubled.shape[0] // 2
    count = filters.shape[0]
    return pl.pallas_call(
        functools.partial(spectral_kernel, length, width),
        grid=(count // PER_STEP,),
        in_specs=[*specs, pl.BlockSpec((2 * channels, length), lambda k: (0, 0)), *segs],
        out_specs=pl.BlockSpec((2, PER_STEP, channels, length), lambda k: (0, k, 0, 0)),
        out_shape=jax.ShapeDtypeStruct((2, count, channels, length), jnp.bfloat16),
        scratch_shapes=[slabs, masks],
        compiler_params=pltpu.CompilerParams(vmem_limit_bytes=40 << 20),
        name="spectral_maps",
    )(filters[:, None, :], doubled, segment_ids[None, :], segment_ids[:, None])


def spectral_back(grads, filters, segment_ids):
    length, width, specs, segs, slabs, masks = common_specs(filters, segment_ids)
    channels = grads.shape[2]
    count = filters.shape[0]
    return pl.pallas_call(
        functools.partial(spectral_back_kernel, length, width),
        grid=(count // PER_STEP,),
        in_specs=[
            *specs,
            pl.BlockSpec((2, PER_STEP, channels, length), lambda k: (0, k, 0, 0)),
            *segs,
        ],
        out_specs=pl.BlockSpec((channels, length), lambda k: (0, 0)),
        out_shape=jax.ShapeDtypeStruct((channels, length), jnp.float32),
        scratch_shapes=[slabs, masks, pltpu.VMEM((2 * channels, length), jnp.float32)],
        compiler_params=pltpu.CompilerParams(vmem_limit_bytes=40 << 20),
        name="spectral_back",
    )(filters[:, None, :], grads, segment_ids[None, :], segment_ids[:, None])


def same_mask(segment_ids, offset):
    length = segment_ids.shape[0]
    before = jnp.concatenate([jnp.full((offset,), -1, jnp.int32), segment_ids[: length - offset]])
    return before == segment_ids


def swap(values, axis, mask):
    count = lax.axis_size(axis)
    return lax.ppermute(values, axis, [(i, i ^ mask) for i in range(count)])


def bits_of(axis):
    return [1 << b for b in range(lax.axis_size(axis).bit_length() - 1)]


def join(mine, other, high, dim):
    return jnp.where(
        high, jnp.concatenate([other, mine], dim), jnp.concatenate([mine, other], dim)
    )


def doubled_gather(values, order):
    me = lax.axis_index("chan")
    held = values[None]
    sizes = []
    for mask in order:
        held = join(held[None], swap(held, "chan", mask)[None], (me & mask) != 0, 0)
        held = held.reshape(-1, *values.shape)
        sizes.insert(0, mask)
    bits = len(order)
    split = held.reshape(*([2] * bits), *values.shape)
    place = [sizes.index(m) for m in sorted(order, reverse=True)]
    split = jnp.transpose(split, place + list(range(bits, split.ndim)))
    return split.reshape(-1, *values.shape)


def gather_tokens(values):
    masks = bits_of("chan")
    half = values.shape[0] // 2
    first = doubled_gather(values[:half], masks[::-1])
    second = doubled_gather(values[half:], masks[:1] + masks[:0:-1])
    return jnp.concatenate([first, second], axis=1).reshape(-1, values.shape[1])


def halved_sum(values, order):
    me = lax.axis_index("chan")
    masks = bits_of("chan")[::-1]
    held = values.reshape(*([2] * len(masks)), *values.shape[1:])
    for mask in order:
        dim, bit = masks.index(mask), (me & mask) // mask
        keep = lax.dynamic_slice_in_dim(held, bit, 1, dim)
        give = lax.dynamic_slice_in_dim(held, 1 - bit, 1, dim)
        got = swap(give, "chan", mask)
        held = keep.astype(jnp.float32) + got.astype(jnp.float32)
        if mask != order[-1]:
            held = held.astype(jnp.bfloat16)
    return held.reshape(values.shape[1:])


def scatter_tokens(values):
    count = lax.axis_size("chan")
    masks = bits_of("chan")
    pieces = values.reshape(count, -1, values.shape[1])
    half = values.shape[1] // 2
    return jnp.concatenate(
        [
            halved_sum(pieces[..., :half], masks[:1] + masks[1:]),
            halved_sum(pieces[..., half:], masks[1:] + masks[:1]),
        ],
        axis=1,
    )


def sum_rows(values):
    me = lax.axis_index("rows")
    masks = bits_of("rows")
    half = values.shape[0] // 2
    high = (me & 1) != 0
    keep = lax.dynamic_slice_in_dim(values, (me & 1) * half, half, 0)
    give = lax.dynamic_slice_in_dim(values, (1 - (me & 1)) * half, half, 0)
    held = keep.astype(jnp.float32) + swap(give, "rows", 1).astype(jnp.float32)
    for mask in masks[1:]:
        held = held.astype(jnp.bfloat16)
        held = held.astype(jnp.float32) + swap(held, "rows", mask).astype(jnp.float32)
    held = held.astype(jnp.bfloat16)
    return join(held, swap(held, "rows", 1), high, 0)


def sum_rows_small(values):
    for mask in bits_of("rows"):
        values = values + swap(values, "rows", mask)
    return values


def shards(
    hidden_in, segments, filters, gain_one, mixing, gain_two, w_gate, w_up, w_down, out_grad
):
    chans = lax.axis_size("chan")
    me = lax.axis_index("chan")
    tokens = hidden_in[0].astype(jnp.float32)
    cotangent = out_grad[0]
    normed_one = rms_scale(tokens, gain_one).astype(jnp.bfloat16)
    share, width = normed_one.shape
    inputs = lax.all_to_all(
        normed_one.T.reshape(chans, width // chans, share), "chan", split_axis=0, concat_axis=0
    )
    inputs = jnp.swapaxes(inputs, 0, 1).reshape(width // chans, -1)
    segment_ids = segments[0]
    channels, length = inputs.shape
    model_width = mixing.shape[2]
    flat_mixing = mixing.reshape(-1, model_width)
    spectral_rows = 2 * K * channels
    parity = (1 - 2 * (lax.iota(jnp.int32, length) % 2)).astype(jnp.bfloat16)
    doubled = jnp.concatenate([inputs, inputs * parity], axis=0)
    maps = spectral_maps(doubled, filters, segment_ids).reshape(spectral_rows, length)
    lags = jnp.concatenate(
        [
            jnp.concatenate(
                [jnp.zeros((channels, j), jnp.bfloat16), inputs[:, : length - j]], axis=1
            )
            * same_mask(segment_ids, j).astype(jnp.bfloat16)
            for j in range(AR)
        ],
        axis=0,
    )
    mixed = contract_first(maps, flat_mixing[:spectral_rows]) + contract_first(
        lags, flat_mixing[spectral_rows:]
    )
    mixed = scatter_tokens(mixed.astype(jnp.bfloat16))
    resid = tokens + mixed
    normed_two = rms_scale(resid, gain_two).astype(jnp.bfloat16)
    gate_value = jnp.dot(normed_two, w_gate, preferred_element_type=jnp.float32)
    upper_value = jnp.dot(normed_two, w_up, preferred_element_type=jnp.float32)
    hidden = gelu_product(gate_value, upper_value).astype(jnp.bfloat16)
    output = (resid + jnp.dot(hidden, w_down, preferred_element_type=jnp.float32)).astype(
        jnp.bfloat16
    )
    hidden_grad = contract_last(cotangent, w_down)
    _, gelu_pull = jax.vjp(gelu_product, gate_value, upper_value)
    gate_float, upper_float = gelu_pull(hidden_grad)
    normed_grad = contract_last(gate_float.astype(jnp.bfloat16), w_gate) + contract_last(
        upper_float.astype(jnp.bfloat16), w_up
    )
    _, second_pull = jax.vjp(rms_scale, resid, gain_two)
    resid_part, second_local = second_pull(normed_grad)
    resid_grad = cotangent.astype(jnp.float32) + resid_part
    full_grad = gather_tokens(resid_grad.astype(jnp.bfloat16))
    all_normed = gather_tokens(normed_two)
    all_cotangent = gather_tokens(cotangent)
    units = w_gate.shape[1] // chans
    gate_part = lax.dynamic_slice_in_dim(w_gate, me * units, units, 1)
    up_part = lax.dynamic_slice_in_dim(w_up, me * units, units, 1)
    down_part = lax.dynamic_slice_in_dim(w_down, me * units, units, 0)
    gate_units = jnp.dot(all_normed, gate_part, preferred_element_type=jnp.float32)
    upper_units = jnp.dot(all_normed, up_part, preferred_element_type=jnp.float32)
    product, unit_pull = jax.vjp(gelu_product, gate_units, upper_units)
    gate_back, upper_back = unit_pull(contract_last(all_cotangent, down_part))
    gate_local = contract_first(all_normed, gate_back.astype(jnp.bfloat16))
    up_local = contract_first(all_normed, upper_back.astype(jnp.bfloat16))
    down_local = contract_first(product.astype(jnp.bfloat16), all_cotangent)
    ff_sum = sum_rows(
        jnp.concatenate(
            [gate_local.astype(jnp.bfloat16), up_local.astype(jnp.bfloat16)], axis=1
        )
    ).astype(jnp.float32)
    down_sum = sum_rows(down_local.astype(jnp.bfloat16)).astype(jnp.float32)

    spectral_grad = contract_last(flat_mixing[:spectral_rows], full_grad).astype(jnp.bfloat16)
    lag_grad = contract_last(flat_mixing[spectral_rows:], full_grad)
    input_back = spectral_back(
        spectral_grad.reshape(2, K, channels, length), filters, segment_ids
    )
    for j in range(AR):
        lag_term = lag_grad[j * channels : (j + 1) * channels]
        lag_term = lag_term * same_mask(segment_ids, j).astype(jnp.float32)
        input_back = input_back + jnp.concatenate(
            [lag_term[:, j:], jnp.zeros((channels, j), jnp.float32)], axis=1
        )
    back = input_back.astype(jnp.bfloat16)
    token_grad = lax.all_to_all(
        jnp.swapaxes(back.reshape(channels, chans, share), 0, 1),
        "chan",
        split_axis=0,
        concat_axis=0,
    ).reshape(width, share).T
    mixing_local = jnp.concatenate(
        [
            jnp.dot(maps, full_grad, preferred_element_type=jnp.float32).astype(jnp.bfloat16),
            jnp.dot(lags, full_grad, preferred_element_type=jnp.float32).astype(jnp.bfloat16),
        ],
        axis=0,
    )
    mixing_sum = sum_rows(mixing_local).astype(jnp.float32).reshape(mixing.shape)
    first_local = jnp.sum(back.astype(jnp.float32) * inputs.astype(jnp.float32), axis=1)
    first_local = first_local / lax.dynamic_slice_in_dim(gain_one, me * channels, channels, 0)
    second_pieces = lax.all_to_all(
        second_local.reshape(chans, 1, channels), "chan", split_axis=0, concat_axis=0
    )
    gains = sum_rows_small(jnp.stack([first_local, jnp.sum(second_pieces, axis=(0, 1))]))
    _, first_pull = jax.vjp(rms_scale, tokens, gain_one)
    tokens_part, _ = first_pull(token_grad.astype(jnp.float32))
    input_total = resid_grad + tokens_part
    return (
        output[None],
        input_total[None],
        mixing_sum,
        ff_sum[:, :units],
        ff_sum[:, units:],
        down_sum,
        gains[0],
        gains[1],
    )


def solution(mesh):
    in_specs = (
        P("rows", "chan", None),
        P("rows", None),
        P(),
        P(),
        P(None, "chan", None),
        P(),
        P(),
        P(),
        P(),
        P("rows", "chan", None),
    )
    out_specs = (
        P("rows", "chan", None),
        P("rows", "chan", None),
        P(None, "chan", None),
        P(None, "chan"),
        P(None, "chan"),
        P("chan", None),
        P("chan"),
        P("chan"),
    )
    return jax.shard_map(shards, mesh=mesh, in_specs=in_specs, out_specs=out_specs, check_vma=False)
```

```python
import functools
import math

import jax
import jax.numpy as jnp
from jax import lax
from jax.experimental import pallas as pl
from jax.experimental.pallas import tpu as pltpu
from jax.sharding import PartitionSpec as P

K = 24
AR = 3
TILE = 256
HALF = 128
PER_STEP = 4

eps_norm = 1e-05


def rms_scale(values, scales):
    return values * lax.rsqrt(jnp.mean(values * values, axis=-1, keepdims=True) + eps_norm) * scales


def contract_first(left, right):
    return lax.dot_general(
        left, right, (((0,), (0,)), ((), ())), preferred_element_type=jnp.float32
    )


def contract_last(left, right):
    return lax.dot_general(
        left, right, (((1,), (1,)), ((), ())), preferred_element_type=jnp.float32
    )


def product(left, right):
    return jnp.dot(left, right, preferred_element_type=jnp.float32)


def in_hbm(value):
    return pltpu.with_memory_space_constraint(value, pltpu.HBM)


def whole(shape):
    return pl.BlockSpec(shape, lambda *_: (0,) * len(shape))


def vmem(mebibytes):
    return pltpu.CompilerParams(vmem_limit_bytes=mebibytes << 20)


def first_norm_kernel(me, hidden, gain, segments, pieces):
    count, rows, share = pieces.shape
    channels = hidden.shape[2] // count
    normed = rms_scale(hidden[0].astype(jnp.float32), gain[...])
    normed = normed.T.astype(jnp.bfloat16)
    ids = segments[:, pl.ds(pl.multiple_of(me[0] * share, share), share)]
    ids = jnp.broadcast_to(ids.astype(jnp.float32), (rows - channels, share)).astype(jnp.bfloat16)
    for i in range(count):
        pieces[i, :channels, :] = normed[i * channels : (i + 1) * channels]
        pieces[i, channels:, :] = ids


def first_norm(me, hidden_in, gain, segments, count):
    _, share, width = hidden_in.shape
    shape = (count, width // count + 16, share)
    return pl.pallas_call(
        first_norm_kernel,
        grid_spec=pltpu.PrefetchScalarGridSpec(
            num_scalar_prefetch=1,
            grid=(1,),
            in_specs=[whole(hidden_in.shape), whole((1, width)), whole(segments.shape)],
            out_specs=whole(shape),
        ),
        out_shape=jax.ShapeDtypeStruct(shape, jnp.bfloat16),
        name="first_norm",
    )(me, hidden_in, gain[None, :], segments)


def first_norm_back_kernel(came, hidden, gain, grad, out):
    count, channels, share = came.shape
    normed_grad = came[...].astype(jnp.float32).reshape(count * channels, share).T
    tokens = hidden[0].astype(jnp.float32)
    scale = lax.rsqrt(jnp.mean(tokens * tokens, axis=-1, keepdims=True) + eps_norm)
    weighed = normed_grad * gain[...]
    along = jnp.mean(weighed * tokens, axis=-1, keepdims=True)
    out[0] = grad[...] + scale * (weighed - tokens * (scale * scale * along))


def first_norm_back(came, hidden_in, gain, grad):
    return pl.pallas_call(
        first_norm_back_kernel,
        out_shape=jax.ShapeDtypeStruct(hidden_in.shape, jnp.float32),
        name="first_norm_back",
    )(came, hidden_in, gain[None, :], grad)


def tile_pairs(length):
    blocks, reach = length // TILE, length // 2 // TILE
    return [(tb, sb) for tb in range(blocks) for sb in range(max(0, tb - reach), tb + 1)]


def slab_width(length):
    return length // 2 + TILE


def parity_lanes(rows, lanes, dtype=jnp.float32):
    lane = lax.broadcasted_iota(jnp.int32, (rows, lanes), 1)
    return (1 - 2 * (lane % 2)).astype(dtype)


def block(index):
    return slice(index * TILE, (index + 1) * TILE)


def segment_row(pieces):
    row = pieces.shape[1] - 8
    return jnp.concatenate(
        [pieces[i, row:, :].astype(jnp.float32) for i in range(pieces.shape[0])], axis=1
    )


def build_masks(ids, masks, length, targets_in_rows):
    row = lax.broadcasted_iota(jnp.int32, (TILE, TILE), 0)
    col = lax.broadcasted_iota(jnp.int32, (TILE, TILE), 1)
    in_lanes = [jnp.broadcast_to(ids[:1, block(b)], (TILE, TILE)) for b in range(length // TILE)]
    in_rows = [value.T for value in in_lanes]
    for index, (tb, sb) in enumerate(tile_pairs(length)):
        rows_of, lanes_of = (tb, sb) if targets_in_rows else (sb, tb)
        same = in_rows[rows_of] == in_lanes[lanes_of]
        if tb == sb:
            same = same & ((row >= col) if targets_in_rows else (col >= row))
        masks[index] = jnp.where(same, 1.0, 0.0).astype(jnp.bfloat16)


def lag_keep(ids, lag):
    lane = lax.broadcasted_iota(jnp.int32, ids.shape, 1)
    same = (pltpu.roll(ids, lag, 1) == ids) & (lane >= lag)
    return jnp.where(same, 1.0, 0.0)[:1]


def build_slab(taps, slab, width):
    rolled = pltpu.roll(jnp.broadcast_to(taps, (HALF, width)), 0, 1, stride=1, stride_axis=0)
    rolled = rolled.astype(jnp.bfloat16)
    slab[:HALF, :] = rolled
    slab[HALF:, HALF:] = rolled[:, : width - HALF]
    slab[HALF:, :HALF] = rolled[:, :HALF]


def start_maps(filters, pieces, lags, taps, masks, doubled):
    count, _, share = pieces.shape
    channels, length = lags.shape[1:]
    ids = segment_row(pieces)
    build_masks(ids, masks, length, False)
    taps[...] = filters[:, : taps.shape[1]].astype(jnp.float32)
    sign = parity_lanes(channels, share, jnp.bfloat16)
    for i in range(count):
        part = pieces[i, :channels, :]
        doubled[:channels, i * share : (i + 1) * share] = part
        doubled[channels:, i * share : (i + 1) * share] = part * sign
    inputs = doubled[:channels, :]
    lags[0] = inputs
    inputs = inputs.astype(jnp.float32)
    for j in range(1, AR):
        lags[j] = (pltpu.roll(inputs, j, 1) * lag_keep(ids, j)).astype(jnp.bfloat16)


def step_maps(first, maps, taps, slabs, masks, doubled):
    channels, length = maps.shape[2:]
    width = taps.shape[1]
    pairs = tile_pairs(length)
    parity = parity_lanes(channels, TILE)
    for k in range(PER_STEP):
        slab = slabs.at[k]
        build_slab(taps[pl.ds(first + k, 1), :], slab, width)
        for tb in range(length // TILE):
            chosen = [(i, sb) for i, (t, sb) in enumerate(pairs) if t == tb]
            tiles = [slab[:, block(tb - sb)] * masks[i] for i, sb in chosen]
            low = chosen[0][1]
            both = product(
                doubled[:, low * TILE : (tb + 1) * TILE], jnp.concatenate(tiles, axis=0)
            )
            maps[0, k, :, block(tb)] = both[:channels].astype(jnp.bfloat16)
            maps[1, k, :, block(tb)] = (both[channels:] * parity).astype(jnp.bfloat16)


def maps_kernel(start, filters, pieces, *refs):
    maps, lags, taps, slabs, masks, doubled = refs[-6:]
    step = pl.program_id(0)

    @pl.when(step == 0)
    def _():
        start_maps(filters, pieces, lags, taps, masks, doubled)

    step_maps(start + step * PER_STEP, maps, taps, slabs, masks, doubled)


def mixed_kernel(
    me,
    filters,
    pieces,
    plus_mixing,
    minus_mixing,
    lag_mixing,
    maps,
    lags,
    keep0,
    give0,
    keep1,
    give1,
    taps,
    slabs,
    masks,
    doubled,
    acc,
):
    _, channels, model_width = plus_mixing.shape
    count, _, share = pieces.shape
    length = lags.shape[2]
    step = pl.program_id(0)

    @pl.when(step == 0)
    def _():
        start_maps(filters, pieces, lags, taps, masks, doubled)
        acc[...] = jnp.zeros_like(acc)

    step_maps(step * PER_STEP, maps, taps, slabs, masks, doubled)
    rows = PER_STEP * channels

    def part(weights, values):
        return contract_first(weights.reshape(-1, model_width), values.reshape(-1, length))

    total = part(plus_mixing[...], maps[0]) + part(minus_mixing[...], maps[1])
    for i in range(count):
        acc[i] += total[:, i * share : (i + 1) * share]

    @pl.when(step == pl.num_programs(0) - 1)
    def _():
        last = part(lag_mixing[...], lags[...])
        for i in range(count):
            acc[i] += last[:, i * share : (i + 1) * share]
        half = model_width // 2
        low, near = me[0] & 1, (me[0] >> 1) & 1
        for r in range(count // 4):
            for a in range(2):
                for other, (out0, out1) in enumerate(((keep0, keep1), (give0, give1))):
                    out0[r, a] = acc[r * 4 + a * 2 + (low ^ other), :half].astype(jnp.bfloat16)
                    out1[r, a] = acc[r * 4 + (near ^ other) * 2 + a, half:].astype(jnp.bfloat16)


def place_tokens(me, parts, out):
    rows = parts[0].shape[2]
    for half, pair in enumerate((parts[:2], parts[2:])):
        for other, part in enumerate(pair):
            low, near = me & 1, (me >> 1) & 1
            for a in range(2):
                for r in range(part.shape[1]):
                    if half == 0:
                        owner = r * 4 + a * 2 + (low ^ other)
                    else:
                        owner = r * 4 + (near ^ other) * 2 + a
                    start = pl.multiple_of((owner * 2 + half) * rows, rows)
                    out[pl.ds(start, rows), :] = part[a, r, :rows, :]


def place_kernel(me, part0, part1, part2, part3, out):
    place_tokens(me[0], (part0, part1, part2, part3), out)


def place(me, parts):
    count = 2 * sum(math.prod(part.shape[:-1]) for part in parts[:2])
    shape = (count, parts[0].shape[-1])
    return pl.pallas_call(
        place_kernel,
        grid_spec=pltpu.PrefetchScalarGridSpec(
            num_scalar_prefetch=1,
            grid=(1,),
            in_specs=[whole(part.shape) for part in parts],
            out_specs=whole(shape),
        ),
        out_shape=pltpu.VMEM(shape, jnp.bfloat16),
        name="place",
    )(me, *parts)


def spectral_back_kernel(
    filters, plus_mixing, minus_mixing, pieces, grads, acc, taps, slabs, masks, both
):
    _, channels, model_width = plus_mixing.shape
    length, width = acc.shape[1], taps.shape[1]
    reach = length // 2
    pairs = tile_pairs(length)
    rows = PER_STEP * channels
    step = pl.program_id(0)

    @pl.when(step == 0)
    def _():
        build_masks(segment_row(pieces), masks, length, True)
        acc[...] = jnp.zeros_like(acc)
        source = lax.broadcasted_iota(jnp.int32, (width, width), 0)
        target = lax.broadcasted_iota(jnp.int32, (width, width), 1)
        flip = jnp.where(source + target == reach, 1.0, 0.0).astype(jnp.bfloat16)
        taps[...] = product(filters[:, :width], flip)

    sign = parity_lanes(rows, length, jnp.bfloat16)
    plus = contract_last(plus_mixing[...].reshape(rows, model_width), grads[...])
    both[:, :channels, :] = plus.astype(jnp.bfloat16).reshape(PER_STEP, channels, length)
    minus = contract_last(minus_mixing[...].reshape(rows, model_width), grads[...])
    both[:, channels:, :] = (minus.astype(jnp.bfloat16) * sign).reshape(
        PER_STEP, channels, length
    )
    for k in range(PER_STEP):
        build_slab(taps[pl.ds(step * PER_STEP + k, 1), :], slabs.at[k], width)
    for sb in range(length // TILE):
        chosen = [(i, tb) for i, (tb, s) in enumerate(pairs) if s == sb]
        last = chosen[-1][1]
        total = acc[:, block(sb)]
        for k in range(PER_STEP):
            tiles = []
            for i, tb in chosen:
                start = reach - (tb - sb) * TILE
                tiles.append(slabs[k, :, start : start + TILE] * masks[i])
            total = total + product(
                both[k, :, sb * TILE : (last + 1) * TILE], jnp.concatenate(tiles, axis=0)
            )
        acc[:, block(sb)] = total


def lag_back_kernel(acc, lag_mixing, grads, inputs, pieces, out, gain):
    _, channels, model_width = lag_mixing.shape
    length = acc.shape[1]
    count, _, share = out.shape
    ids = segment_row(pieces)
    lag_grad = contract_last(lag_mixing[...].reshape(AR * channels, model_width), grads[...])
    total = acc[:channels] + parity_lanes(channels, length) * acc[channels:]
    for j in range(AR):
        term = lag_grad[j * channels : (j + 1) * channels]
        if j:
            term = pltpu.roll(term * lag_keep(ids, j), length - j, 1)
        total = total + term
    back = total.astype(jnp.bfloat16)
    for i in range(count):
        out[i] = back[:, i * share : (i + 1) * share]
    weighed = back.astype(jnp.float32) * inputs[0].astype(jnp.float32)
    by_lane = jnp.broadcast_to(jnp.sum(weighed, axis=1, keepdims=True), (channels, 128))
    row = lax.broadcasted_iota(jnp.int32, by_lane.shape, 0)
    lane = lax.broadcasted_iota(jnp.int32, by_lane.shape, 1)
    total = jnp.sum(jnp.where(row == lane, by_lane, 0.0), axis=0, keepdims=True)
    gain[...] = jnp.broadcast_to(total, gain.shape)


def toeplitz_scratch(length, count):
    width = slab_width(length)
    return [
        pltpu.VMEM((count, width), jnp.float32),
        pltpu.VMEM((PER_STEP, TILE, width), jnp.bfloat16),
        pltpu.VMEM((len(tile_pairs(length)), TILE, TILE), jnp.bfloat16),
    ]


def maps_scratch(channels, length, count):
    return [
        *toeplitz_scratch(length, count),
        pltpu.VMEM((2 * channels, length), jnp.bfloat16),
    ]


def spectral_maps(pieces, filters, channels, start, count, into=None):
    length = filters.shape[1]
    first = start // PER_STEP
    given = [] if into is None else [in_hbm(into)]
    return pl.pallas_call(
        functools.partial(maps_kernel, start),
        grid=(count // PER_STEP,),
        in_specs=[
            whole(filters.shape),
            whole(pieces.shape),
            *[pl.BlockSpec(memory_space=pltpu.HBM) for _ in given],
        ],
        out_specs=[
            pl.BlockSpec((2, PER_STEP, channels, length), lambda k: (0, k + first, 0, 0)),
            whole((AR, channels, length)),
        ],
        out_shape=[
            pltpu.HBM((2, K, channels, length), jnp.bfloat16),
            jax.ShapeDtypeStruct((AR, channels, length), jnp.bfloat16),
        ],
        scratch_shapes=maps_scratch(channels, length, filters.shape[0]),
        input_output_aliases={2: 0} if given else {},
        compiler_params=vmem(16),
        cost_estimate=pl.CostEstimate(
            flops=6 * channels * count * length * length, transcendentals=0, bytes_accessed=4 << 20
        ),
        name="spectral_maps",
    )(filters, pieces, *given)


def spectral_mixed(me, pieces, filters, mixing):
    owners, _, share = pieces.shape
    channels, model_width = mixing.shape[1:]
    count, length = filters.shape
    steps = count // PER_STEP
    cut = (owners // 4, 2, model_width // 2, share)
    mix_block = (PER_STEP, channels, model_width)
    return pl.pallas_call(
        mixed_kernel,
        grid_spec=pltpu.PrefetchScalarGridSpec(
            num_scalar_prefetch=1,
            grid=(steps,),
            in_specs=[
                whole(filters.shape),
                whole(pieces.shape),
                pl.BlockSpec(mix_block, lambda k, _: (k, 0, 0)),
                pl.BlockSpec(mix_block, lambda k, _: (k + steps, 0, 0)),
                pl.BlockSpec((AR, channels, model_width), lambda k, _: (2 * count // AR, 0, 0)),
            ],
            out_specs=[
                pl.BlockSpec((2, PER_STEP, channels, length), lambda k, _: (0, k, 0, 0)),
                whole((AR, channels, length)),
                *[whole(cut)] * 4,
            ],
            scratch_shapes=[
                *maps_scratch(channels, length, count),
                pltpu.VMEM((owners, model_width, share), jnp.float32),
            ],
        ),
        out_shape=[
            pltpu.HBM((2, count, channels, length), jnp.bfloat16),
            jax.ShapeDtypeStruct((AR, channels, length), jnp.bfloat16),
            *[jax.ShapeDtypeStruct(cut, jnp.bfloat16)] * 4,
        ],
        compiler_params=vmem(24),
        name="spectral_mixed",
    )(me, filters, pieces, *[in_hbm(mixing)] * 3)


def spectral_back(grads, mixing, filters, pieces):
    channels, model_width = mixing.shape[1:]
    count, length = filters.shape
    steps = count // PER_STEP
    mix_block = (PER_STEP, channels, model_width)
    return pl.pallas_call(
        spectral_back_kernel,
        grid=(steps,),
        in_specs=[
            whole(filters.shape),
            pl.BlockSpec(mix_block, lambda k: (k, 0, 0)),
            pl.BlockSpec(mix_block, lambda k: (k + steps, 0, 0)),
            whole(pieces.shape),
            whole(grads.shape),
        ],
        out_specs=whole((2 * channels, length)),
        scratch_shapes=[
            *toeplitz_scratch(length, count),
            pltpu.VMEM((PER_STEP, 2 * channels, length), jnp.bfloat16),
        ],
        out_shape=jax.ShapeDtypeStruct((2 * channels, length), jnp.float32),
        compiler_params=vmem(24),
        name="spectral_back",
    )(filters, *[in_hbm(mixing)] * 2, pieces, grads)


def lag_back(acc, mixing, grads, lags, pieces):
    channels, model_width = mixing.shape[1:]
    owners, _, share = pieces.shape
    sent = (owners, channels, share)
    return pl.pallas_call(
        lag_back_kernel,
        grid=(1,),
        in_specs=[
            whole(acc.shape),
            pl.BlockSpec((AR, channels, model_width), lambda k: (2 * K // AR, 0, 0)),
            whole(grads.shape),
            pl.BlockSpec((1, *lags.shape[1:]), lambda k: (0, 0, 0)),
            whole(pieces.shape),
        ],
        out_specs=[whole(sent), whole((8, 128))],
        out_shape=[
            jax.ShapeDtypeStruct(sent, jnp.bfloat16),
            jax.ShapeDtypeStruct((8, 128), jnp.float32),
        ],
        compiler_params=vmem(16),
        name="lag_back",
    )(acc, in_hbm(mixing), grads, in_hbm(lags), pieces)


def gelu_parts(gate_value, upper_value, hidden_grad):
    slope = math.sqrt(2 / math.pi)
    square = gate_value * gate_value
    tanh = jnp.tanh(slope * gate_value * (1.0 + 0.044715 * square))
    rise = 0.5 * (1.0 + tanh)
    gelu = gate_value * rise
    bend = 0.5 * slope * (1.0 - tanh * tanh) * (1.0 + 3 * 0.044715 * square)
    return (
        gelu * upper_value,
        hidden_grad * upper_value * (rise + gate_value * bend),
        hidden_grad * gelu,
    )


def feed_forward_kernel(
    bit,
    held,
    got,
    hidden_in,
    gain,
    cotangent,
    gate,
    up,
    down,
    output,
    normed_out,
    grad,
    grad_low,
    normed,
    resid,
    acc,
    normed_grad,
):
    step = pl.program_id(0)
    share = resid.shape[0]

    @pl.when(step == 0)
    def _():
        mixed = held[bit[0]].astype(jnp.float32) + got[...].astype(jnp.float32)
        resid[...] = hidden_in[0].astype(jnp.float32) + mixed.T
        normed[...] = rms_scale(resid[...], gain[...]).astype(jnp.bfloat16)
        acc[...] = jnp.zeros_like(acc)
        normed_grad[...] = jnp.zeros_like(normed_grad)

    gate_value = product(normed[...], gate[...])
    upper_value = product(normed[...], up[...])
    hidden_grad = contract_last(cotangent[0], down[...])
    hidden, gate_back, upper_back = gelu_parts(gate_value, upper_value, hidden_grad)
    acc[...] += product(hidden.astype(jnp.bfloat16), down[...])
    normed_grad[...] += contract_last(gate_back.astype(jnp.bfloat16), gate[...]) + contract_last(
        upper_back.astype(jnp.bfloat16), up[...]
    )

    @pl.when(step == pl.num_programs(0) - 1)
    def _():
        value, back = resid[...], normed_grad[...]
        output[0] = (value + acc[...]).astype(jnp.bfloat16)
        scale = lax.rsqrt(jnp.mean(value * value, axis=-1, keepdims=True) + eps_norm)
        weighed = back * gain[...]
        along = jnp.mean(weighed * value, axis=-1, keepdims=True)
        total = cotangent[0].astype(jnp.float32) + scale * (
            weighed - value * (scale * scale * along)
        )
        grad[...] = total
        grad_low[...] = total.astype(jnp.bfloat16)
        gains = jnp.sum(back * value * scale, axis=0, keepdims=True)
        high = jnp.broadcast_to(gains, (16, gains.shape[1])).astype(jnp.bfloat16)
        low = (gains - high.astype(jnp.float32)).astype(jnp.bfloat16)
        row = lax.broadcasted_iota(jnp.int32, low.shape, 0)
        normed_out[:share, :] = normed[...]
        normed_out[share:, :] = jnp.where(row < 8, high, low)


def feed_forward(bit, held, got, hidden_in, gain, cotangent, w_gate, w_up, w_down):
    _, share, width = hidden_in.shape
    steps = 4
    units = w_gate.shape[1] // steps
    tokens = (share, width)
    return pl.pallas_call(
        feed_forward_kernel,
        grid_spec=pltpu.PrefetchScalarGridSpec(
            num_scalar_prefetch=1,
            grid=(steps,),
            in_specs=[
                whole(held.shape),
                whole(got.shape),
                whole(hidden_in.shape),
                whole((1, width)),
                whole(cotangent.shape),
                pl.BlockSpec((width, units), lambda k, _: (0, k)),
                pl.BlockSpec((width, units), lambda k, _: (0, k)),
                pl.BlockSpec((units, width), lambda k, _: (k, 0)),
            ],
            out_specs=[
                whole(hidden_in.shape),
                whole((share + 16, width)),
                whole(tokens),
                whole(tokens),
            ],
            scratch_shapes=[
                pltpu.VMEM(tokens, jnp.bfloat16),
                *[pltpu.VMEM(tokens, jnp.float32)] * 3,
            ],
        ),
        out_shape=[
            jax.ShapeDtypeStruct(hidden_in.shape, jnp.bfloat16),
            jax.ShapeDtypeStruct((share + 16, width), jnp.bfloat16),
            jax.ShapeDtypeStruct(tokens, jnp.float32),
            jax.ShapeDtypeStruct(tokens, jnp.bfloat16),
        ],
        compiler_params=vmem(16),
        name="feed_forward",
    )(bit, held, got, hidden_in, gain[None, :], cotangent, *map(in_hbm, (w_gate, w_up, w_down)))


def own_mixing_grad_kernel(maps, lags, grads, out, lag_out):
    maps = maps[...].reshape(-1, maps.shape[-1])
    out[...] = product(maps, grads[...]).astype(out.dtype).reshape(out.shape)

    @pl.when(pl.program_id(0) == pl.num_programs(0) - 1)
    def _():
        values = lags[...].reshape(-1, lags.shape[-1])
        lag_out[...] = product(values, grads[...]).astype(out.dtype).reshape(lag_out.shape)


def own_mixing_grad(maps, lags, grads):
    _, count, channels, length = maps.shape
    width = grads.shape[1]
    steps, rows = 4, count // 4
    return pl.pallas_call(
        own_mixing_grad_kernel,
        grid=(steps,),
        in_specs=[
            pl.BlockSpec((2, rows, channels, length), lambda k: (0, k, 0, 0)),
            whole(lags.shape),
            whole(grads.shape),
        ],
        out_specs=[
            pl.BlockSpec((2, rows, channels, width), lambda k: (0, k, 0, 0)),
            whole((AR, channels, width)),
        ],
        out_shape=[
            pltpu.HBM((2, count, channels, width), jnp.bfloat16),
            pltpu.HBM((AR, channels, width), jnp.bfloat16),
        ],
        compiler_params=vmem(24),
        name="own_mixing_grad",
    )(in_hbm(maps), in_hbm(lags), grads)


def mixing_grad_kernel(with_lags, maps, lags, grads, own, own_lags, out):
    step, size = pl.program_id(0), maps.shape[0] * maps.shape[1]

    def total(left, mine):
        values = product(left[...].reshape(-1, left.shape[-1]), grads[...])
        return (values + mine[...].reshape(values.shape).astype(jnp.float32)).astype(out.dtype)

    out[pl.ds(pl.multiple_of(step * size, size), size), :] = total(maps, own)

    if with_lags:

        @pl.when(step == pl.num_programs(0) - 1)
        def _():
            out[size * pl.num_programs(0) :, :] = total(lags, own_lags)


def mixing_grad(which, maps, lags, grads, own, own_lags):
    _, count, channels, length = maps.shape
    width = grads.shape[1]
    steps, rows = 3, count // 3
    total = (count + which * AR) * channels
    return pl.pallas_call(
        functools.partial(mixing_grad_kernel, bool(which)),
        grid=(steps,),
        in_specs=[
            pl.BlockSpec((None, rows, channels, length), lambda k: (which, k, 0, 0)),
            whole(lags.shape),
            whole(grads.shape),
            pl.BlockSpec((None, rows, channels, width), lambda k: (which, k, 0, 0)),
            whole(own_lags.shape),
        ],
        out_specs=whole((total, width)),
        out_shape=jax.ShapeDtypeStruct((total, width), jnp.bfloat16),
        compiler_params=vmem(24),
        name="mixing_grad",
    )(in_hbm(maps), in_hbm(lags), in_hbm(grads), in_hbm(own), in_hbm(own_lags))


def unit_grads_kernel(me, *refs):
    *parts, gate, up, down, first_gain, out, normed, cotangent = refs
    place_tokens(me[0], parts[:4], normed)
    place_tokens(me[0], parts[4:], cotangent)
    width, units = gate.shape
    hidden_grad = contract_last(cotangent[...], down[...])
    gate_value = product(normed[...], gate[...])
    upper_value = product(normed[...], up[...])
    hidden, gate_back, upper_back = gelu_parts(gate_value, upper_value, hidden_grad)
    gate_part = contract_first(normed[...], gate_back.astype(jnp.bfloat16))
    up_part = contract_first(normed[...], upper_back.astype(jnp.bfloat16))
    down_part = contract_first(hidden.astype(jnp.bfloat16), cotangent[...])
    out[:width] = gate_part.astype(jnp.bfloat16)
    out[width : 2 * width] = up_part.astype(jnp.bfloat16)
    for i in range(width // units):
        start = 2 * width + i * units
        out[start : start + units] = down_part[:, i * units : (i + 1) * units].astype(
            jnp.bfloat16
        )
    share_rows = parts[0].shape[2]
    second_gain = jnp.zeros((16, width), jnp.float32)
    for part in parts[2:4]:
        for a in range(2):
            for r in range(part.shape[1]):
                second_gain = second_gain + part[a, r, share_rows:, :].astype(jnp.float32)
    second_gain = (second_gain[:8] + second_gain[8:]).astype(jnp.bfloat16)
    start = 3 * width
    for i in range(width // units):
        out[start + 16 * i : start + 16 * i + 8] = second_gain[:, i * units : (i + 1) * units]
    start += 16 * (width // units)
    out[start : start + 8, : first_gain.shape[1]] = first_gain[...].astype(jnp.bfloat16)


def unit_grads(me, normed_parts, cotangent_parts, w_gate, w_up, w_down, first_gain):
    width, hidden = w_gate.shape
    chans = lax.axis_size("chan")
    units = hidden // chans
    rows = 3 * width + 16 * (width // units) + 16
    parts = [*normed_parts, *cotangent_parts]
    tokens = 2 * sum(math.prod(part.shape[:-1]) for part in normed_parts[:2])
    return pl.pallas_call(
        unit_grads_kernel,
        grid_spec=pltpu.PrefetchScalarGridSpec(
            num_scalar_prefetch=1,
            grid=(1,),
            in_specs=[
                *[whole(part.shape) for part in parts],
                pl.BlockSpec((width, units), lambda k, me: (0, me[0])),
                pl.BlockSpec((width, units), lambda k, me: (0, me[0])),
                pl.BlockSpec((units, width), lambda k, me: (me[0], 0)),
                whole(first_gain.shape),
            ],
            out_specs=whole((rows, units)),
            scratch_shapes=[pltpu.VMEM((tokens, width), jnp.bfloat16)] * 2,
        ),
        out_shape=jax.ShapeDtypeStruct((rows, units), jnp.bfloat16),
        compiler_params=vmem(24),
        name="unit_grads",
    )(me, *parts, in_hbm(w_gate), in_hbm(w_up), in_hbm(w_down), first_gain)


def swap(values, axis, mask):
    count = lax.axis_size(axis)
    return lax.ppermute(values, axis, [(i, i ^ mask) for i in range(count)])


def bits_of(axis):
    return [1 << b for b in range(lax.axis_size(axis).bit_length() - 1)]


def join(mine, other, high, dim):
    return jnp.where(
        high, jnp.concatenate([other, mine], dim), jnp.concatenate([mine, other], dim)
    )


def tie(*values):
    return lax.optimization_barrier(values)


def gather_round(held, mask):
    me = lax.axis_index("chan")
    return join(held[None], swap(held, "chan", mask)[None], (me & mask) != 0, 0)


class Gather:
    def __init__(self, values, half):
        masks = bits_of("chan")
        self.half = half
        self.shape = values.shape
        self.common = masks[2:]
        self.orders = [(masks[1], masks[0]), (masks[0], masks[1])]
        self.held = values[None]

    def first(self):
        for mask in self.common:
            self.held = gather_round(self.held, mask).reshape(-1, *self.shape)
        return self.held

    def second(self):
        self.halves = [self.held[:, : self.half], self.held[:, self.half :]]
        self.halves = [
            gather_round(h, order[0]) for h, order in zip(self.halves, self.orders, strict=True)
        ]
        return self.halves

    def third(self):
        self.others = [
            swap(h, "chan", order[1]) for h, order in zip(self.halves, self.orders, strict=True)
        ]
        return self.others

    def parts(self):
        return (self.halves[0], self.others[0], self.halves[1], self.others[1])


def add(left, right):
    return left.astype(jnp.float32) + right.astype(jnp.float32)


def own_entry(values, mask, dim):
    return add(*exchange(values, mask, dim)).squeeze(dim)


def exchange(values, mask, dim):
    bit = (lax.axis_index("chan") & mask) // mask
    keep = lax.dynamic_slice_in_dim(values, bit, 1, dim)
    give = lax.dynamic_slice_in_dim(values, 1 - bit, 1, dim)
    return keep, swap(give, "chan", mask)


def scatter_tokens(keep0, give0, keep1, give1, beside):
    masks = bits_of("chan")
    got0, got1 = swap(give0, "chan", masks[0]), swap(give1, "chan", masks[1])
    half0 = add(keep0, got0).astype(jnp.bfloat16)
    half1 = add(keep1, got1).astype(jnp.bfloat16)
    half0, half1, *beside = tie(half0, half1, *beside)
    half0 = own_entry(half0, masks[1], 1)
    half1 = own_entry(half1, masks[0], 1)
    held = jnp.concatenate([half0, half1], axis=1)
    for mask in masks[:2:-1]:
        held = held.astype(jnp.bfloat16).reshape(2, -1, *held.shape[1:])
        held = own_entry(held, mask, 0)
    held = held.astype(jnp.bfloat16)
    return held, exchange(held, masks[2], 0)[1][0], beside


def core_halves(values):
    core = lax.axis_index("rows") & 1
    half = values.shape[0] // 2
    return [lax.dynamic_slice_in_dim(values, which * half, half, 0) for which in (core, 1 - core)]


def both_halves(held, dim):
    other = swap(held, "rows", 1).astype(jnp.float32)
    return join(held.astype(jnp.float32), other, (lax.axis_index("rows") & 1) != 0, dim)


def shards(
    hidden_in, segments, filters, gain_one, mixing, gain_two, w_gate, w_up, w_down, out_grad
):
    chans = lax.axis_size("chan")
    me = lax.axis_index("chan").astype(jnp.int32)
    at = me.reshape(1)
    _, share, width = hidden_in.shape
    channels = width // chans
    cotangent_gather = Gather(out_grad[0], share // 2)
    cotangent_gather.first()
    pieces = lax.all_to_all(
        first_norm(at, hidden_in, gain_one, segments, chans),
        "chan",
        split_axis=0,
        concat_axis=0,
    )
    peer_pieces = swap(pieces, "rows", 2)
    maps, lags, *cut = spectral_mixed(at, pieces, filters, mixing)
    peer_pieces, lags = tie(peer_pieces, lags)
    peer_maps, peer_lags = spectral_maps(peer_pieces, filters, channels, 0, K // 2)
    cotangent_gather.second()
    beside = (peer_maps, *cotangent_gather.third())
    held, got, (peer_maps, *cotangent_gather.others) = scatter_tokens(*cut, beside)
    last_bit = ((me >> 2) & 1).reshape(1)
    output, normed_two, resid_grad, resid_low = feed_forward(
        last_bit, held, got, hidden_in, gain_two, out_grad, w_gate, w_up, w_down
    )
    grad_gather = Gather(resid_low, share // 2)
    first = grad_gather.first()
    peer_pieces, resid_grad = tie(peer_pieces, resid_grad)
    peer_maps, _ = spectral_maps(peer_pieces, filters, channels, K // 2, K // 2, peer_maps)
    normed_two, grad_gather.held, peer_maps = tie(normed_two, first, peer_maps)
    normed_gather = Gather(normed_two, share // 2)
    normed_gather.first()
    grad_gather.second()
    normed_gather.second()
    grad_gather.third()
    normed_gather.third()
    full_grad = place(at, grad_gather.parts())
    peer_grad = swap(full_grad, "rows", 2)
    acc = spectral_back(full_grad, mixing, filters, pieces)
    back, first_local = lag_back(acc, mixing, full_grad, lags, pieces)
    came = lax.all_to_all(back, "chan", split_axis=0, concat_axis=0)
    first_local, *normed_parts = tie(first_local, *normed_gather.parts())
    unit_parts = unit_grads(
        at, normed_parts, cotangent_gather.parts(), w_gate, w_up, w_down, first_local
    )
    unit_parts, full_grad = tie(unit_parts, full_grad)
    keep, give = core_halves(unit_parts)
    unit_given = swap(give, "rows", 1)
    own, own_lags = own_mixing_grad(maps, lags, full_grad)
    own_lags, unit_given = tie(own_lags, unit_given)
    unit_half = add(keep, unit_given).astype(jnp.bfloat16)
    unit_half, peer_grad = tie(unit_half, peer_grad)
    unit_other = swap(unit_half, "rows", 2)
    first_part = mixing_grad(0, peer_maps, peer_lags, peer_grad, own, own_lags)
    first_part, peer_grad = tie(first_part, peer_grad)
    second_part = mixing_grad(1, peer_maps, peer_lags, peer_grad, own, own_lags)
    second_part, came, unit_other = tie(second_part, came, unit_other)
    sums = []
    for part in (first_part, second_part):
        for mask in [1, *bits_of("rows")[2:]]:
            part = add(part, swap(part, "rows", mask)).astype(jnp.bfloat16)
        sums.append(part.astype(jnp.float32))
    mixing_sum = jnp.concatenate(sums, axis=0).reshape(mixing.shape)
    input_total = first_norm_back(came, hidden_in, gain_one, resid_grad)
    unit_half = add(unit_half, unit_other).astype(jnp.bfloat16)
    for mask in bits_of("rows")[2:]:
        unit_half = add(unit_half, swap(unit_half, "rows", mask)).astype(jnp.bfloat16)
    unit_sum = both_halves(unit_half, 0)
    units = w_gate.shape[1] // chans
    columns = range(0, width, units)
    down_sum = jnp.concatenate([unit_sum[2 * width + i : 2 * width + i + units] for i in columns], 1)
    gains = [unit_sum[3 * width + 16 * i] for i in range(len(columns))]
    second_gain = lax.dynamic_slice_in_dim(jnp.concatenate(gains), me * channels, channels)
    first_gain = unit_sum[3 * width + 16 * len(columns), :channels] / (
        lax.dynamic_slice_in_dim(gain_one, me * channels, channels)
    )
    return (
        output,
        input_total,
        mixing_sum,
        unit_sum[:width],
        unit_sum[width : 2 * width],
        down_sum,
        first_gain,
        second_gain,
    )


def solution(mesh):
    in_specs = (
        P("rows", "chan", None),
        P("rows", None),
        P(),
        P(),
        P(None, "chan", None),
        P(),
        P(),
        P(),
        P(),
        P("rows", "chan", None),
    )
    out_specs = (
        P("rows", "chan", None),
        P("rows", "chan", None),
        P(None, "chan", None),
        P(None, "chan"),
        P(None, "chan"),
        P("chan", None),
        P("chan"),
        P("chan"),
    )
    return jax.shard_map(shards, mesh=mesh, in_specs=in_specs, out_specs=out_specs, check_vma=False)
```

```python
import functools
import math

import jax
import jax.numpy as jnp
from jax import lax
from jax.experimental import pallas as pl
from jax.experimental.pallas import tpu as pltpu
from jax.sharding import PartitionSpec as P

K = 24
AR = 3
TILE = 256
HALF = 128
PER_STEP = 4

eps_norm = 1e-05


def rms_scale(values, scales):
    return values * lax.rsqrt(jnp.mean(values * values, axis=-1, keepdims=True) + eps_norm) * scales


def contract_first(left, right):
    return lax.dot_general(
        left, right, (((0,), (0,)), ((), ())), preferred_element_type=jnp.float32
    )


def contract_last(left, right):
    return lax.dot_general(
        left, right, (((1,), (1,)), ((), ())), preferred_element_type=jnp.float32
    )


def product(left, right):
    return jnp.dot(left, right, preferred_element_type=jnp.float32)


def in_hbm(value):
    return pltpu.with_memory_space_constraint(value, pltpu.HBM)


def in_vmem():
    return pl.BlockSpec(memory_space=pltpu.VMEM)


def whole(shape):
    return pl.BlockSpec(shape, lambda *_: (0,) * len(shape))


def vmem(mebibytes):
    return pltpu.CompilerParams(vmem_limit_bytes=mebibytes << 20)


def first_norm_kernel(me, hidden, gain, segments, pieces):
    count, rows, share = pieces.shape
    channels = hidden.shape[2] // count
    normed = rms_scale(hidden[0].astype(jnp.float32), gain[...])
    normed = normed.T.astype(jnp.bfloat16)
    ids = segments[:, pl.ds(pl.multiple_of(me[0] * share, share), share)]
    ids = jnp.broadcast_to(ids.astype(jnp.float32), (rows - channels, share)).astype(jnp.bfloat16)
    for i in range(count):
        pieces[i, :channels, :] = normed[i * channels : (i + 1) * channels]
        pieces[i, channels:, :] = ids


def first_norm(me, hidden_in, gain, segments, count):
    _, share, width = hidden_in.shape
    shape = (count, width // count + 16, share)
    return pl.pallas_call(
        first_norm_kernel,
        grid_spec=pltpu.PrefetchScalarGridSpec(
            num_scalar_prefetch=1,
            grid=(1,),
            in_specs=[whole(hidden_in.shape), whole((1, width)), whole(segments.shape)],
            out_specs=whole(shape),
        ),
        out_shape=jax.ShapeDtypeStruct(shape, jnp.bfloat16),
        compiler_params=vmem(8),
        name="first_norm",
    )(me, in_hbm(hidden_in), in_hbm(gain[None, :]), in_hbm(segments))


def first_norm_back_kernel(me, kept, came, hidden, gain, grad, out):
    half, channels, share = kept.shape
    parts = []
    for i in range(2 * half):
        other = i ^ me[0]
        pick = jnp.where(other < half, kept[other % half], came[other % half])
        parts.append(pick.astype(jnp.float32))
    normed_grad = jnp.concatenate(parts, axis=0).T
    tokens = hidden[0].astype(jnp.float32)
    scale = lax.rsqrt(jnp.mean(tokens * tokens, axis=-1, keepdims=True) + eps_norm)
    weighed = normed_grad * gain[...]
    along = jnp.mean(weighed * tokens, axis=-1, keepdims=True)
    out[0] = grad[...] + scale * (weighed - tokens * (scale * scale * along))


def first_norm_back(me, kept, came, hidden_in, gain, grad):
    _, share, width = hidden_in.shape
    return pl.pallas_call(
        first_norm_back_kernel,
        grid_spec=pltpu.PrefetchScalarGridSpec(
            num_scalar_prefetch=1,
            grid=(1,),
            in_specs=[
                whole(kept.shape),
                whole(came.shape),
                whole(hidden_in.shape),
                whole((1, width)),
                whole(grad.shape),
            ],
            out_specs=whole(hidden_in.shape),
        ),
        out_shape=jax.ShapeDtypeStruct(hidden_in.shape, jnp.float32),
        compiler_params=vmem(8),
        name="first_norm_back",
    )(me, kept, came, hidden_in, gain[None, :], grad)


def tile_pairs(length):
    blocks, reach = length // TILE, length // 2 // TILE
    return [(tb, sb) for tb in range(blocks) for sb in range(max(0, tb - reach), tb + 1)]


def slab_width(length):
    return length // 2 + TILE


def parity_lanes(rows, lanes, dtype=jnp.float32):
    lane = lax.broadcasted_iota(jnp.int32, (rows, lanes), 1)
    return (1 - 2 * (lane % 2)).astype(dtype)


def block(index):
    return slice(index * TILE, (index + 1) * TILE)


def segment_row(pieces):
    row = pieces.shape[1] - 8
    return jnp.concatenate(
        [pieces[i, row:, :].astype(jnp.float32) for i in range(pieces.shape[0])], axis=1
    )


def build_masks(ids, masks, length, targets_in_rows):
    row = lax.broadcasted_iota(jnp.int32, (TILE, TILE), 0)
    col = lax.broadcasted_iota(jnp.int32, (TILE, TILE), 1)
    in_lanes = [jnp.broadcast_to(ids[:1, block(b)], (TILE, TILE)) for b in range(length // TILE)]
    in_rows = [value.T for value in in_lanes]
    for index, (tb, sb) in enumerate(tile_pairs(length)):
        rows_of, lanes_of = (tb, sb) if targets_in_rows else (sb, tb)
        same = in_rows[rows_of] == in_lanes[lanes_of]
        if tb == sb:
            same = same & ((row >= col) if targets_in_rows else (col >= row))
        masks[index] = jnp.where(same, 1.0, 0.0).astype(jnp.bfloat16)


def lag_keep(ids, lag):
    lane = lax.broadcasted_iota(jnp.int32, ids.shape, 1)
    same = (pltpu.roll(ids, lag, 1) == ids) & (lane >= lag)
    return jnp.where(same, 1.0, 0.0)[:1]


def build_slab(taps, slab, width):
    rolled = pltpu.roll(jnp.broadcast_to(taps, (HALF, width)), 0, 1, stride=1, stride_axis=0)
    rolled = rolled.astype(jnp.bfloat16)
    slab[:HALF, :] = rolled
    slab[HALF:, HALF:] = rolled[:, : width - HALF]
    slab[HALF:, :HALF] = rolled[:, :HALF]


def start_maps(filters, pieces, lags, taps, masks, doubled):
    count, _, share = pieces.shape
    channels, length = lags.shape[1:]
    ids = segment_row(pieces)
    build_masks(ids, masks, length, False)
    taps[...] = filters[:, : taps.shape[1]].astype(jnp.float32)
    sign = parity_lanes(channels, share, jnp.bfloat16)
    for i in range(count):
        part = pieces[i, :channels, :]
        doubled[:channels, i * share : (i + 1) * share] = part
        doubled[channels:, i * share : (i + 1) * share] = part * sign
    inputs = doubled[:channels, :]
    lags[0] = inputs
    inputs = inputs.astype(jnp.float32)
    for j in range(1, AR):
        lags[j] = (pltpu.roll(inputs, j, 1) * lag_keep(ids, j)).astype(jnp.bfloat16)


def step_maps(first, maps, taps, slabs, masks, doubled):
    channels, length = maps.shape[2:]
    width = taps.shape[1]
    pairs = tile_pairs(length)
    parity = parity_lanes(channels, TILE)
    for k in range(PER_STEP):
        slab = slabs.at[k]
        build_slab(taps[pl.ds(first + k, 1), :], slab, width)
        for tb in range(length // TILE):
            chosen = [(i, sb) for i, (t, sb) in enumerate(pairs) if t == tb]
            tiles = [slab[:, block(tb - sb)] * masks[i] for i, sb in chosen]
            low = chosen[0][1]
            both = product(
                doubled[:, low * TILE : (tb + 1) * TILE], jnp.concatenate(tiles, axis=0)
            )
            maps[0, first + k, :, block(tb)] = both[:channels].astype(jnp.bfloat16)
            maps[1, first + k, :, block(tb)] = (both[channels:] * parity).astype(jnp.bfloat16)


def maps_kernel(start, filters, pieces, *refs):
    maps, lags, taps, slabs, masks, doubled = refs[-6:]
    step = pl.program_id(0)

    @pl.when(step == 0)
    def _():
        start_maps(filters, pieces, lags, taps, masks, doubled)

    step_maps(start + step * PER_STEP, maps, taps, slabs, masks, doubled)


def mixed_kernel(
    me,
    filters,
    pieces,
    plus_mixing,
    minus_mixing,
    lag_mixing,
    maps,
    lags,
    keep0,
    give0,
    keep1,
    give1,
    taps,
    slabs,
    masks,
    doubled,
    acc,
):
    _, channels, model_width = plus_mixing.shape
    count, _, share = pieces.shape
    length = lags.shape[2]
    step = pl.program_id(0)

    @pl.when(step == 0)
    def _():
        start_maps(filters, pieces, lags, taps, masks, doubled)
        acc[...] = jnp.zeros_like(acc)

    step_maps(step * PER_STEP, maps, taps, slabs, masks, doubled)
    def part(weights, values):
        return contract_first(weights.reshape(-1, model_width), values.reshape(-1, length))

    own = pl.ds(step * PER_STEP, PER_STEP)
    total = part(plus_mixing[...], maps[0, own]) + part(minus_mixing[...], maps[1, own])
    for i in range(count):
        acc[i] += total[:, i * share : (i + 1) * share]

    @pl.when(step == pl.num_programs(0) - 1)
    def _():
        last = part(lag_mixing[...], lags[...])
        for i in range(count):
            acc[i] += last[:, i * share : (i + 1) * share]
        half = model_width // 2
        low, near = me[0] & 1, (me[0] >> 1) & 1
        for r in range(count // 4):
            for a in range(2):
                for other, (out0, out1) in enumerate(((keep0, keep1), (give0, give1))):
                    out0[r, a] = acc[r * 4 + a * 2 + (low ^ other), :half].astype(jnp.bfloat16)
                    out1[r, a] = acc[r * 4 + (near ^ other) * 2 + a, half:].astype(jnp.bfloat16)


def place_tokens(me, parts, out):
    rows = parts[0].shape[2]
    for half, pair in enumerate((parts[:2], parts[2:])):
        for other, part in enumerate(pair):
            low, near = me & 1, (me >> 1) & 1
            for a in range(2):
                for r in range(part.shape[1]):
                    if half == 0:
                        owner = r * 4 + a * 2 + (low ^ other)
                    else:
                        owner = r * 4 + (near ^ other) * 2 + a
                    start = pl.multiple_of((owner * 2 + half) * rows, rows)
                    out[pl.ds(start, rows), :] = part[a, r, :rows, :]


def place_kernel(me, part0, part1, part2, part3, out):
    place_tokens(me[0], (part0, part1, part2, part3), out)


def place(me, parts):
    count = 2 * sum(math.prod(part.shape[:-1]) for part in parts[:2])
    shape = (count, parts[0].shape[-1])
    return pl.pallas_call(
        place_kernel,
        grid_spec=pltpu.PrefetchScalarGridSpec(
            num_scalar_prefetch=1,
            grid=(1,),
            in_specs=[whole(part.shape) for part in parts],
            out_specs=whole(shape),
        ),
        out_shape=pltpu.VMEM(shape, jnp.bfloat16),
        compiler_params=vmem(8),
        name="place",
    )(me, *parts)


def spectral_back_kernel(
    filters, plus_mixing, minus_mixing, pieces, grads, acc, taps, slabs, masks, both
):
    _, channels, model_width = plus_mixing.shape
    length, width = acc.shape[1], taps.shape[1]
    reach = length // 2
    pairs = tile_pairs(length)
    rows = PER_STEP * channels
    step = pl.program_id(0)

    @pl.when(step == 0)
    def _():
        build_masks(segment_row(pieces), masks, length, True)
        acc[...] = jnp.zeros_like(acc)
        source = lax.broadcasted_iota(jnp.int32, (width, width), 0)
        target = lax.broadcasted_iota(jnp.int32, (width, width), 1)
        flip = jnp.where(source + target == reach, 1.0, 0.0).astype(jnp.bfloat16)
        taps[...] = product(filters[:, :width], flip)

    sign = parity_lanes(rows, length, jnp.bfloat16)
    plus = contract_last(plus_mixing[...].reshape(rows, model_width), grads[...])
    both[:, :channels, :] = plus.astype(jnp.bfloat16).reshape(PER_STEP, channels, length)
    minus = contract_last(minus_mixing[...].reshape(rows, model_width), grads[...])
    both[:, channels:, :] = (minus.astype(jnp.bfloat16) * sign).reshape(
        PER_STEP, channels, length
    )
    for k in range(PER_STEP):
        build_slab(taps[pl.ds(step * PER_STEP + k, 1), :], slabs.at[k], width)
    for sb in range(length // TILE):
        chosen = [(i, tb) for i, (tb, s) in enumerate(pairs) if s == sb]
        last = chosen[-1][1]
        total = acc[:, block(sb)]
        for k in range(PER_STEP):
            tiles = []
            for i, tb in chosen:
                start = reach - (tb - sb) * TILE
                tiles.append(slabs[k, :, start : start + TILE] * masks[i])
            total = total + product(
                both[k, :, sb * TILE : (last + 1) * TILE], jnp.concatenate(tiles, axis=0)
            )
        acc[:, block(sb)] = total


def lag_back_kernel(me, acc, lag_mixing, grads, inputs, pieces, scales, kept, given, gain):
    _, channels, model_width = lag_mixing.shape
    length = acc.shape[1]
    half, _, share = kept.shape
    ids = segment_row(pieces)
    lag_grad = contract_last(lag_mixing[...].reshape(AR * channels, model_width), grads[...])
    total = acc[:channels] + parity_lanes(channels, length) * acc[channels:]
    for j in range(AR):
        term = lag_grad[j * channels : (j + 1) * channels]
        if j:
            term = pltpu.roll(term * lag_keep(ids, j), length - j, 1)
        total = total + term
    back = total.astype(jnp.bfloat16)
    for i in range(2 * half):
        part = back[:, i * share : (i + 1) * share]
        other = i ^ me[0]
        place = other >> 1

        @pl.when((other & 1) == 0)
        def _(part=part, place=place):
            kept[place] = part

        @pl.when((other & 1) == 1)
        def _(part=part, place=place):
            given[place] = part

    weighed = back.astype(jnp.float32) * inputs[0].astype(jnp.float32)
    by_lane = jnp.broadcast_to(jnp.sum(weighed, axis=1, keepdims=True), (channels, 128))
    row = lax.broadcasted_iota(jnp.int32, by_lane.shape, 0)
    lane = lax.broadcasted_iota(jnp.int32, by_lane.shape, 1)
    total = jnp.sum(jnp.where(row == lane, by_lane, 0.0), axis=0, keepdims=True)
    gain[...] = jnp.broadcast_to(total / scales[...], gain.shape)


def toeplitz_scratch(length, count):
    width = slab_width(length)
    return [
        pltpu.VMEM((count, width), jnp.float32),
        pltpu.VMEM((PER_STEP, TILE, width), jnp.bfloat16),
        pltpu.VMEM((len(tile_pairs(length)), TILE, TILE), jnp.bfloat16),
    ]


def maps_scratch(channels, length, count):
    return [
        *toeplitz_scratch(length, count),
        pltpu.VMEM((2 * channels, length), jnp.bfloat16),
    ]


def spectral_maps(pieces, filters, channels, start, count, into=None):
    length = filters.shape[1]
    given = [] if into is None else [into]
    return pl.pallas_call(
        functools.partial(maps_kernel, start),
        grid=(count // PER_STEP,),
        in_specs=[
            whole(filters.shape),
            whole(pieces.shape),
            *[in_vmem() for _ in given],
        ],
        out_specs=[in_vmem(), whole((AR, channels, length))],
        out_shape=[
            pltpu.VMEM((2, K, channels, length), jnp.bfloat16),
            jax.ShapeDtypeStruct((AR, channels, length), jnp.bfloat16),
        ],
        scratch_shapes=maps_scratch(channels, length, filters.shape[0]),
        input_output_aliases={2: 0} if given else {},
        compiler_params=vmem(16),
        cost_estimate=pl.CostEstimate(
            flops=6 * channels * count * length * length, transcendentals=0, bytes_accessed=4 << 20
        ),
        name="spectral_maps",
    )(filters, pieces, *given)


def spectral_mixed(me, pieces, filters, mixing):
    owners, _, share = pieces.shape
    channels, model_width = mixing.shape[1:]
    count, length = filters.shape
    steps = count // PER_STEP
    cut = (owners // 4, 2, model_width // 2, share)
    mix_block = (PER_STEP, channels, model_width)
    return pl.pallas_call(
        mixed_kernel,
        grid_spec=pltpu.PrefetchScalarGridSpec(
            num_scalar_prefetch=1,
            grid=(steps,),
            in_specs=[
                whole(filters.shape),
                whole(pieces.shape),
                pl.BlockSpec(mix_block, lambda k, _: (k, 0, 0)),
                pl.BlockSpec(mix_block, lambda k, _: (k + steps, 0, 0)),
                pl.BlockSpec((AR, channels, model_width), lambda k, _: (2 * count // AR, 0, 0)),
            ],
            out_specs=[in_vmem(), whole((AR, channels, length)), *[whole(cut)] * 4],
            scratch_shapes=[
                *maps_scratch(channels, length, count),
                pltpu.VMEM((owners, model_width, share), jnp.float32),
            ],
        ),
        out_shape=[
            pltpu.VMEM((2, count, channels, length), jnp.bfloat16),
            jax.ShapeDtypeStruct((AR, channels, length), jnp.bfloat16),
            *[jax.ShapeDtypeStruct(cut, jnp.bfloat16)] * 4,
        ],
        compiler_params=vmem(24),
        name="spectral_mixed",
    )(me, filters, pieces, *[in_hbm(mixing)] * 3)


def spectral_back(grads, mixing, filters, pieces):
    channels, model_width = mixing.shape[1:]
    count, length = filters.shape
    steps = count // PER_STEP
    mix_block = (PER_STEP, channels, model_width)
    return pl.pallas_call(
        spectral_back_kernel,
        grid=(steps,),
        in_specs=[
            whole(filters.shape),
            pl.BlockSpec(mix_block, lambda k: (k, 0, 0)),
            pl.BlockSpec(mix_block, lambda k: (k + steps, 0, 0)),
            whole(pieces.shape),
            whole(grads.shape),
        ],
        out_specs=whole((2 * channels, length)),
        scratch_shapes=[
            *toeplitz_scratch(length, count),
            pltpu.VMEM((PER_STEP, 2 * channels, length), jnp.bfloat16),
        ],
        out_shape=jax.ShapeDtypeStruct((2 * channels, length), jnp.float32),
        compiler_params=vmem(24),
        name="spectral_back",
    )(filters, *[in_hbm(mixing)] * 2, pieces, grads)


def lag_back(me, acc, mixing, grads, lags, pieces, scales):
    channels, model_width = mixing.shape[1:]
    owners, _, share = pieces.shape
    sent = (owners // 2, channels, share)
    return pl.pallas_call(
        lag_back_kernel,
        grid_spec=pltpu.PrefetchScalarGridSpec(
            num_scalar_prefetch=1,
            grid=(1,),
            in_specs=[
                whole(acc.shape),
                pl.BlockSpec((AR, channels, model_width), lambda k, _: (2 * K // AR, 0, 0)),
                whole(grads.shape),
                pl.BlockSpec((1, *lags.shape[1:]), lambda k, _: (0, 0, 0)),
                whole(pieces.shape),
                whole(scales.shape),
            ],
            out_specs=[whole(sent), whole(sent), whole((8, 128))],
        ),
        out_shape=[
            jax.ShapeDtypeStruct(sent, jnp.bfloat16),
            jax.ShapeDtypeStruct(sent, jnp.bfloat16),
            jax.ShapeDtypeStruct((8, 128), jnp.float32),
        ],
        compiler_params=vmem(16),
        name="lag_back",
    )(me, acc, in_hbm(mixing), grads, lags, pieces, scales)


def gelu_parts(gate_value, upper_value, hidden_grad):
    slope = math.sqrt(2 / math.pi)
    square = gate_value * gate_value
    tanh = jnp.tanh(slope * gate_value * (1.0 + 0.044715 * square))
    rise = 0.5 * (1.0 + tanh)
    gelu = gate_value * rise
    bend = 0.5 * slope * (1.0 - tanh * tanh) * (1.0 + 3 * 0.044715 * square)
    return (
        gelu * upper_value,
        hidden_grad * upper_value * (rise + gate_value * bend),
        hidden_grad * gelu,
    )


def feed_forward_kernel(
    bit,
    held,
    got,
    hidden_in,
    gain,
    cotangent,
    gate,
    up,
    down,
    output,
    normed_out,
    grad,
    grad_low,
    normed,
    resid,
    acc,
    normed_grad,
):
    step = pl.program_id(0)
    share = resid.shape[0]

    @pl.when(step == 0)
    def _():
        mixed = held[bit[0]].astype(jnp.float32) + got[...].astype(jnp.float32)
        resid[...] = hidden_in[0].astype(jnp.float32) + mixed.T
        normed[...] = rms_scale(resid[...], gain[...]).astype(jnp.bfloat16)
        acc[...] = jnp.zeros_like(acc)
        normed_grad[...] = jnp.zeros_like(normed_grad)

    gate_value = product(normed[...], gate[...])
    upper_value = product(normed[...], up[...])
    hidden_grad = contract_last(cotangent[0], down[...])
    hidden, gate_back, upper_back = gelu_parts(gate_value, upper_value, hidden_grad)
    acc[...] += product(hidden.astype(jnp.bfloat16), down[...])
    normed_grad[...] += contract_last(gate_back.astype(jnp.bfloat16), gate[...]) + contract_last(
        upper_back.astype(jnp.bfloat16), up[...]
    )

    @pl.when(step == pl.num_programs(0) - 1)
    def _():
        value, back = resid[...], normed_grad[...]
        output[0] = (value + acc[...]).astype(jnp.bfloat16)
        scale = lax.rsqrt(jnp.mean(value * value, axis=-1, keepdims=True) + eps_norm)
        weighed = back * gain[...]
        along = jnp.mean(weighed * value, axis=-1, keepdims=True)
        total = cotangent[0].astype(jnp.float32) + scale * (
            weighed - value * (scale * scale * along)
        )
        grad[...] = total
        grad_low[...] = total.astype(jnp.bfloat16)
        gains = jnp.sum(back * value * scale, axis=0, keepdims=True)
        high = jnp.broadcast_to(gains, (16, gains.shape[1])).astype(jnp.bfloat16)
        low = (gains - high.astype(jnp.float32)).astype(jnp.bfloat16)
        row = lax.broadcasted_iota(jnp.int32, low.shape, 0)
        normed_out[:share, :] = normed[...]
        normed_out[share:, :] = jnp.where(row < 8, high, low)


def feed_forward(bit, held, got, hidden_in, gain, cotangent, w_gate, w_up, w_down):
    _, share, width = hidden_in.shape
    steps = 4
    units = w_gate.shape[1] // steps
    tokens = (share, width)
    return pl.pallas_call(
        feed_forward_kernel,
        grid_spec=pltpu.PrefetchScalarGridSpec(
            num_scalar_prefetch=1,
            grid=(steps,),
            in_specs=[
                whole(held.shape),
                whole(got.shape),
                whole(hidden_in.shape),
                whole((1, width)),
                whole(cotangent.shape),
                pl.BlockSpec((width, units), lambda k, _: (0, k)),
                pl.BlockSpec((width, units), lambda k, _: (0, k)),
                pl.BlockSpec((units, width), lambda k, _: (k, 0)),
            ],
            out_specs=[
                whole(hidden_in.shape),
                whole((share + 16, width)),
                whole(tokens),
                whole(tokens),
            ],
            scratch_shapes=[
                pltpu.VMEM(tokens, jnp.bfloat16),
                *[pltpu.VMEM(tokens, jnp.float32)] * 3,
            ],
        ),
        out_shape=[
            jax.ShapeDtypeStruct(hidden_in.shape, jnp.bfloat16),
            jax.ShapeDtypeStruct((share + 16, width), jnp.bfloat16),
            jax.ShapeDtypeStruct(tokens, jnp.float32),
            jax.ShapeDtypeStruct(tokens, jnp.bfloat16),
        ],
        compiler_params=vmem(16),
        name="feed_forward",
    )(bit, held, got, hidden_in, gain[None, :], cotangent, w_gate, w_up, w_down)


CHUNK = 6


def own_mixing_grad_kernel(maps, lags, grads, out, lag_out):
    def chunk(index, _):
        own = pl.ds(index * CHUNK, CHUNK)
        for which in range(2):
            values = maps[which, own]
            total = product(values.reshape(-1, values.shape[-1]), grads[...])
            out[which, own] = total.astype(out.dtype).reshape(CHUNK, *out.shape[2:])

    lax.fori_loop(0, maps.shape[1] // CHUNK, chunk, None)
    values = lags[...].reshape(-1, lags.shape[-1])
    lag_out[...] = product(values, grads[...]).astype(out.dtype).reshape(lag_out.shape)


def own_mixing_grad(maps, lags, grads):
    _, count, channels, _ = maps.shape
    width = grads.shape[1]
    return pl.pallas_call(
        own_mixing_grad_kernel,
        in_specs=[in_vmem()] * 3,
        out_specs=[in_vmem()] * 2,
        out_shape=[
            pltpu.VMEM((2, count, channels, width), jnp.bfloat16),
            pltpu.VMEM((AR, channels, width), jnp.bfloat16),
        ],
        compiler_params=vmem(16),
        name="own_mixing_grad",
    )(maps, lags, grads)


def mixing_grad_kernel(which, maps, lags, grads, own, own_lags, out):
    def total(values, mine):
        values = product(values.reshape(-1, values.shape[-1]), grads[...])
        return (values + mine.reshape(values.shape).astype(jnp.float32)).astype(out.dtype)

    count, channels = maps.shape[1:3]

    def chunk(index, _):
        part = pl.ds(index * CHUNK, CHUNK)
        start = pl.multiple_of(index * CHUNK * channels, CHUNK * channels)
        out[pl.ds(start, CHUNK * channels), :] = total(maps[which, part], own[which, part])

    lax.fori_loop(0, count // CHUNK, chunk, None)
    if which:
        out[count * channels :, :] = total(lags[...], own_lags[...])


def mixing_grad(which, maps, lags, grads, own, own_lags):
    _, count, channels, _ = maps.shape
    shape = ((count + which * AR) * channels, grads.shape[1])
    return pl.pallas_call(
        functools.partial(mixing_grad_kernel, which),
        in_specs=[in_vmem()] * 5,
        out_specs=in_vmem(),
        out_shape=pltpu.VMEM(shape, jnp.bfloat16),
        compiler_params=vmem(16),
        name="mixing_grad",
    )(maps, lags, grads, own, own_lags)


def finish_mixing_kernel(part, got, *refs):
    out = refs[-1]
    out[...] = (part[...].astype(jnp.float32) + got[...].astype(jnp.float32)).reshape(out.shape)


def finish_mixing(part, got, first, total, into=None):
    channels = total[1]
    count = part.shape[0] // channels
    steps = 3
    size = count // steps
    given = [] if into is None else [into]
    return pl.pallas_call(
        finish_mixing_kernel,
        grid=(steps,),
        in_specs=[
            pl.BlockSpec((size * channels, total[2]), lambda k: (k, 0)),
            pl.BlockSpec((size * channels, total[2]), lambda k: (k, 0)),
            *[pl.BlockSpec(memory_space=pl.ANY) for _ in given],
        ],
        out_specs=pl.BlockSpec(
            tuple(map(pl.Element, (size, *total[1:]))), lambda k: (first + k * size, 0, 0)
        ),
        out_shape=jax.ShapeDtypeStruct(total, jnp.float32),
        input_output_aliases={2: 0} if given else {},
        compiler_params=vmem(16),
        name="finish_mixing",
    )(part, got, *given)


def unit_rows(width, units):
    blocks = width // units // 2
    return [width + units * i for i in range(blocks)], width + units * blocks + 16


def unit_grads_kernel(channels, me, *refs):
    *parts, gate, up, down, first_gain, out, normed, cotangent = refs
    place_tokens(me[0], parts[:4], normed)
    place_tokens(me[0], parts[4:], cotangent)
    width, units = gate.shape
    hidden_grad = contract_last(cotangent[...], down[...])
    gate_value = product(normed[...], gate[...])
    upper_value = product(normed[...], up[...])
    hidden, gate_back, upper_back = gelu_parts(gate_value, upper_value, hidden_grad)
    gate_part = contract_first(normed[...], gate_back.astype(jnp.bfloat16))
    up_part = contract_first(normed[...], upper_back.astype(jnp.bfloat16))
    down_part = contract_first(hidden.astype(jnp.bfloat16), cotangent[...]).astype(jnp.bfloat16)
    starts, size = unit_rows(width, units)
    out[0, :width] = gate_part.astype(jnp.bfloat16)
    out[1, :width] = up_part.astype(jnp.bfloat16)
    for i in range(2 * len(starts)):
        half, start = i // len(starts), starts[i % len(starts)]
        out[half, start : start + units] = down_part[:, i * units : (i + 1) * units]
    share_rows = parts[0].shape[2]
    second = jnp.zeros((16, width), jnp.float32)
    for part in parts[2:4]:
        for a in range(2):
            for r in range(part.shape[1]):
                second = second + part[a, r, share_rows:, :].astype(jnp.float32)
    second = second[:8] + second[8:]
    second = pltpu.roll(second, lax.rem(width - me[0] * channels, width), 1)
    out[0, size - 16 :] = jnp.zeros((16, units), jnp.bfloat16)
    out[1, size - 16 :] = jnp.zeros((16, units), jnp.bfloat16)
    lanes = first_gain.shape[1]
    gains = jnp.concatenate([second[:, :lanes], first_gain[...]], axis=0)
    out[0, size - 16 :, :lanes] = gains.astype(jnp.bfloat16)


def unit_grads(me, normed_parts, cotangent_parts, w_gate, w_up, w_down, first_gain):
    width, hidden = w_gate.shape
    chans = lax.axis_size("chan")
    units = hidden // chans
    parts = [*normed_parts, *cotangent_parts]
    tokens = 2 * sum(math.prod(part.shape[:-1]) for part in normed_parts[:2])
    shape = (2, unit_rows(width, units)[1], units)
    return pl.pallas_call(
        functools.partial(unit_grads_kernel, width // chans),
        grid_spec=pltpu.PrefetchScalarGridSpec(
            num_scalar_prefetch=1,
            grid=(1,),
            in_specs=[
                *[whole(part.shape) for part in parts],
                pl.BlockSpec((width, units), lambda k, me: (0, me[0])),
                pl.BlockSpec((width, units), lambda k, me: (0, me[0])),
                pl.BlockSpec((units, width), lambda k, me: (me[0], 0)),
                whole(first_gain.shape),
            ],
            out_specs=whole(shape),
            scratch_shapes=[pltpu.VMEM((tokens, width), jnp.bfloat16)] * 2,
        ),
        out_shape=jax.ShapeDtypeStruct(shape, jnp.bfloat16),
        compiler_params=vmem(24),
        name="unit_grads",
    )(me, *parts, in_hbm(w_gate), in_hbm(w_up), in_hbm(w_down), first_gain)


def finish_units_kernel(core, mine, other, gate, up, down, gains):
    width, units = gate.shape
    starts, size = unit_rows(width, units)
    for which, (low, high) in enumerate(((mine, other), (other, mine))):

        @pl.when(core[0] == which)
        def _(low=low, high=high):
            gate[...] = low[:width].astype(jnp.float32)
            up[...] = high[:width].astype(jnp.float32)
            for i in range(2 * len(starts)):
                source, start = (low, high)[i // len(starts)], starts[i % len(starts)]
                part = source[start : start + units].astype(jnp.float32)
                down[:, i * units : (i + 1) * units] = part
            gains[...] = low[size - 16 :].astype(jnp.float32)


def finish_units(core, mine, other, width):
    units = mine.shape[1]
    shapes = [(width, units), (width, units), (units, width), (16, units)]
    return pl.pallas_call(
        finish_units_kernel,
        grid_spec=pltpu.PrefetchScalarGridSpec(
            num_scalar_prefetch=1,
            grid=(1,),
            in_specs=[whole(mine.shape), whole(mine.shape)],
            out_specs=[whole(shape) for shape in shapes],
        ),
        out_shape=[jax.ShapeDtypeStruct(shape, jnp.float32) for shape in shapes],
        compiler_params=vmem(16),
        name="finish_units",
    )(core, mine, other)


def swap(values, axis, mask):
    count = lax.axis_size(axis)
    return lax.ppermute(values, axis, [(i, i ^ mask) for i in range(count)])


def bits_of(axis):
    return [1 << b for b in range(lax.axis_size(axis).bit_length() - 1)]


def entry(values, index, dim):
    return lax.dynamic_slice_in_dim(values, index, 1, dim, allow_negative_indices=False)


def join(mine, other, high, dim):
    return jnp.where(
        high, jnp.concatenate([other, mine], dim), jnp.concatenate([mine, other], dim)
    )


def tie(*values):
    return lax.optimization_barrier(values)


def gather_round(held, mask, bits):
    return join(held[None], swap(held, "chan", mask)[None], bits[mask][0] != 0, 0)


class Gather:
    def __init__(self, values, half, bits):
        masks = bits_of("chan")
        self.half, self.bits = half, bits
        self.shape = values.shape
        self.common = masks[2:]
        self.orders = [(masks[1], masks[0]), (masks[0], masks[1])]
        self.held = values[None]

    def first(self):
        for mask in self.common:
            self.held = gather_round(self.held, mask, self.bits).reshape(-1, *self.shape)
        return self.held

    def second(self):
        self.halves = [self.held[:, : self.half], self.held[:, self.half :]]
        self.halves = [
            gather_round(h, order[0], self.bits)
            for h, order in zip(self.halves, self.orders, strict=True)
        ]
        return self.halves

    def third(self):
        self.others = [
            swap(h, "chan", order[1]) for h, order in zip(self.halves, self.orders, strict=True)
        ]
        return self.others

    def parts(self):
        return (self.halves[0], self.others[0], self.halves[1], self.others[1])


def add(left, right):
    return left.astype(jnp.float32) + right.astype(jnp.float32)


def own_entry(values, mask, dim, bits):
    return add(*exchange(values, mask, dim, bits)).squeeze(dim)


def exchange_rest(kept, came):
    count = 2 * kept.shape[0]
    held = jnp.stack([kept, came], axis=1).reshape(count, *kept.shape[1:])
    for mask in bits_of("chan")[1:]:
        split = held.reshape(-1, 2, mask, *held.shape[1:])
        kept, came = split[:, 0], swap(split[:, 1], "chan", mask)
        held = jnp.stack([kept, came], axis=1).reshape(held.shape)
    return kept.reshape(count // 2, *held.shape[1:]), came.reshape(count // 2, *held.shape[1:])


def exchange(values, mask, dim, bits):
    keep, give = (entry(values, bit, dim) for bit in bits[mask])
    return keep, swap(give, "chan", mask)


def scatter_tokens(keep0, give0, keep1, give1, beside, bits):
    masks = bits_of("chan")
    got0, got1 = swap(give0, "chan", masks[0]), swap(give1, "chan", masks[1])
    half0 = add(keep0, got0).astype(jnp.bfloat16)
    half1 = add(keep1, got1).astype(jnp.bfloat16)
    half0, half1, *beside = tie(half0, half1, *beside)
    half0 = own_entry(half0, masks[1], 1, bits)
    half1 = own_entry(half1, masks[0], 1, bits)
    held = jnp.concatenate([half0, half1], axis=1)
    for mask in masks[:2:-1]:
        held = held.astype(jnp.bfloat16).reshape(2, -1, *held.shape[1:])
        held = own_entry(held, mask, 0, bits)
    held = held.astype(jnp.bfloat16)
    return held, exchange(held, masks[2], 0, bits)[1][0], beside


def shards(
    hidden_in, segments, filters, gain_one, mixing, gain_two, w_gate, w_up, w_down, out_grad
):
    chans = lax.axis_size("chan")
    me = lax.axis_index("chan").astype(jnp.int32)
    at = me.reshape(1)
    _, share, width = hidden_in.shape
    channels = width // chans
    core = lax.axis_index("rows").astype(jnp.int32) & 1
    other_core = 1 - core
    bits = [(me >> b) & 1 for b in range(len(bits_of("chan")))]
    bits = [bit ^ flip for bit in bits for flip in range(2)]
    scales = lax.dynamic_slice_in_dim(gain_one, me * channels, channels)
    scales = jnp.pad(scales, (0, 128 - channels), constant_values=1.0)[None, :]
    hidden_in, scales, at, core, other_core, *bits = tie(
        hidden_in, scales, at, core, other_core, *bits
    )
    bits = dict(zip(bits_of("chan"), zip(bits[::2], bits[1::2], strict=True), strict=True))
    cotangent_gather = Gather(out_grad[0], share // 2, bits)
    cotangent_gather.first()
    pieces = lax.all_to_all(
        first_norm(at, hidden_in, gain_one, segments, chans),
        "chan",
        split_axis=0,
        concat_axis=0,
    )
    peer_pieces = swap(pieces, "rows", 2)
    maps, lags, *cut = spectral_mixed(at, pieces, filters, mixing)
    peer_pieces, lags = tie(peer_pieces, lags)
    peer_maps, peer_lags = spectral_maps(peer_pieces, filters, channels, 0, K // 2)
    cotangent_gather.second()
    lags, *cotangent_gather.halves = tie(lags, *cotangent_gather.halves)
    beside = (peer_maps, *cotangent_gather.third())
    held, got, (peer_maps, *cotangent_gather.others) = scatter_tokens(*cut, beside, bits)
    last_bit = bits[4][0].reshape(1)
    output, normed_two, resid_grad, resid_low = feed_forward(
        last_bit, held, got, hidden_in, gain_two, out_grad, w_gate, w_up, w_down
    )
    grad_gather = Gather(resid_low, share // 2, bits)
    first = grad_gather.first()
    peer_pieces, resid_grad = tie(peer_pieces, resid_grad)
    peer_maps, _ = spectral_maps(peer_pieces, filters, channels, K // 2, K // 2, peer_maps)
    normed_two, grad_gather.held, peer_maps = tie(normed_two, first, peer_maps)
    normed_gather = Gather(normed_two, share // 2, bits)
    normed_gather.first()
    grad_gather.second()
    normed_gather.second()
    grad_gather.third()
    normed_gather.third()
    full_grad = place(at, grad_gather.parts())
    peer_grad = swap(full_grad, "rows", 2)
    acc = spectral_back(full_grad, mixing, filters, pieces)
    back, give, first_local = lag_back(at, acc, mixing, full_grad, lags, pieces, scales)
    came = swap(give, "chan", 1)
    first_local, *normed_parts = tie(first_local, *normed_gather.parts())
    unit_parts = unit_grads(
        at, normed_parts, cotangent_gather.parts(), w_gate, w_up, w_down, first_local
    )
    unit_parts, full_grad, back, came = tie(unit_parts, full_grad, back, came)
    back, came = exchange_rest(back, came)
    keep = entry(unit_parts, core, 0)[0]
    unit_given = swap(entry(unit_parts, other_core, 0)[0], "rows", 1)
    own, own_lags = own_mixing_grad(maps, lags, full_grad)
    own_lags, unit_given = tie(own_lags, unit_given)
    unit_half = add(keep, unit_given).astype(jnp.bfloat16)
    unit_half, peer_grad = tie(unit_half, peer_grad)
    unit_other = swap(unit_half, "rows", 2)
    first_part = mixing_grad(0, peer_maps, peer_lags, peer_grad, own, own_lags)
    first_part, peer_grad = tie(first_part, peer_grad)
    second_part = mixing_grad(1, peer_maps, peer_lags, peer_grad, own, own_lags)
    second_part, came, unit_other = tie(second_part, came, unit_other)
    input_total = first_norm_back(at, back, came, hidden_in, gain_one, resid_grad)
    unit_half = add(unit_half, unit_other).astype(jnp.bfloat16)
    for mask in bits_of("rows")[2:]:
        unit_half = add(unit_half, swap(unit_half, "rows", mask)).astype(jnp.bfloat16)
    gate_sum, up_sum, down_sum, gains = finish_units(
        core.reshape(1), unit_half, swap(unit_half, "rows", 1), width
    )
    mixing_sum = None
    for part, first in ((first_part, 0), (second_part, K)):
        masks = [1, *bits_of("rows")[2:]]
        for mask in masks[:-1]:
            part = add(part, swap(part, "rows", mask)).astype(jnp.bfloat16)
        got = swap(part, "rows", masks[-1])
        mixing_sum = finish_mixing(part, got, first, mixing.shape, mixing_sum)
    return (
        output,
        input_total,
        mixing_sum,
        gate_sum,
        up_sum,
        down_sum,
        gains[8, :channels],
        gains[0, :channels],
    )


def solution(mesh):
    in_specs = (
        P("rows", "chan", None),
        P("rows", None),
        P(),
        P(),
        P(None, "chan", None),
        P(),
        P(),
        P(),
        P(),
        P("rows", "chan", None),
    )
    out_specs = (
        P("rows", "chan", None),
        P("rows", "chan", None),
        P(None, "chan", None),
        P(None, "chan"),
        P(None, "chan"),
        P("chan", None),
        P("chan"),
        P("chan"),
    )
    return jax.shard_map(shards, mesh=mesh, in_specs=in_specs, out_specs=out_specs, check_vma=False)
```

```python
import functools
import math

import jax
import jax.numpy as jnp
from jax import lax
from jax.experimental import pallas as pl
from jax.experimental.pallas import tpu as pltpu
from jax.sharding import PartitionSpec as P

K = 24
AR = 3
TILE = 256
HALF = 128
PER_STEP = 8

eps_norm = 1e-05


def rms_scale(values, scales):
    return values * lax.rsqrt(jnp.mean(values * values, axis=-1, keepdims=True) + eps_norm) * scales


def contract_first(left, right):
    return lax.dot_general(
        left, right, (((0,), (0,)), ((), ())), preferred_element_type=jnp.float32
    )


def contract_last(left, right):
    return lax.dot_general(
        left, right, (((1,), (1,)), ((), ())), preferred_element_type=jnp.float32
    )


def product(left, right):
    return jnp.dot(left, right, preferred_element_type=jnp.float32)


def in_hbm(value):
    return pltpu.with_memory_space_constraint(value, pltpu.HBM)


def in_vmem():
    return pl.BlockSpec(memory_space=pltpu.VMEM)


def whole(shape):
    return pl.BlockSpec(shape, lambda *_: (0,) * len(shape))


def vmem(mebibytes):
    return pltpu.CompilerParams(vmem_limit_bytes=mebibytes << 20)


def first_norm_kernel(me, hidden, gain, segments, pieces):
    count, rows, share = pieces.shape
    channels = hidden.shape[2] // count
    normed = rms_scale(hidden[0].astype(jnp.float32), gain[...])
    normed = normed.T.astype(jnp.bfloat16)
    ids = segments[:, pl.ds(pl.multiple_of(me[0] * share, share), share)]
    ids = jnp.broadcast_to(ids.astype(jnp.float32), (rows - channels, share)).astype(jnp.bfloat16)
    for i in range(count):
        pieces[i, :channels, :] = normed[i * channels : (i + 1) * channels]
        pieces[i, channels:, :] = ids


def first_norm(me, hidden_in, gain, segments, count):
    _, share, width = hidden_in.shape
    shape = (count, width // count + 16, share)
    return pl.pallas_call(
        first_norm_kernel,
        grid_spec=pltpu.PrefetchScalarGridSpec(
            num_scalar_prefetch=1,
            grid=(1,),
            in_specs=[whole(hidden_in.shape), whole((1, width)), whole(segments.shape)],
            out_specs=whole(shape),
        ),
        out_shape=jax.ShapeDtypeStruct(shape, jnp.bfloat16),
        compiler_params=vmem(8),
        name="first_norm",
    )(me, in_hbm(hidden_in), in_hbm(gain[None, :]), in_hbm(segments))


def first_norm_back_kernel(me, kept, came, hidden, gain, grad, out):
    half, channels, share = kept.shape
    parts = []
    for i in range(2 * half):
        other = i ^ me[0]
        pick = jnp.where(other < half, kept[other % half], came[other % half])
        parts.append(pick.astype(jnp.float32))
    normed_grad = jnp.concatenate(parts, axis=0).T
    tokens = hidden[0].astype(jnp.float32)
    scale = lax.rsqrt(jnp.mean(tokens * tokens, axis=-1, keepdims=True) + eps_norm)
    weighed = normed_grad * gain[...]
    along = jnp.mean(weighed * tokens, axis=-1, keepdims=True)
    out[0] = grad[...] + scale * (weighed - tokens * (scale * scale * along))


def first_norm_back(me, kept, came, hidden_in, gain, grad):
    _, share, width = hidden_in.shape
    return pl.pallas_call(
        first_norm_back_kernel,
        grid_spec=pltpu.PrefetchScalarGridSpec(
            num_scalar_prefetch=1,
            grid=(1,),
            in_specs=[in_vmem()] * 5,
            out_specs=whole(hidden_in.shape),
        ),
        out_shape=jax.ShapeDtypeStruct(hidden_in.shape, jnp.float32),
        compiler_params=vmem(8),
        name="first_norm_back",
    )(me, kept, came, hidden_in, gain[None, :], grad)


def tile_pairs(length):
    blocks, reach = length // TILE, length // 2 // TILE
    return [(tb, sb) for tb in range(blocks) for sb in range(max(0, tb - reach), tb + 1)]


def slab_width(length):
    return length // 2 + TILE


def parity_lanes(rows, lanes, dtype=jnp.float32):
    lane = lax.broadcasted_iota(jnp.int32, (rows, lanes), 1)
    return (1 - 2 * (lane % 2)).astype(dtype)


def block(index):
    return slice(index * TILE, (index + 1) * TILE)


def segment_row(pieces):
    row = pieces.shape[1] - 8
    return jnp.concatenate(
        [pieces[i, row:, :].astype(jnp.float32) for i in range(pieces.shape[0])], axis=1
    )


def build_masks(ids, masks, length, targets_in_rows):
    row = lax.broadcasted_iota(jnp.int32, (TILE, TILE), 0)
    col = lax.broadcasted_iota(jnp.int32, (TILE, TILE), 1)
    in_lanes = [jnp.broadcast_to(ids[:1, block(b)], (TILE, TILE)) for b in range(length // TILE)]
    in_rows = [value.T for value in in_lanes]
    for index, (tb, sb) in enumerate(tile_pairs(length)):
        rows_of, lanes_of = (tb, sb) if targets_in_rows else (sb, tb)
        same = in_rows[rows_of] == in_lanes[lanes_of]
        if tb == sb:
            same = same & ((row >= col) if targets_in_rows else (col >= row))
        masks[index] = jnp.where(same, 1.0, 0.0).astype(jnp.bfloat16)


def lag_keep(ids, lag):
    lane = lax.broadcasted_iota(jnp.int32, ids.shape, 1)
    same = (pltpu.roll(ids, lag, 1) == ids) & (lane >= lag)
    return jnp.where(same, 1.0, 0.0)[:1]


def build_slab(taps, slab, width):
    rolled = pltpu.roll(jnp.broadcast_to(taps, (HALF, width)), 0, 1, stride=1, stride_axis=0)
    rolled = rolled.astype(jnp.bfloat16)
    slab[:HALF, :] = rolled
    slab[HALF:, HALF:] = rolled[:, : width - HALF]
    slab[HALF:, :HALF] = rolled[:, :HALF]


def start_maps(filters, pieces, lags, taps, masks, doubled):
    count, _, share = pieces.shape
    channels, length = lags.shape[1:]
    ids = segment_row(pieces)
    build_masks(ids, masks, length, False)
    taps[...] = filters[:, : taps.shape[1]].astype(jnp.float32)
    sign = parity_lanes(channels, share, jnp.bfloat16)
    for i in range(count):
        part = pieces[i, :channels, :]
        doubled[:channels, i * share : (i + 1) * share] = part
        doubled[channels:, i * share : (i + 1) * share] = part * sign
    inputs = doubled[:channels, :]
    lags[0] = inputs
    inputs = inputs.astype(jnp.float32)
    for j in range(1, AR):
        lags[j] = (pltpu.roll(inputs, j, 1) * lag_keep(ids, j)).astype(jnp.bfloat16)


def step_maps(first, maps, taps, slabs, masks, doubled):
    channels, length = maps.shape[2:]
    width = taps.shape[1]
    pairs = tile_pairs(length)
    parity = parity_lanes(channels, TILE)
    for k in range(slabs.shape[0]):
        slab = slabs.at[k]
        build_slab(taps[pl.ds(first + k, 1), :], slab, width)
        for tb in range(length // TILE):
            chosen = [(i, sb) for i, (t, sb) in enumerate(pairs) if t == tb]
            tiles = [slab[:, block(tb - sb)] * masks[i] for i, sb in chosen]
            low = chosen[0][1]
            both = product(
                doubled[:, low * TILE : (tb + 1) * TILE], jnp.concatenate(tiles, axis=0)
            )
            maps[0, first + k, :, block(tb)] = both[:channels].astype(jnp.bfloat16)
            maps[1, first + k, :, block(tb)] = (both[channels:] * parity).astype(jnp.bfloat16)


def maps_kernel(start, filters, pieces, *refs):
    maps, lags, taps, slabs, masks, doubled = refs[-6:]
    start_maps(filters, pieces, lags, taps, masks, doubled)
    step_maps(start, maps, taps, slabs, masks, doubled)


def mixed_kernel(
    me,
    filters,
    pieces,
    mixing_given,
    maps,
    lags,
    keep0,
    give0,
    keep1,
    give1,
    taps,
    slabs,
    masks,
    doubled,
    acc,
    mixing,
    arrived,
):
    _, _, model_width = mixing.shape
    count, _, share = pieces.shape
    filter_count, length = maps.shape[1], lags.shape[2]
    step = pl.program_id(0)

    copy = pltpu.make_async_copy(mixing_given, mixing, arrived)

    @pl.when(step == 0)
    def _():
        copy.start()
        start_maps(filters, pieces, lags, taps, masks, doubled)
        acc[...] = jnp.zeros_like(acc)

    step_maps(step * PER_STEP, maps, taps, slabs, masks, doubled)

    @pl.when(step == 0)
    def _():
        copy.wait()

    def part(weights, values):
        return contract_first(weights.reshape(-1, model_width), values.reshape(-1, length))

    plus = pl.ds(step * PER_STEP, PER_STEP)
    minus = pl.ds(filter_count + step * PER_STEP, PER_STEP)
    total = part(mixing[plus], maps[0, plus]) + part(mixing[minus], maps[1, plus])
    for i in range(count):
        acc[i] += total[:, i * share : (i + 1) * share]

    @pl.when(step == pl.num_programs(0) - 1)
    def _():
        last = part(mixing[2 * filter_count :], lags[...])
        for i in range(count):
            acc[i] += last[:, i * share : (i + 1) * share]
        half = model_width // 2
        low, near = me[0] & 1, (me[0] >> 1) & 1
        for r in range(count // 4):
            for a in range(2):
                for other, (out0, out1) in enumerate(((keep0, keep1), (give0, give1))):
                    out0[r, a] = acc[r * 4 + a * 2 + (low ^ other), :half].astype(jnp.bfloat16)
                    out1[r, a] = acc[r * 4 + (near ^ other) * 2 + a, half:].astype(jnp.bfloat16)


def place_tokens(me, parts, out):
    rows = parts[0].shape[2]
    for half, pair in enumerate((parts[:2], parts[2:])):
        for other, part in enumerate(pair):
            low, near = me & 1, (me >> 1) & 1
            for a in range(2):
                for r in range(part.shape[1]):
                    if half == 0:
                        owner = r * 4 + a * 2 + (low ^ other)
                    else:
                        owner = r * 4 + (near ^ other) * 2 + a
                    start = pl.multiple_of((owner * 2 + half) * rows, rows)
                    out[pl.ds(start, rows), :] = part[a, r, :rows, :]


def place_kernel(me, part0, part1, part2, part3, out):
    place_tokens(me[0], (part0, part1, part2, part3), out)


def place(me, parts):
    count = 2 * sum(math.prod(part.shape[:-1]) for part in parts[:2])
    shape = (count, parts[0].shape[-1])
    return pl.pallas_call(
        place_kernel,
        grid_spec=pltpu.PrefetchScalarGridSpec(
            num_scalar_prefetch=1,
            grid=(1,),
            in_specs=[in_vmem()] * 4,
            out_specs=in_vmem(),
        ),
        out_shape=pltpu.VMEM(shape, jnp.bfloat16),
        compiler_params=vmem(8),
        name="place",
    )(me, *parts)


def spectral_back_kernel(filters, mixing, pieces, grads, acc, taps, slabs, masks, both):
    _, channels, model_width = mixing.shape
    count = filters.shape[0]
    length, width = acc.shape[1], taps.shape[1]
    reach = length // 2
    pairs = tile_pairs(length)
    rows = PER_STEP * channels
    step = pl.program_id(0)

    @pl.when(step == 0)
    def _():
        build_masks(segment_row(pieces), masks, length, True)
        acc[...] = jnp.zeros_like(acc)
        source = lax.broadcasted_iota(jnp.int32, (width, width), 0)
        target = lax.broadcasted_iota(jnp.int32, (width, width), 1)
        flip = jnp.where(source + target == reach, 1.0, 0.0).astype(jnp.bfloat16)
        taps[...] = product(filters[:, :width], flip)

    sign = parity_lanes(rows, length, jnp.bfloat16)
    plus = contract_last(
        mixing[pl.ds(step * PER_STEP, PER_STEP)].reshape(rows, model_width), grads[...]
    )
    both[:, :channels, :] = plus.astype(jnp.bfloat16).reshape(PER_STEP, channels, length)
    minus = contract_last(
        mixing[pl.ds(count + step * PER_STEP, PER_STEP)].reshape(rows, model_width), grads[...]
    )
    both[:, channels:, :] = (minus.astype(jnp.bfloat16) * sign).reshape(
        PER_STEP, channels, length
    )
    for k in range(PER_STEP):
        build_slab(taps[pl.ds(step * PER_STEP + k, 1), :], slabs.at[k], width)
    for sb in range(length // TILE):
        chosen = [(i, tb) for i, (tb, s) in enumerate(pairs) if s == sb]
        last = chosen[-1][1]
        total = acc[:, block(sb)]
        for k in range(PER_STEP):
            tiles = []
            for i, tb in chosen:
                start = reach - (tb - sb) * TILE
                tiles.append(slabs[k, :, start : start + TILE] * masks[i])
            total = total + product(
                both[k, :, sb * TILE : (last + 1) * TILE], jnp.concatenate(tiles, axis=0)
            )
        acc[:, block(sb)] = total


def lag_back_kernel(me, acc, mixing, grads, inputs, pieces, scales, kept, given, gain):
    _, channels, model_width = mixing.shape
    length = acc.shape[1]
    half, _, share = kept.shape
    ids = segment_row(pieces)
    lag_grad = contract_last(mixing[2 * K :].reshape(AR * channels, model_width), grads[...])
    total = acc[:channels] + parity_lanes(channels, length) * acc[channels:]
    for j in range(AR):
        term = lag_grad[j * channels : (j + 1) * channels]
        if j:
            term = pltpu.roll(term * lag_keep(ids, j), length - j, 1)
        total = total + term
    back = total.astype(jnp.bfloat16)
    for i in range(2 * half):
        part = back[:, i * share : (i + 1) * share]
        other = i ^ me[0]
        place = other >> 1

        @pl.when((other & 1) == 0)
        def _(part=part, place=place):
            kept[place] = part

        @pl.when((other & 1) == 1)
        def _(part=part, place=place):
            given[place] = part

    weighed = back.astype(jnp.float32) * inputs[0].astype(jnp.float32)
    by_lane = jnp.broadcast_to(jnp.sum(weighed, axis=1, keepdims=True), (channels, 128))
    row = lax.broadcasted_iota(jnp.int32, by_lane.shape, 0)
    lane = lax.broadcasted_iota(jnp.int32, by_lane.shape, 1)
    total = jnp.sum(jnp.where(row == lane, by_lane, 0.0), axis=0, keepdims=True)
    width = scales.shape[1]
    turned = jnp.broadcast_to(scales[...], (8, width))
    turned = pltpu.roll(turned, lax.rem(width - me[0] * channels, width), 1)
    gain[...] = jnp.broadcast_to(total, gain.shape) / turned[:, :128]


def toeplitz_scratch(length, count, slabs):
    width = slab_width(length)
    return [
        pltpu.VMEM((count, width), jnp.float32),
        pltpu.VMEM((slabs, TILE, width), jnp.bfloat16),
        pltpu.VMEM((len(tile_pairs(length)), TILE, TILE), jnp.bfloat16),
    ]


def maps_scratch(channels, length, count, slabs):
    return [
        *toeplitz_scratch(length, count, slabs),
        pltpu.VMEM((2 * channels, length), jnp.bfloat16),
    ]


def spectral_maps(pieces, filters, channels, start, count, into=None):
    length = filters.shape[1]
    given = [] if into is None else [into]
    return pl.pallas_call(
        functools.partial(maps_kernel, start),
        in_specs=[in_vmem(), in_vmem(), *[in_vmem() for _ in given]],
        out_specs=[in_vmem()] * 2,
        out_shape=[
            pltpu.VMEM((2, K, channels, length), jnp.bfloat16),
            pltpu.VMEM((AR, channels, length), jnp.bfloat16),
        ],
        scratch_shapes=maps_scratch(channels, length, filters.shape[0], count),
        input_output_aliases={2: 0} if given else {},
        compiler_params=vmem(20),
        cost_estimate=pl.CostEstimate(
            flops=6 * channels * count * length * length, transcendentals=0, bytes_accessed=4 << 20
        ),
        name="spectral_maps",
    )(filters, pieces, *given)


def spectral_mixed(me, pieces, filters, mixing):
    owners, _, share = pieces.shape
    channels, model_width = mixing.shape[1:]
    count, length = filters.shape
    cut = (owners // 4, 2, model_width // 2, share)
    return pl.pallas_call(
        mixed_kernel,
        grid_spec=pltpu.PrefetchScalarGridSpec(
            num_scalar_prefetch=1,
            grid=(count // PER_STEP,),
            in_specs=[
                whole(filters.shape),
                in_vmem(),
                pl.BlockSpec(memory_space=pltpu.HBM),
            ],
            out_specs=[in_vmem()] * 6,
            scratch_shapes=[
                *maps_scratch(channels, length, count, PER_STEP),
                pltpu.VMEM((owners, model_width, share), jnp.float32),
                pltpu.VMEM(mixing.shape, jnp.bfloat16),
                pltpu.SemaphoreType.DMA,
            ],
        ),
        out_shape=[
            pltpu.VMEM((2, count, channels, length), jnp.bfloat16),
            pltpu.VMEM((AR, channels, length), jnp.bfloat16),
            *[pltpu.VMEM(cut, jnp.bfloat16)] * 4,
        ],
        compiler_params=vmem(20),
        cost_estimate=pl.CostEstimate(
            flops=10 * channels * count * length * length, transcendentals=0, bytes_accessed=4 << 20
        ),
        name="spectral_mixed",
    )(me, in_hbm(filters), pieces, in_hbm(mixing))


def spectral_back(grads, mixing, filters, pieces):
    channels = mixing.shape[1]
    count, length = filters.shape
    return pl.pallas_call(
        spectral_back_kernel,
        grid=(count // PER_STEP,),
        in_specs=[in_vmem()] * 4,
        out_specs=in_vmem(),
        scratch_shapes=[
            *toeplitz_scratch(length, count, PER_STEP),
            pltpu.VMEM((PER_STEP, 2 * channels, length), jnp.bfloat16),
        ],
        out_shape=pltpu.VMEM((2 * channels, length), jnp.float32),
        compiler_params=vmem(20),
        name="spectral_back",
    )(filters, mixing, pieces, grads)


def lag_back(me, acc, mixing, grads, lags, pieces, gain):
    channels = mixing.shape[1]
    owners, _, share = pieces.shape
    sent = pltpu.VMEM((owners // 2, channels, share), jnp.bfloat16)
    return pl.pallas_call(
        lag_back_kernel,
        grid_spec=pltpu.PrefetchScalarGridSpec(
            num_scalar_prefetch=1,
            grid=(1,),
            in_specs=[in_vmem()] * 6,
            out_specs=[in_vmem()] * 3,
        ),
        out_shape=[sent, sent, pltpu.VMEM((8, 128), jnp.float32)],
        compiler_params=vmem(12),
        name="lag_back",
    )(me, acc, mixing, grads, lags, pieces, gain[None, :])


def gelu_parts(gate_value, upper_value, hidden_grad):
    slope = math.sqrt(2 / math.pi)
    square = gate_value * gate_value
    tanh = jnp.tanh(slope * gate_value * (1.0 + 0.044715 * square))
    rise = 0.5 * (1.0 + tanh)
    gelu = gate_value * rise
    bend = 0.5 * slope * (1.0 - tanh * tanh) * (1.0 + 3 * 0.044715 * square)
    return (
        gelu * upper_value,
        hidden_grad * upper_value * (rise + gate_value * bend),
        hidden_grad * gelu,
    )


def feed_forward_kernel(
    bit,
    held,
    got,
    hidden_in,
    gain,
    cotangent,
    gate,
    up,
    down,
    output,
    normed_out,
    grad,
    grad_low,
    normed,
    resid,
    acc,
    normed_grad,
):
    step = pl.program_id(0)
    share = resid.shape[0]

    @pl.when(step == 0)
    def _():
        mixed = held[bit[0]].astype(jnp.float32) + got[...].astype(jnp.float32)
        resid[...] = hidden_in[0].astype(jnp.float32) + mixed.T
        normed[...] = rms_scale(resid[...], gain[...]).astype(jnp.bfloat16)
        acc[...] = jnp.zeros_like(acc)
        normed_grad[...] = jnp.zeros_like(normed_grad)

    gate_value = product(normed[...], gate[...])
    upper_value = product(normed[...], up[...])
    hidden_grad = contract_last(cotangent[0], down[...])
    hidden, gate_back, upper_back = gelu_parts(gate_value, upper_value, hidden_grad)
    acc[...] += product(hidden.astype(jnp.bfloat16), down[...])
    normed_grad[...] += contract_last(gate_back.astype(jnp.bfloat16), gate[...]) + contract_last(
        upper_back.astype(jnp.bfloat16), up[...]
    )

    @pl.when(step == pl.num_programs(0) - 1)
    def _():
        value, back = resid[...], normed_grad[...]
        output[0] = (value + acc[...]).astype(jnp.bfloat16)
        scale = lax.rsqrt(jnp.mean(value * value, axis=-1, keepdims=True) + eps_norm)
        weighed = back * gain[...]
        along = jnp.mean(weighed * value, axis=-1, keepdims=True)
        total = cotangent[0].astype(jnp.float32) + scale * (
            weighed - value * (scale * scale * along)
        )
        grad[...] = total
        grad_low[...] = total.astype(jnp.bfloat16)
        gains = jnp.sum(back * value * scale, axis=0, keepdims=True)
        high = jnp.broadcast_to(gains, (16, gains.shape[1])).astype(jnp.bfloat16)
        low = (gains - high.astype(jnp.float32)).astype(jnp.bfloat16)
        row = lax.broadcasted_iota(jnp.int32, low.shape, 0)
        normed_out[:share, :] = normed[...]
        normed_out[share:, :] = jnp.where(row < 8, high, low)


def feed_forward(bit, held, got, hidden_in, gain, cotangent, w_gate, w_up, w_down):
    _, share, width = hidden_in.shape
    steps = 4
    units = w_gate.shape[1] // steps
    tokens = (share, width)
    return pl.pallas_call(
        feed_forward_kernel,
        grid_spec=pltpu.PrefetchScalarGridSpec(
            num_scalar_prefetch=1,
            grid=(steps,),
            in_specs=[
                whole(held.shape),
                whole(got.shape),
                whole(hidden_in.shape),
                whole((1, width)),
                whole(cotangent.shape),
                pl.BlockSpec((width, units), lambda k, _: (0, k)),
                pl.BlockSpec((width, units), lambda k, _: (0, k)),
                pl.BlockSpec((units, width), lambda k, _: (k, 0)),
            ],
            out_specs=[
                whole(hidden_in.shape),
                whole((share + 16, width)),
                whole(tokens),
                whole(tokens),
            ],
            scratch_shapes=[
                pltpu.VMEM(tokens, jnp.bfloat16),
                *[pltpu.VMEM(tokens, jnp.float32)] * 3,
            ],
        ),
        out_shape=[
            jax.ShapeDtypeStruct(hidden_in.shape, jnp.bfloat16),
            jax.ShapeDtypeStruct((share + 16, width), jnp.bfloat16),
            jax.ShapeDtypeStruct(tokens, jnp.float32),
            jax.ShapeDtypeStruct(tokens, jnp.bfloat16),
        ],
        compiler_params=vmem(16),
        name="feed_forward",
    )(bit, held, got, hidden_in, gain[None, :], cotangent, w_gate, w_up, w_down)


CHUNK = 6


def own_mixing_grad_kernel(maps, lags, grads, out, lag_out):
    def chunk(index, _):
        own = pl.ds(index * CHUNK, CHUNK)
        for which in range(2):
            values = maps[which, own]
            total = product(values.reshape(-1, values.shape[-1]), grads[...])
            out[which, own] = total.astype(out.dtype).reshape(CHUNK, *out.shape[2:])

    lax.fori_loop(0, maps.shape[1] // CHUNK, chunk, None)
    values = lags[...].reshape(-1, lags.shape[-1])
    lag_out[...] = product(values, grads[...]).astype(out.dtype).reshape(lag_out.shape)


def own_mixing_grad(maps, lags, grads):
    _, count, channels, _ = maps.shape
    width = grads.shape[1]
    return pl.pallas_call(
        own_mixing_grad_kernel,
        in_specs=[in_vmem()] * 3,
        out_specs=[in_vmem()] * 2,
        out_shape=[
            pltpu.VMEM((2, count, channels, width), jnp.bfloat16),
            pltpu.VMEM((AR, channels, width), jnp.bfloat16),
        ],
        compiler_params=vmem(16),
        name="own_mixing_grad",
    )(maps, lags, grads)


def mixing_grad_kernel(which, maps, lags, grads, own, own_lags, out):
    def total(values, mine):
        values = product(values.reshape(-1, values.shape[-1]), grads[...])
        return (values + mine.reshape(values.shape).astype(jnp.float32)).astype(out.dtype)

    count, channels = maps.shape[1:3]

    def chunk(index, _):
        part = pl.ds(index * CHUNK, CHUNK)
        start = pl.multiple_of(index * CHUNK * channels, CHUNK * channels)
        out[pl.ds(start, CHUNK * channels), :] = total(maps[which, part], own[which, part])

    lax.fori_loop(0, count // CHUNK, chunk, None)
    if which:
        out[count * channels :, :] = total(lags[...], own_lags[...])


def mixing_grad(which, maps, lags, grads, own, own_lags):
    _, count, channels, _ = maps.shape
    shape = ((count + which * AR) * channels, grads.shape[1])
    return pl.pallas_call(
        functools.partial(mixing_grad_kernel, which),
        in_specs=[in_vmem()] * 5,
        out_specs=in_vmem(),
        out_shape=pltpu.VMEM(shape, jnp.bfloat16),
        compiler_params=vmem(16),
        name="mixing_grad",
    )(maps, lags, grads, own, own_lags)


def finish_mixing_kernel(part, got, *refs):
    out = refs[-1]
    out[...] = (part[...].astype(jnp.float32) + got[...].astype(jnp.float32)).reshape(out.shape)


def finish_mixing(part, got, first, total, into=None):
    channels = total[1]
    count = part.shape[0] // channels
    steps = 3
    size = count // steps
    given = [] if into is None else [into]
    return pl.pallas_call(
        finish_mixing_kernel,
        grid=(steps,),
        in_specs=[
            pl.BlockSpec((size * channels, total[2]), lambda k: (k, 0)),
            pl.BlockSpec((size * channels, total[2]), lambda k: (k, 0)),
            *[pl.BlockSpec(memory_space=pl.ANY) for _ in given],
        ],
        out_specs=pl.BlockSpec(
            tuple(map(pl.Element, (size, *total[1:]))), lambda k: (first + k * size, 0, 0)
        ),
        out_shape=jax.ShapeDtypeStruct(total, jnp.float32),
        input_output_aliases={2: 0} if given else {},
        compiler_params=vmem(16),
        name="finish_mixing",
    )(part, got, *given)


def unit_rows(width, units):
    blocks = width // units // 2
    return [width + units * i for i in range(blocks)], width + units * blocks + 16


def unit_grads_kernel(channels, me, *refs):
    *parts, gate, up, down, first_gain, out, normed, cotangent = refs
    place_tokens(me[0], parts[:4], normed)
    place_tokens(me[0], parts[4:], cotangent)
    width, units = gate.shape
    hidden_grad = contract_last(cotangent[...], down[...])
    gate_value = product(normed[...], gate[...])
    upper_value = product(normed[...], up[...])
    hidden, gate_back, upper_back = gelu_parts(gate_value, upper_value, hidden_grad)
    gate_part = contract_first(normed[...], gate_back.astype(jnp.bfloat16))
    up_part = contract_first(normed[...], upper_back.astype(jnp.bfloat16))
    down_part = contract_first(hidden.astype(jnp.bfloat16), cotangent[...]).astype(jnp.bfloat16)
    starts, size = unit_rows(width, units)
    out[0, :width] = gate_part.astype(jnp.bfloat16)
    out[1, :width] = up_part.astype(jnp.bfloat16)
    for i in range(2 * len(starts)):
        half, start = i // len(starts), starts[i % len(starts)]
        out[half, start : start + units] = down_part[:, i * units : (i + 1) * units]
    share_rows = parts[0].shape[2]
    second = jnp.zeros((16, width), jnp.float32)
    for part in parts[2:4]:
        for a in range(2):
            for r in range(part.shape[1]):
                second = second + part[a, r, share_rows:, :].astype(jnp.float32)
    second = second[:8] + second[8:]
    second = pltpu.roll(second, lax.rem(width - me[0] * channels, width), 1)
    out[0, size - 16 :] = jnp.zeros((16, units), jnp.bfloat16)
    out[1, size - 16 :] = jnp.zeros((16, units), jnp.bfloat16)
    lanes = first_gain.shape[1]
    gains = jnp.concatenate([second[:, :lanes], first_gain[...]], axis=0)
    out[0, size - 16 :, :lanes] = gains.astype(jnp.bfloat16)


def unit_grads(me, normed_parts, cotangent_parts, w_gate, w_up, w_down, first_gain):
    width, hidden = w_gate.shape
    chans = lax.axis_size("chan")
    units = hidden // chans
    parts = [*normed_parts, *cotangent_parts]
    tokens = 2 * sum(math.prod(part.shape[:-1]) for part in normed_parts[:2])
    shape = (2, unit_rows(width, units)[1], units)
    return pl.pallas_call(
        functools.partial(unit_grads_kernel, width // chans),
        grid_spec=pltpu.PrefetchScalarGridSpec(
            num_scalar_prefetch=1,
            grid=(1,),
            in_specs=[
                *[in_vmem() for _ in parts],
                pl.BlockSpec((width, units), lambda k, me: (0, me[0])),
                pl.BlockSpec((width, units), lambda k, me: (0, me[0])),
                pl.BlockSpec((units, width), lambda k, me: (me[0], 0)),
                in_vmem(),
            ],
            out_specs=in_vmem(),
            scratch_shapes=[pltpu.VMEM((tokens, width), jnp.bfloat16)] * 2,
        ),
        out_shape=pltpu.VMEM(shape, jnp.bfloat16),
        compiler_params=vmem(24),
        name="unit_grads",
    )(me, *parts, in_hbm(w_gate), in_hbm(w_up), in_hbm(w_down), first_gain)


def finish_units_kernel(core, mine, other, gate, up, down, gains):
    width, units = gate.shape
    starts, size = unit_rows(width, units)
    for which, (low, high) in enumerate(((mine, other), (other, mine))):

        @pl.when(core[0] == which)
        def _(low=low, high=high):
            gate[...] = low[:width].astype(jnp.float32)
            up[...] = high[:width].astype(jnp.float32)
            for i in range(2 * len(starts)):
                source, start = (low, high)[i // len(starts)], starts[i % len(starts)]
                part = source[start : start + units].astype(jnp.float32)
                down[:, i * units : (i + 1) * units] = part
            gains[...] = low[size - 16 :].astype(jnp.float32)


def finish_units(core, mine, other, width):
    units = mine.shape[1]
    shapes = [(width, units), (width, units), (units, width), (16, units)]
    return pl.pallas_call(
        finish_units_kernel,
        grid_spec=pltpu.PrefetchScalarGridSpec(
            num_scalar_prefetch=1,
            grid=(1,),
            in_specs=[in_vmem()] * 2,
            out_specs=[whole(shape) for shape in shapes],
        ),
        out_shape=[jax.ShapeDtypeStruct(shape, jnp.float32) for shape in shapes],
        compiler_params=vmem(16),
        name="finish_units",
    )(core, mine, other)


def swap(values, axis, mask):
    count = lax.axis_size(axis)
    return lax.ppermute(values, axis, [(i, i ^ mask) for i in range(count)])


def bits_of(axis):
    return [1 << b for b in range(lax.axis_size(axis).bit_length() - 1)]


def entry(values, index, dim):
    return lax.dynamic_slice_in_dim(values, index, 1, dim, allow_negative_indices=False)


def join(mine, other, high, dim):
    return jnp.where(
        high, jnp.concatenate([other, mine], dim), jnp.concatenate([mine, other], dim)
    )


def tie(*values):
    return lax.optimization_barrier(values)


def gather_round(held, mask, bits, came=None):
    came = swap(held, "chan", mask) if came is None else came
    return join(held[None], came[None], bits[mask][2], 0)


class Gather:
    def __init__(self, values, half, bits):
        masks = bits_of("chan")
        self.half, self.bits = half, bits
        self.shape = values.shape
        self.common = masks[2:]
        self.orders = [(masks[1], masks[0]), (masks[0], masks[1])]
        self.held = values[None]

    def first(self, came=None):
        for mask in self.common:
            self.held = gather_round(self.held, mask, self.bits, came).reshape(-1, *self.shape)
            came = None
        return self.held

    def second(self):
        self.halves = [self.held[:, : self.half], self.held[:, self.half :]]
        self.halves = [
            gather_round(h, order[0], self.bits)
            for h, order in zip(self.halves, self.orders, strict=True)
        ]
        return self.halves

    def third(self):
        self.others = [
            swap(h, "chan", order[1]) for h, order in zip(self.halves, self.orders, strict=True)
        ]
        return self.others

    def parts(self):
        return (self.halves[0], self.others[0], self.halves[1], self.others[1])


def add(left, right):
    return left.astype(jnp.float32) + right.astype(jnp.float32)


def own_entry(values, mask, dim, bits):
    return add(*exchange(values, mask, dim, bits)).squeeze(dim)


def exchange_rest(kept, came):
    count = 2 * kept.shape[0]
    held = jnp.stack([kept, came], axis=1).reshape(count, *kept.shape[1:])
    for mask in bits_of("chan")[1:]:
        split = held.reshape(-1, 2, mask, *held.shape[1:])
        kept, came = split[:, 0], swap(split[:, 1], "chan", mask)
        held = jnp.stack([kept, came], axis=1).reshape(held.shape)
    return kept.reshape(count // 2, *held.shape[1:]), came.reshape(count // 2, *held.shape[1:])


def exchange(values, mask, dim, bits):
    keep, give = (entry(values, bit, dim) for bit in bits[mask][:2])
    return keep, swap(give, "chan", mask)


def scatter_tokens(keep0, give0, keep1, give1, bits, beside):
    masks = bits_of("chan")
    got0, got1 = swap(give0, "chan", masks[0]), swap(give1, "chan", masks[1])
    half0 = add(keep0, got0).astype(jnp.bfloat16)
    half1 = add(keep1, got1).astype(jnp.bfloat16)
    half0, half1 = beside(half0, half1)
    half0 = own_entry(half0, masks[1], 1, bits)
    half1 = own_entry(half1, masks[0], 1, bits)
    held = jnp.concatenate([half0, half1], axis=1)
    for mask in masks[:2:-1]:
        held = held.astype(jnp.bfloat16).reshape(2, -1, *held.shape[1:])
        held = own_entry(held, mask, 0, bits)
    return held.astype(jnp.bfloat16)


def shards(
    hidden_in, segments, filters, gain_one, mixing, gain_two, w_gate, w_up, w_down, out_grad
):
    chans = lax.axis_size("chan")
    me = lax.axis_index("chan").astype(jnp.int32)
    at = me.reshape(1)
    _, share, width = hidden_in.shape
    channels = width // chans
    core = lax.axis_index("rows").astype(jnp.int32) & 1
    other_core = 1 - core
    bits = [(me >> b) & 1 for b in range(len(bits_of("chan")))]
    bits = [value for bit in bits for value in (bit, bit ^ 1, bit != 0)]
    hidden_in, at, core, other_core, *bits = tie(hidden_in, at, core, other_core, *bits)
    bits = {mask: bits[3 * i : 3 * i + 3] for i, mask in enumerate(bits_of("chan"))}
    pieces = lax.all_to_all(
        first_norm(at, hidden_in, gain_one, segments, chans),
        "chan",
        split_axis=0,
        concat_axis=0,
    )
    pieces, cotangent = tie(pieces, out_grad)
    cotangent_gather = Gather(cotangent[0], share // 2, bits)
    came = swap(cotangent_gather.held, "chan", 4)
    maps, lags, *cut = spectral_mixed(at, pieces, filters, mixing)
    pieces, lags, came = tie(pieces, lags, came)
    cotangent_gather.first(came)
    peer_pieces = swap(pieces, "rows", 2)

    def beside(*values):
        *values, cotangent_gather.held = tie(*values, cotangent_gather.held)
        cotangent_gather.second()
        return values

    held = scatter_tokens(*cut, bits, beside)
    held, peer_pieces, *cotangent_gather.halves = tie(
        held, peer_pieces, *cotangent_gather.halves
    )
    got = exchange(held, 4, 0, bits)[1][0]
    peer_maps, peer_lags = spectral_maps(peer_pieces, filters, channels, 0, K // 2)
    held, got, peer_maps = tie(held, got, peer_maps)
    cotangent_gather.third()
    output, normed_two, resid_grad, resid_low = feed_forward(
        bits[4][0].reshape(1), held, got, hidden_in, gain_two, out_grad, w_gate, w_up, w_down
    )
    grad_gather = Gather(resid_low, share // 2, bits)
    first, *cotangent_gather.others = tie(grad_gather.first(), *cotangent_gather.others)
    peer_pieces, resid_grad = tie(peer_pieces, resid_grad)
    peer_maps, _ = spectral_maps(peer_pieces, filters, channels, K // 2, K // 2, peer_maps)
    grad_gather.held, peer_maps = tie(first, peer_maps)
    grad_gather.second()
    normed_two, *grad_gather.halves = tie(normed_two, *grad_gather.halves)
    grad_gather.third()
    normed_gather = Gather(normed_two, share // 2, bits)
    normed_gather.first()
    full_grad = place(at, grad_gather.parts())
    peer_grad = swap(full_grad, "rows", 2)
    normed_gather.second()
    acc = spectral_back(full_grad, mixing, filters, pieces)
    acc, *normed_gather.halves = tie(acc, *normed_gather.halves)
    normed_gather.third()
    back, give, first_local = lag_back(at, acc, mixing, full_grad, lags, pieces, gain_one)
    came = swap(give, "chan", 1)
    first_local, full_grad = tie(first_local, full_grad)
    own, own_lags = own_mixing_grad(maps, lags, full_grad)
    own_lags, back, came, *normed_parts = tie(own_lags, back, came, *normed_gather.parts())
    unit_parts = unit_grads(
        at, normed_parts, cotangent_gather.parts(), w_gate, w_up, w_down, first_local
    )
    back, came = exchange_rest(back, came)
    unit_given = swap(entry(unit_parts, other_core, 0)[0], "rows", 1)
    unit_half = add(entry(unit_parts, core, 0)[0], unit_given).astype(jnp.bfloat16)
    unit_half, peer_grad = tie(unit_half, peer_grad)
    unit_other = swap(unit_half, "rows", 2)
    first_part = mixing_grad(0, peer_maps, peer_lags, peer_grad, own, own_lags)
    first_part, peer_grad = tie(first_part, peer_grad)
    second_part = mixing_grad(1, peer_maps, peer_lags, peer_grad, own, own_lags)
    second_part, came, unit_other = tie(second_part, came, unit_other)
    input_total = first_norm_back(at, back, came, hidden_in, gain_one, resid_grad)
    unit_half = add(unit_half, unit_other).astype(jnp.bfloat16)
    for mask in bits_of("rows")[2:]:
        unit_half = add(unit_half, swap(unit_half, "rows", mask)).astype(jnp.bfloat16)
    unit_other = swap(unit_half, "rows", 1)
    mixing_sum = None
    for part, first in ((first_part, 0), (second_part, K)):
        masks = [1, *bits_of("rows")[2:]]
        for mask in masks[:-1]:
            part = add(part, swap(part, "rows", mask)).astype(jnp.bfloat16)
        got = swap(part, "rows", masks[-1])
        mixing_sum = finish_mixing(part, got, first, mixing.shape, mixing_sum)
        if not first:
            mixing_sum, unit_half = tie(mixing_sum, unit_half)
    gate_sum, up_sum, down_sum, gains = finish_units(
        core.reshape(1), unit_half, unit_other, width
    )
    return (
        output,
        input_total,
        mixing_sum,
        gate_sum,
        up_sum,
        down_sum,
        gains[8, :channels],
        gains[0, :channels],
    )


def solution(mesh):
    in_specs = (
        P("rows", "chan", None),
        P("rows", None),
        P(),
        P(),
        P(None, "chan", None),
        P(),
        P(),
        P(),
        P(),
        P("rows", "chan", None),
    )
    out_specs = (
        P("rows", "chan", None),
        P("rows", "chan", None),
        P(None, "chan", None),
        P(None, "chan"),
        P(None, "chan"),
        P("chan", None),
        P("chan"),
        P("chan"),
    )
    return jax.shard_map(shards, mesh=mesh, in_specs=in_specs, out_specs=out_specs, check_vma=False)
```

```python
import functools
import math

import jax
import jax.numpy as jnp
from jax import lax
from jax.experimental import pallas as pl
from jax.experimental.pallas import tpu as pltpu
from jax.sharding import PartitionSpec as P

K = 24
AR = 3
TILE = 256
HALF = 128
PER_STEP = 12
FEED_STEPS = 4

eps_norm = 1e-05


def rms_scale(values, scales):
    return values * lax.rsqrt(jnp.mean(values * values, axis=-1, keepdims=True) + eps_norm) * scales


def contract_first(left, right):
    return lax.dot_general(
        left, right, (((0,), (0,)), ((), ())), preferred_element_type=jnp.float32
    )


def contract_last(left, right):
    return lax.dot_general(
        left, right, (((1,), (1,)), ((), ())), preferred_element_type=jnp.float32
    )


def product(left, right):
    return jnp.dot(left, right, preferred_element_type=jnp.float32)


def in_hbm(value):
    return pltpu.with_memory_space_constraint(value, pltpu.HBM)


def in_vmem():
    return pl.BlockSpec(memory_space=pltpu.VMEM)


def whole(shape):
    return pl.BlockSpec(shape, lambda *_: (0,) * len(shape))


def vmem(mebibytes):
    return pltpu.CompilerParams(vmem_limit_bytes=mebibytes << 20)


def first_norm_kernel(me, hidden, gain, segments, pieces):
    count, rows, share = pieces.shape
    channels = hidden.shape[2] // count
    normed = rms_scale(hidden[0].astype(jnp.float32), gain[...])
    normed = normed.T.astype(jnp.bfloat16)
    ids = segments[:, pl.ds(pl.multiple_of(me[0] * share, share), share)]
    ids = jnp.broadcast_to(ids.astype(jnp.float32), (rows - channels, share)).astype(jnp.bfloat16)
    for i in range(count):
        pieces[i, :channels, :] = normed[i * channels : (i + 1) * channels]
        pieces[i, channels:, :] = ids


def first_norm(me, hidden_in, gain, segments, count):
    _, share, width = hidden_in.shape
    shape = (count, width // count + 16, share)
    return pl.pallas_call(
        first_norm_kernel,
        grid_spec=pltpu.PrefetchScalarGridSpec(
            num_scalar_prefetch=1,
            grid=(1,),
            in_specs=[whole(hidden_in.shape), whole((1, width)), whole(segments.shape)],
            out_specs=whole(shape),
        ),
        out_shape=jax.ShapeDtypeStruct(shape, jnp.bfloat16),
        compiler_params=vmem(8),
        name="first_norm",
    )(me, in_hbm(hidden_in), in_hbm(gain[None, :]), in_hbm(segments))


def first_norm_back_kernel(me, kept, came, hidden, gain, grad, out):
    half, channels, share = kept.shape
    parts = []
    for i in range(2 * half):
        other = i ^ me[0]
        pick = jnp.where(other < half, kept[other % half], came[other % half])
        parts.append(pick.astype(jnp.float32))
    normed_grad = jnp.concatenate(parts, axis=0).T
    tokens = hidden[0].astype(jnp.float32)
    scale = lax.rsqrt(jnp.mean(tokens * tokens, axis=-1, keepdims=True) + eps_norm)
    weighed = normed_grad * gain[...]
    along = jnp.mean(weighed * tokens, axis=-1, keepdims=True)
    out[0] = grad[...] + scale * (weighed - tokens * (scale * scale * along))


def first_norm_back(me, kept, came, hidden_in, gain, grad):
    _, share, width = hidden_in.shape
    return pl.pallas_call(
        first_norm_back_kernel,
        grid_spec=pltpu.PrefetchScalarGridSpec(
            num_scalar_prefetch=1,
            grid=(1,),
            in_specs=[in_vmem()] * 5,
            out_specs=whole(hidden_in.shape),
        ),
        out_shape=jax.ShapeDtypeStruct(hidden_in.shape, jnp.float32),
        compiler_params=vmem(8),
        name="first_norm_back",
    )(me, kept, came, hidden_in, gain[None, :], grad)


def tile_pairs(length):
    blocks, reach = length // TILE, length // 2 // TILE
    return [(tb, sb) for tb in range(blocks) for sb in range(max(0, tb - reach), tb + 1)]


def slab_width(length):
    return length // 2 + TILE


def parity_lanes(rows, lanes, dtype=jnp.float32):
    lane = lax.broadcasted_iota(jnp.int32, (rows, lanes), 1)
    return (1 - 2 * (lane % 2)).astype(dtype)


def block(index):
    return slice(index * TILE, (index + 1) * TILE)


def segment_row(pieces):
    row = pieces.shape[1] - 8
    return jnp.concatenate(
        [pieces[i, row:, :].astype(jnp.float32) for i in range(pieces.shape[0])], axis=1
    )


def build_masks(ids, masks, length, targets_in_rows):
    row = lax.broadcasted_iota(jnp.int32, (TILE, TILE), 0)
    col = lax.broadcasted_iota(jnp.int32, (TILE, TILE), 1)
    in_lanes = [jnp.broadcast_to(ids[:1, block(b)], (TILE, TILE)) for b in range(length // TILE)]
    in_rows = [value.T for value in in_lanes]
    for index, (tb, sb) in enumerate(tile_pairs(length)):
        rows_of, lanes_of = (tb, sb) if targets_in_rows else (sb, tb)
        same = in_rows[rows_of] == in_lanes[lanes_of]
        if tb == sb:
            same = same & ((row >= col) if targets_in_rows else (col >= row))
        masks[index] = jnp.where(same, 1.0, 0.0).astype(jnp.bfloat16)


def lag_keep(ids, lag):
    lane = lax.broadcasted_iota(jnp.int32, ids.shape, 1)
    same = (pltpu.roll(ids, lag, 1) == ids) & (lane >= lag)
    return jnp.where(same, 1.0, 0.0)[:1]


def build_slab(taps, slab, width):
    rolled = pltpu.roll(jnp.broadcast_to(taps, (HALF, width)), 0, 1, stride=1, stride_axis=0)
    rolled = rolled.astype(jnp.bfloat16)
    slab[:HALF, :] = rolled
    slab[HALF:, HALF:] = rolled[:, : width - HALF]
    slab[HALF:, :HALF] = rolled[:, :HALF]


def start_maps(filters, pieces, lags, taps, masks, doubled):
    count, _, share = pieces.shape
    channels, length = lags.shape[1:]
    ids = segment_row(pieces)
    build_masks(ids, masks, length, False)
    taps[...] = filters[:, : taps.shape[1]].astype(jnp.float32)
    sign = parity_lanes(channels, share, jnp.bfloat16)
    for i in range(count):
        part = pieces[i, :channels, :]
        doubled[:channels, i * share : (i + 1) * share] = part
        doubled[channels:, i * share : (i + 1) * share] = part * sign
    inputs = doubled[:channels, :]
    lags[0] = inputs
    inputs = inputs.astype(jnp.float32)
    for j in range(1, AR):
        lags[j] = (pltpu.roll(inputs, j, 1) * lag_keep(ids, j)).astype(jnp.bfloat16)


def step_maps(first, place, maps, taps, slabs, masks, doubled):
    channels, length = maps.shape[2:]
    width = taps.shape[1]
    pairs = tile_pairs(length)
    parity = parity_lanes(channels, TILE)
    for k in range(slabs.shape[0]):
        slab = slabs.at[k]
        build_slab(taps[pl.ds(first + k, 1), :], slab, width)
        for tb in range(length // TILE):
            chosen = [(i, sb) for i, (t, sb) in enumerate(pairs) if t == tb]
            tiles = [slab[:, block(tb - sb)] * masks[i] for i, sb in chosen]
            low = chosen[0][1]
            both = product(
                doubled[:, low * TILE : (tb + 1) * TILE], jnp.concatenate(tiles, axis=0)
            )
            maps[0, place + k, :, block(tb)] = both[:channels].astype(jnp.bfloat16)
            maps[1, place + k, :, block(tb)] = (both[channels:] * parity).astype(jnp.bfloat16)


def maps_kernel(start, filters, pieces, maps, lags, taps, slabs, masks, doubled):
    start_maps(filters, pieces, lags, taps, masks, doubled)
    step_maps(start, 0, maps, taps, slabs, masks, doubled)


def mixed_kernel(
    me,
    filters,
    pieces,
    mixing_given,
    maps,
    lags,
    keep0,
    give0,
    keep1,
    give1,
    taps,
    slabs,
    masks,
    doubled,
    acc,
    mixing,
    arrived,
):
    _, _, model_width = mixing.shape
    count, _, share = pieces.shape
    filter_count, length = maps.shape[1], lags.shape[2]
    step = pl.program_id(0)

    copy = pltpu.make_async_copy(mixing_given, mixing, arrived)

    @pl.when(step == 0)
    def _():
        copy.start()
        start_maps(filters, pieces, lags, taps, masks, doubled)
        acc[...] = jnp.zeros_like(acc)

    step_maps(step * PER_STEP, step * PER_STEP, maps, taps, slabs, masks, doubled)

    @pl.when(step == 0)
    def _():
        copy.wait()

    def part(weights, values):
        return contract_first(weights.reshape(-1, model_width), values.reshape(-1, length))

    plus = pl.ds(step * PER_STEP, PER_STEP)
    minus = pl.ds(filter_count + step * PER_STEP, PER_STEP)
    total = part(mixing[plus], maps[0, plus]) + part(mixing[minus], maps[1, plus])
    for i in range(count):
        acc[i] += total[:, i * share : (i + 1) * share]

    @pl.when(step == pl.num_programs(0) - 1)
    def _():
        last = part(mixing[2 * filter_count :], lags[...])
        for i in range(count):
            acc[i] += last[:, i * share : (i + 1) * share]
        half = model_width // 2
        low, near = me[0] & 1, (me[0] >> 1) & 1
        for r in range(count // 4):
            for a in range(2):
                for other, (out0, out1) in enumerate(((keep0, keep1), (give0, give1))):
                    out0[r, a] = acc[r * 4 + a * 2 + (low ^ other), :half].astype(jnp.bfloat16)
                    out1[r, a] = acc[r * 4 + (near ^ other) * 2 + a, half:].astype(jnp.bfloat16)


def place_tokens(me, parts, out):
    low, near = me & 1, (me >> 1) & 1
    halves = len(parts) // 2
    rest = parts[0].shape[1]
    rows = out.shape[0] // (4 * rest * halves)
    for index, part in enumerate(parts):
        half, other = index // 2, index % 2
        for a in range(2):
            for r in range(rest):
                if half == 0:
                    owner = r * 4 + a * 2 + (low ^ other)
                else:
                    owner = r * 4 + (near ^ other) * 2 + a
                start = pl.multiple_of((owner * halves + half) * rows, rows)
                out[pl.ds(start, rows), :] = part[a, r, :rows, :]


def place_kernel(me, *refs):
    place_tokens(me[0], refs[:-1], refs[-1])


def place(me, parts):
    count = sum(math.prod(part.shape[:-1]) for part in parts)
    shape = (count, parts[0].shape[-1])
    return pl.pallas_call(
        place_kernel,
        grid_spec=pltpu.PrefetchScalarGridSpec(
            num_scalar_prefetch=1,
            grid=(1,),
            in_specs=[in_vmem()] * 4,
            out_specs=in_vmem(),
        ),
        out_shape=pltpu.VMEM(shape, jnp.bfloat16),
        compiler_params=vmem(8),
        name="place",
    )(me, *parts)


def spectral_back_kernel(start, filters, mixing, pieces, grads, *refs):
    *before, acc, taps, slabs, masks, both = refs
    _, channels, model_width = mixing.shape
    count = filters.shape[0]
    length, width = acc.shape[1], taps.shape[1]
    reach = length // 2
    pairs = tile_pairs(length)
    some = slabs.shape[0]
    rows = some * channels
    build_masks(segment_row(pieces), masks, length, True)
    source = lax.broadcasted_iota(jnp.int32, (width, width), 0)
    target = lax.broadcasted_iota(jnp.int32, (width, width), 1)
    flip = jnp.where(source + target == reach, 1.0, 0.0).astype(jnp.bfloat16)
    taps[...] = product(filters[:, :width], flip)
    sign = parity_lanes(rows, length, jnp.bfloat16)

    def by_map(first):
        weights = mixing[first : first + some].reshape(rows, model_width)
        return contract_last(weights, grads[...]).astype(jnp.bfloat16)

    both[:, :channels, :] = by_map(start).reshape(some, channels, length)
    both[:, channels:, :] = (by_map(count + start) * sign).reshape(some, channels, length)
    for k in range(some):
        build_slab(taps[start + k : start + k + 1, :], slabs.at[k], width)
    for sb in range(length // TILE):
        chosen = [(i, tb) for i, (tb, s) in enumerate(pairs) if s == sb]
        last = chosen[-1][1]
        total = before[0][:, block(sb)] if before else jnp.zeros((2 * channels, TILE), jnp.float32)
        for k in range(some):
            tiles = []
            for i, tb in chosen:
                place = reach - (tb - sb) * TILE
                tiles.append(slabs[k, :, place : place + TILE] * masks[i])
            total = total + product(
                both[k, :, sb * TILE : (last + 1) * TILE], jnp.concatenate(tiles, axis=0)
            )
        acc[:, block(sb)] = total


def lag_back_kernel(me, acc, mixing, grads, inputs, pieces, scales, kept, given, gain):
    _, channels, model_width = mixing.shape
    length = acc.shape[1]
    half, _, share = kept.shape
    ids = segment_row(pieces)
    lag_grad = contract_last(mixing[2 * K :].reshape(AR * channels, model_width), grads[...])
    total = acc[:channels] + parity_lanes(channels, length) * acc[channels:]
    for j in range(AR):
        term = lag_grad[j * channels : (j + 1) * channels]
        if j:
            term = pltpu.roll(term * lag_keep(ids, j), length - j, 1)
        total = total + term
    back = total.astype(jnp.bfloat16)
    for i in range(2 * half):
        part = back[:, i * share : (i + 1) * share]
        other = i ^ me[0]
        place = other >> 1

        @pl.when((other & 1) == 0)
        def _(part=part, place=place):
            kept[place] = part

        @pl.when((other & 1) == 1)
        def _(part=part, place=place):
            given[place] = part

    weighed = back.astype(jnp.float32) * inputs[0].astype(jnp.float32)
    by_lane = jnp.broadcast_to(jnp.sum(weighed, axis=1, keepdims=True), (channels, 128))
    row = lax.broadcasted_iota(jnp.int32, by_lane.shape, 0)
    lane = lax.broadcasted_iota(jnp.int32, by_lane.shape, 1)
    total = jnp.sum(jnp.where(row == lane, by_lane, 0.0), axis=0, keepdims=True)
    width = scales.shape[1]
    turned = jnp.broadcast_to(scales[...], (8, width))
    turned = pltpu.roll(turned, lax.rem(width - me[0] * channels, width), 1)
    gain[...] = jnp.broadcast_to(total, gain.shape) / turned[:, :128]


def toeplitz_scratch(length, count, slabs):
    width = slab_width(length)
    return [
        pltpu.VMEM((count, width), jnp.float32),
        pltpu.VMEM((slabs, TILE, width), jnp.bfloat16),
        pltpu.VMEM((len(tile_pairs(length)), TILE, TILE), jnp.bfloat16),
    ]


def maps_scratch(channels, length, count, slabs):
    return [
        *toeplitz_scratch(length, count, slabs),
        pltpu.VMEM((2 * channels, length), jnp.bfloat16),
    ]


def spectral_maps(pieces, filters, channels, start, count):
    length = filters.shape[1]
    return pl.pallas_call(
        functools.partial(maps_kernel, start),
        in_specs=[in_vmem()] * 2,
        out_specs=[in_vmem()] * 2,
        out_shape=[
            pltpu.VMEM((2, count, channels, length), jnp.bfloat16),
            pltpu.VMEM((AR, channels, length), jnp.bfloat16),
        ],
        scratch_shapes=maps_scratch(channels, length, filters.shape[0], count),
        compiler_params=vmem(12 + length // 128),
        cost_estimate=pl.CostEstimate(
            flops=6 * channels * count * length * length, transcendentals=0, bytes_accessed=4 << 20
        ),
        name="spectral_maps",
    )(filters, pieces)


def spectral_mixed(me, pieces, filters, mixing):
    owners, _, share = pieces.shape
    channels, model_width = mixing.shape[1:]
    count, length = filters.shape
    cut = (owners // 4, 2, model_width // 2, share)
    return pl.pallas_call(
        mixed_kernel,
        grid_spec=pltpu.PrefetchScalarGridSpec(
            num_scalar_prefetch=1,
            grid=(count // PER_STEP,),
            in_specs=[
                whole(filters.shape),
                in_vmem(),
                pl.BlockSpec(memory_space=pltpu.HBM),
            ],
            out_specs=[in_vmem()] * 6,
            scratch_shapes=[
                *maps_scratch(channels, length, count, PER_STEP),
                pltpu.VMEM((owners, model_width, share), jnp.float32),
                pltpu.VMEM(mixing.shape, jnp.bfloat16),
                pltpu.SemaphoreType.DMA,
            ],
        ),
        out_shape=[
            pltpu.VMEM((2, count, channels, length), jnp.bfloat16),
            pltpu.VMEM((AR, channels, length), jnp.bfloat16),
            *[pltpu.VMEM(cut, jnp.bfloat16)] * 4,
        ],
        compiler_params=vmem(12 + length // 128),
        name="spectral_mixed",
    )(me, in_hbm(filters), pieces, in_hbm(mixing))


def spectral_back(grads, mixing, filters, pieces, start, some, *before):
    channels = mixing.shape[1]
    count, length = filters.shape
    return pl.pallas_call(
        functools.partial(spectral_back_kernel, start),
        in_specs=[in_vmem() for _ in range(4 + len(before))],
        out_specs=in_vmem(),
        scratch_shapes=[
            *toeplitz_scratch(length, count, some),
            pltpu.VMEM((some, 2 * channels, length), jnp.bfloat16),
        ],
        out_shape=pltpu.VMEM((2 * channels, length), jnp.float32),
        compiler_params=vmem(12 + length // 128),
        name="spectral_back",
    )(filters, mixing, pieces, grads, *before)


def lag_back(me, acc, mixing, grads, lags, pieces, gain):
    channels = mixing.shape[1]
    owners, _, share = pieces.shape
    sent = pltpu.VMEM((owners // 2, channels, share), jnp.bfloat16)
    return pl.pallas_call(
        lag_back_kernel,
        grid_spec=pltpu.PrefetchScalarGridSpec(
            num_scalar_prefetch=1,
            grid=(1,),
            in_specs=[in_vmem()] * 6,
            out_specs=[in_vmem()] * 3,
        ),
        out_shape=[sent, sent, pltpu.VMEM((8, 128), jnp.float32)],
        compiler_params=vmem(12),
        name="lag_back",
    )(me, acc, mixing, grads, lags, pieces, gain[None, :])


def gelu_parts(gate_value, upper_value, hidden_grad):
    slope = math.sqrt(2 / math.pi)
    square = gate_value * gate_value
    tanh = jnp.tanh(slope * gate_value * (1.0 + 0.044715 * square))
    rise = 0.5 * (1.0 + tanh)
    gelu = gate_value * rise
    bend = 0.5 * slope * (1.0 - tanh * tanh) * (1.0 + 3 * 0.044715 * square)
    return (
        gelu * upper_value,
        hidden_grad * upper_value * (rise + gate_value * bend),
        hidden_grad * gelu,
    )


def feed_forward_kernel(
    bit, held, got, hidden_in, gain, cotangent, gate, up, down, output, normed_out, grad, grad_low
):
    share, width = grad.shape
    mixed = held[bit[0]].astype(jnp.float32) + got[...].astype(jnp.float32)
    resid = hidden_in[0].astype(jnp.float32) + mixed.T
    scale = lax.rsqrt(jnp.mean(resid * resid, axis=-1, keepdims=True) + eps_norm)
    normed = (resid * scale * gain[...]).astype(jnp.bfloat16)
    value, back = resid, jnp.zeros_like(resid)
    units = gate.shape[1] // FEED_STEPS
    for step in range(FEED_STEPS):
        own = slice(step * units, (step + 1) * units)
        gate_value = product(normed, gate[:, own])
        upper_value = product(normed, up[:, own])
        hidden_grad = contract_last(cotangent[0], down[own, :])
        hidden, gate_back, upper_back = gelu_parts(gate_value, upper_value, hidden_grad)
        value = value + product(hidden.astype(jnp.bfloat16), down[own, :])
        back = back + contract_last(gate_back.astype(jnp.bfloat16), gate[:, own])
        back = back + contract_last(upper_back.astype(jnp.bfloat16), up[:, own])
    output[0] = value.astype(jnp.bfloat16)
    weighed = back * gain[...]
    along = jnp.mean(weighed * resid, axis=-1, keepdims=True)
    total = scale * (weighed - resid * (scale * scale * along))
    total = cotangent[0].astype(jnp.float32) + total
    grad[...] = total
    grad_low[...] = total.astype(jnp.bfloat16)
    gains = jnp.sum(back * resid * scale, axis=0, keepdims=True)
    high = jnp.broadcast_to(gains, (16, width)).astype(jnp.bfloat16)
    low = (gains - high.astype(jnp.float32)).astype(jnp.bfloat16)
    row = lax.broadcasted_iota(jnp.int32, low.shape, 0)
    normed_out[:share, :] = normed
    normed_out[share:, :] = jnp.where(row < 8, high, low)


def feed_forward(bit, held, got, hidden_in, gain, cotangent, w_gate, w_up, w_down):
    _, share, width = hidden_in.shape
    return pl.pallas_call(
        feed_forward_kernel,
        grid_spec=pltpu.PrefetchScalarGridSpec(
            num_scalar_prefetch=1,
            grid=(1,),
            in_specs=[in_vmem()] * 8,
            out_specs=[whole(hidden_in.shape), *[in_vmem()] * 3],
        ),
        out_shape=[
            jax.ShapeDtypeStruct(hidden_in.shape, jnp.bfloat16),
            pltpu.VMEM((share + 16, width), jnp.bfloat16),
            pltpu.VMEM((share, width), jnp.float32),
            pltpu.VMEM((share, width), jnp.bfloat16),
        ],
        compiler_params=vmem(16),
        name="feed_forward",
    )(bit, held, got, hidden_in, gain[None, :], cotangent, w_gate, w_up, w_down)


CHUNK = 6


def own_mixing_grad_kernel(maps, lags, grads, out, lag_out):
    def chunk(index, _):
        own = pl.ds(index * CHUNK, CHUNK)
        for which in range(2):
            values = maps[which, own]
            total = product(values.reshape(-1, values.shape[-1]), grads[...])
            out[which, own] = total.astype(out.dtype).reshape(CHUNK, *out.shape[2:])

    lax.fori_loop(0, maps.shape[1] // CHUNK, chunk, None)
    values = lags[...].reshape(-1, lags.shape[-1])
    lag_out[...] = product(values, grads[...]).astype(out.dtype).reshape(lag_out.shape)


def own_mixing_grad(maps, lags, grads):
    _, count, channels, _ = maps.shape
    width = grads.shape[1]
    return pl.pallas_call(
        own_mixing_grad_kernel,
        in_specs=[in_vmem()] * 3,
        out_specs=[in_vmem()] * 2,
        out_shape=[
            pltpu.VMEM((2, count, channels, width), jnp.bfloat16),
            pltpu.VMEM((AR, channels, width), jnp.bfloat16),
        ],
        compiler_params=vmem(16),
        name="own_mixing_grad",
    )(maps, lags, grads)


def mixing_grad_kernel(which, maps0, maps1, lags, grads, own, own_lags, out):
    def total(values, mine):
        values = product(values.reshape(-1, values.shape[-1]), grads[...])
        return (values + mine.reshape(values.shape).astype(jnp.float32)).astype(out.dtype)

    channels = lags.shape[1]
    done = 0
    for maps in (maps0, maps1):

        def chunk(index, _, maps=maps, done=done):
            part, place = (pl.ds(start + index * CHUNK, CHUNK) for start in (0, done))
            rows = CHUNK * channels
            start = pl.multiple_of(done * channels + index * rows, rows)
            out[pl.ds(start, rows), :] = total(maps[which, part], own[which, place])

        lax.fori_loop(0, maps.shape[1] // CHUNK, chunk, None)
        done += maps.shape[1]
    if which:
        out[done * channels :, :] = total(lags[...], own_lags[...])


def mixing_grad(which, maps, lags, grads, own, own_lags):
    channels = lags.shape[1]
    count = own.shape[1]
    shape = ((count + which * AR) * channels, grads.shape[1])
    return pl.pallas_call(
        functools.partial(mixing_grad_kernel, which),
        in_specs=[in_vmem()] * 6,
        out_specs=in_vmem(),
        out_shape=pltpu.VMEM(shape, jnp.bfloat16),
        compiler_params=vmem(16),
        name="mixing_grad",
    )(*maps, lags, grads, own, own_lags)


def finish_mixing_kernel(part, got, *refs):
    out = refs[-1]
    rows = out.shape[0] * out.shape[1]
    own = pl.ds(pl.multiple_of(pl.program_id(0) * rows, rows), rows)
    out[...] = (part[own, :].astype(jnp.float32) + got[own, :].astype(jnp.float32)).reshape(out.shape)


def finish_mixing(part, got, first, total, into=None):
    channels = total[1]
    count = part.shape[0] // channels
    steps = 3
    size = count // steps
    given = [] if into is None else [into]
    return pl.pallas_call(
        finish_mixing_kernel,
        grid=(steps,),
        in_specs=[in_vmem(), in_vmem(), *[pl.BlockSpec(memory_space=pl.ANY) for _ in given]],
        out_specs=pl.BlockSpec(
            tuple(map(pl.Element, (size, *total[1:]))), lambda k: (first + k * size, 0, 0)
        ),
        out_shape=jax.ShapeDtypeStruct(total, jnp.float32),
        input_output_aliases={2: 0} if given else {},
        compiler_params=vmem(16),
        name="finish_mixing",
    )(part, got, *given)


def unit_rows(width, units):
    blocks = width // units // 2
    return [width + units * i for i in range(blocks)], width + units * blocks + 16


def unit_grads_kernel(channels, me, *refs):
    *parts, gate, up, down, first_gain, out, normed, cotangent = refs
    place_tokens(me[0], parts[:4], normed)
    place_tokens(me[0], parts[4:], cotangent)
    width, units = gate.shape[0], out.shape[2]
    mine = pl.ds(pl.multiple_of(me[0] * units, units), units)
    hidden_grad = contract_last(cotangent[...], down[mine, :])
    gate_value = product(normed[...], gate[:, mine])
    upper_value = product(normed[...], up[:, mine])
    hidden, gate_back, upper_back = gelu_parts(gate_value, upper_value, hidden_grad)
    gate_part = contract_first(normed[...], gate_back.astype(jnp.bfloat16))
    up_part = contract_first(normed[...], upper_back.astype(jnp.bfloat16))
    down_part = contract_first(hidden.astype(jnp.bfloat16), cotangent[...]).astype(jnp.bfloat16)
    starts, size = unit_rows(width, units)
    out[0, :width] = gate_part.astype(jnp.bfloat16)
    out[1, :width] = up_part.astype(jnp.bfloat16)
    for i in range(2 * len(starts)):
        half, start = i // len(starts), starts[i % len(starts)]
        out[half, start : start + units] = down_part[:, i * units : (i + 1) * units]
    second = jnp.zeros((16, width), jnp.float32)
    for part in parts[2:4]:
        for a in range(2):
            for r in range(part.shape[1]):
                second = second + part[a, r, -16:, :].astype(jnp.float32)
    second = second[:8] + second[8:]
    second = pltpu.roll(second, lax.rem(width - me[0] * channels, width), 1)
    out[0, size - 16 :] = jnp.zeros((16, units), jnp.bfloat16)
    out[1, size - 16 :] = jnp.zeros((16, units), jnp.bfloat16)
    lanes = first_gain.shape[1]
    gains = jnp.concatenate([second[:, :lanes], first_gain[...]], axis=0)
    out[0, size - 16 :, :lanes] = gains.astype(jnp.bfloat16)


def unit_grads(me, normed_parts, cotangent_parts, w_gate, w_up, w_down, first_gain):
    width, hidden = w_gate.shape
    chans = lax.axis_size("chan")
    units = hidden // chans
    parts = [*normed_parts, *cotangent_parts]
    tokens = sum(math.prod(part.shape[:-1]) for part in cotangent_parts)
    shape = (2, unit_rows(width, units)[1], units)
    return pl.pallas_call(
        functools.partial(unit_grads_kernel, width // chans),
        grid_spec=pltpu.PrefetchScalarGridSpec(
            num_scalar_prefetch=1,
            grid=(1,),
            in_specs=[
                *[in_vmem() for _ in parts],
                *[in_vmem()] * 4,
            ],
            out_specs=in_vmem(),
            scratch_shapes=[pltpu.VMEM((tokens, width), jnp.bfloat16)] * 2,
        ),
        out_shape=pltpu.VMEM(shape, jnp.bfloat16),
        compiler_params=vmem(24),
        name="unit_grads",
    )(me, *parts, w_gate, w_up, w_down, first_gain)


def finish_units_kernel(core, mine, other, gate, up, down, gains):
    width, units = gate.shape
    starts, size = unit_rows(width, units)
    for which, (low, high) in enumerate(((mine, other), (other, mine))):

        @pl.when(core[0] == which)
        def _(low=low, high=high):
            gate[...] = low[:width].astype(jnp.float32)
            up[...] = high[:width].astype(jnp.float32)
            for i in range(2 * len(starts)):
                source, start = (low, high)[i // len(starts)], starts[i % len(starts)]
                part = source[start : start + units].astype(jnp.float32)
                down[:, i * units : (i + 1) * units] = part
            gains[...] = low[size - 16 :].astype(jnp.float32)


def finish_units(core, mine, other, width):
    units = mine.shape[1]
    shapes = [(width, units), (width, units), (units, width), (16, units)]
    return pl.pallas_call(
        finish_units_kernel,
        grid_spec=pltpu.PrefetchScalarGridSpec(
            num_scalar_prefetch=1,
            grid=(1,),
            in_specs=[in_vmem()] * 2,
            out_specs=[whole(shape) for shape in shapes],
        ),
        out_shape=[jax.ShapeDtypeStruct(shape, jnp.float32) for shape in shapes],
        compiler_params=vmem(16),
        name="finish_units",
    )(core, mine, other)


def swap(values, axis, mask):
    count = lax.axis_size(axis)
    return lax.ppermute(values, axis, [(i, i ^ mask) for i in range(count)])


def bits_of(axis):
    return [1 << b for b in range(lax.axis_size(axis).bit_length() - 1)]


def entry(values, index, dim):
    return lax.dynamic_slice_in_dim(values, index, 1, dim, allow_negative_indices=False)


def join(mine, other, high, dim):
    return jnp.where(
        high, jnp.concatenate([other, mine], dim), jnp.concatenate([mine, other], dim)
    )


def tie(*values):
    return lax.optimization_barrier(values)


def gather_round(held, mask, bits, came=None):
    came = swap(held, "chan", mask) if came is None else came
    return join(held[None], came[None], bits[mask][2], 0)


class Gather:
    def __init__(self, values, halves, bits):
        masks = bits_of("chan")
        self.bits = bits
        self.shape = values.shape
        self.common = masks[2:]
        self.orders = [(masks[1], masks[0]), (masks[0], masks[1])][:halves]
        self.held = values[None]

    def first(self, came=None):
        for mask in self.common:
            self.held = gather_round(self.held, mask, self.bits, came).reshape(-1, *self.shape)
            came = None
        return self.held

    def second(self):
        self.halves = [self.held]
        if len(self.orders) == 2:
            half = self.shape[0] // 32 * 16
            self.halves = [self.held[:, :half], self.held[:, half:]]
        self.halves = [
            gather_round(h, order[0], self.bits)
            for h, order in zip(self.halves, self.orders, strict=True)
        ]
        return self.halves

    def third(self):
        self.others = [
            swap(h, "chan", order[1]) for h, order in zip(self.halves, self.orders, strict=True)
        ]
        return self.others

    def parts(self):
        return [part for pair in zip(self.halves, self.others, strict=True) for part in pair]


def add(left, right):
    return left.astype(jnp.float32) + right.astype(jnp.float32)


def own_entry(values, mask, dim, bits):
    return add(*exchange(values, mask, dim, bits)).squeeze(dim)


def exchange_rest(kept, came):
    count = 2 * kept.shape[0]
    held = jnp.stack([kept, came], axis=1).reshape(count, *kept.shape[1:])
    for mask in bits_of("chan")[1:]:
        split = held.reshape(-1, 2, mask, *held.shape[1:])
        kept, came = split[:, 0], swap(split[:, 1], "chan", mask)
        held = jnp.stack([kept, came], axis=1).reshape(held.shape)
    return kept.reshape(count // 2, *held.shape[1:]), came.reshape(count // 2, *held.shape[1:])


def exchange(values, mask, dim, bits):
    keep, give = (entry(values, bit, dim) for bit in bits[mask][:2])
    return keep, swap(give, "chan", mask)


def scatter_tokens(keep0, give0, keep1, give1, bits, beside):
    masks = bits_of("chan")
    got0, got1 = swap(give0, "chan", masks[0]), swap(give1, "chan", masks[1])
    half0 = add(keep0, got0).astype(jnp.bfloat16)
    half1 = add(keep1, got1).astype(jnp.bfloat16)
    half0, half1 = beside(half0, half1)
    half0 = own_entry(half0, masks[1], 1, bits)
    half1 = own_entry(half1, masks[0], 1, bits)
    held = jnp.concatenate([half0, half1], axis=1)
    for mask in masks[:2:-1]:
        held = held.astype(jnp.bfloat16).reshape(2, -1, *held.shape[1:])
        held = own_entry(held, mask, 0, bits)
    return held.astype(jnp.bfloat16)


def shards(
    hidden_in, segments, filters, gain_one, mixing, gain_two, w_gate, w_up, w_down, out_grad
):
    chans = lax.axis_size("chan")
    me = lax.axis_index("chan").astype(jnp.int32)
    at = me.reshape(1)
    _, share, width = hidden_in.shape
    channels = width // chans
    core = lax.axis_index("rows").astype(jnp.int32) & 1
    other_core = 1 - core
    bits = [(me >> b) & 1 for b in range(len(bits_of("chan")))]
    bits = [value for bit in bits for value in (bit, bit ^ 1, bit != 0)]
    hidden_in, at, core, other_core, *bits = tie(hidden_in, at, core, other_core, *bits)
    bits = {mask: bits[3 * i : 3 * i + 3] for i, mask in enumerate(bits_of("chan"))}
    pieces = lax.all_to_all(
        first_norm(at, hidden_in, gain_one, segments, chans),
        "chan",
        split_axis=0,
        concat_axis=0,
    )
    pieces, cotangent = tie(pieces, out_grad)
    cotangent_gather = Gather(cotangent[0], 2, bits)
    came = swap(cotangent_gather.held, "chan", 4)
    maps, lags, *cut = spectral_mixed(at, pieces, filters, mixing)
    pieces, lags, came = tie(pieces, lags, came)
    cotangent_gather.first(came)
    peer_pieces = swap(pieces, "rows", 2)

    def beside(*values):
        *values, cotangent_gather.held = tie(*values, cotangent_gather.held)
        cotangent_gather.second()
        return values

    held = scatter_tokens(*cut, bits, beside)
    held, peer_pieces, *cotangent_gather.halves = tie(
        held, peer_pieces, *cotangent_gather.halves
    )
    got = exchange(held, 4, 0, bits)[1][0]
    first_maps, peer_lags = spectral_maps(peer_pieces, filters, channels, 0, K // 2)
    held, got, first_maps = tie(held, got, first_maps)
    cotangent_gather.third()
    output, normed_two, resid_grad, resid_low = feed_forward(
        bits[4][0].reshape(1), held, got, hidden_in, gain_two, out_grad, w_gate, w_up, w_down
    )
    grad_gather = Gather(resid_low, 2, bits)
    first, *cotangent_gather.others = tie(grad_gather.first(), *cotangent_gather.others)
    peer_pieces, resid_grad = tie(peer_pieces, resid_grad)
    second_maps, _ = spectral_maps(peer_pieces, filters, channels, K // 2, K // 2)
    grad_gather.held, second_maps = tie(first, second_maps)
    peer_maps = (first_maps, second_maps)
    grad_gather.second()
    normed_two, *grad_gather.halves = tie(normed_two, *grad_gather.halves)
    grad_gather.third()
    normed_gather = Gather(normed_two, 2, bits)
    normed_gather.first()
    full_grad = place(at, grad_gather.parts())
    peer_grad = swap(full_grad, "rows", 2)
    normed_gather.second()
    acc = spectral_back(full_grad, mixing, filters, pieces, 0, K // 2)
    acc, *normed_gather.halves = tie(acc, *normed_gather.halves)
    normed_gather.third()
    acc = spectral_back(full_grad, mixing, filters, pieces, K // 2, K // 2, acc)
    back, give, first_local = lag_back(at, acc, mixing, full_grad, lags, pieces, gain_one)
    came = swap(give, "chan", 1)
    first_local, *normed_parts = tie(first_local, *normed_gather.parts())
    unit_parts = unit_grads(
        at, normed_parts, cotangent_gather.parts(), w_gate, w_up, w_down, first_local
    )
    unit_parts, full_grad, back, came = tie(unit_parts, full_grad, back, came)
    own, own_lags = own_mixing_grad(maps, lags, full_grad)
    back, came = exchange_rest(back, came)
    unit_given = swap(entry(unit_parts, other_core, 0)[0], "rows", 1)
    unit_half = add(entry(unit_parts, core, 0)[0], unit_given).astype(jnp.bfloat16)
    own_lags, unit_half, peer_grad = tie(own_lags, unit_half, peer_grad)
    unit_other = swap(unit_half, "rows", 2)
    first_part = mixing_grad(0, peer_maps, peer_lags, peer_grad, own, own_lags)
    first_part, peer_grad = tie(first_part, peer_grad)
    second_part = mixing_grad(1, peer_maps, peer_lags, peer_grad, own, own_lags)
    second_part, came, unit_other = tie(second_part, came, unit_other)
    input_total = first_norm_back(at, back, came, hidden_in, gain_one, resid_grad)
    unit_half = add(unit_half, unit_other).astype(jnp.bfloat16)
    for mask in bits_of("rows")[2:]:
        unit_half = add(unit_half, swap(unit_half, "rows", mask)).astype(jnp.bfloat16)
    unit_other = swap(unit_half, "rows", 1)
    mixing_sum = None
    for part, first in ((first_part, 0), (second_part, K)):
        masks = [1, *bits_of("rows")[2:]]
        for mask in masks[:-1]:
            part = add(part, swap(part, "rows", mask)).astype(jnp.bfloat16)
        got = swap(part, "rows", masks[-1])
        mixing_sum = finish_mixing(part, got, first, mixing.shape, mixing_sum)
        if not first:
            mixing_sum, unit_half = tie(mixing_sum, unit_half)
    gate_sum, up_sum, down_sum, gains = finish_units(
        core.reshape(1), unit_half, unit_other, width
    )
    return (
        output,
        input_total,
        mixing_sum,
        gate_sum,
        up_sum,
        down_sum,
        gains[8, :channels],
        gains[0, :channels],
    )


def solution(mesh):
    in_specs = (
        P("rows", "chan", None),
        P("rows", None),
        P(),
        P(),
        P(None, "chan", None),
        P(),
        P(),
        P(),
        P(),
        P("rows", "chan", None),
    )
    out_specs = (
        P("rows", "chan", None),
        P("rows", "chan", None),
        P(None, "chan", None),
        P(None, "chan"),
        P(None, "chan"),
        P("chan", None),
        P("chan"),
        P("chan"),
    )
    return jax.shard_map(shards, mesh=mesh, in_specs=in_specs, out_specs=out_specs, check_vma=False)
```

```python
import functools
import math

import jax
import jax.numpy as jnp
from jax import lax
from jax.experimental import pallas as pl
from jax.experimental.pallas import tpu as pltpu
from jax.sharding import PartitionSpec as P

K = 24
AR = 3
TILE = 256
HALF = 128
PER_STEP = 12
FEED_STEPS = 2

eps_norm = 1e-05


def rms_scale(values, scales):
    return values * lax.rsqrt(jnp.mean(values * values, axis=-1, keepdims=True) + eps_norm) * scales


def contract_first(left, right):
    return lax.dot_general(
        left, right, (((0,), (0,)), ((), ())), preferred_element_type=jnp.float32
    )


def contract_last(left, right):
    return lax.dot_general(
        left, right, (((1,), (1,)), ((), ())), preferred_element_type=jnp.float32
    )


def product(left, right):
    return jnp.dot(left, right, preferred_element_type=jnp.float32)


def in_hbm(value):
    return pltpu.with_memory_space_constraint(value, pltpu.HBM)


def in_vmem():
    return pl.BlockSpec(memory_space=pltpu.VMEM)


def whole(shape):
    return pl.BlockSpec(shape, lambda *_: (0,) * len(shape))


def vmem(mebibytes):
    return pltpu.CompilerParams(vmem_limit_bytes=mebibytes << 20)


def first_norm_kernel(me, hidden, gain, segments, pieces):
    count, rows, share = pieces.shape
    channels = hidden.shape[2] // count
    normed = rms_scale(hidden[0].astype(jnp.float32), gain[...])
    normed = normed.T.astype(jnp.bfloat16)
    ids = segments[:, pl.ds(pl.multiple_of(me[0] * share, share), share)]
    ids = jnp.broadcast_to(ids.astype(jnp.float32), (rows - channels, share)).astype(jnp.bfloat16)
    for i in range(count):
        pieces[i, :channels, :] = normed[i * channels : (i + 1) * channels]
        pieces[i, channels:, :] = ids


def first_norm(me, hidden_in, gain, segments, count):
    _, share, width = hidden_in.shape
    shape = (count, width // count + 16, share)
    return pl.pallas_call(
        first_norm_kernel,
        grid_spec=pltpu.PrefetchScalarGridSpec(
            num_scalar_prefetch=1,
            grid=(1,),
            in_specs=[whole(hidden_in.shape), whole((1, width)), whole(segments.shape)],
            out_specs=whole(shape),
        ),
        out_shape=jax.ShapeDtypeStruct(shape, jnp.bfloat16),
        compiler_params=vmem(8),
        name="first_norm",
    )(me, in_hbm(hidden_in), in_hbm(gain[None, :]), in_hbm(segments))


def first_norm_back_kernel(me, kept, came, hidden, gain, grad, out):
    half, channels, share = kept.shape
    parts = []
    for i in range(2 * half):
        other = i ^ me[0]
        pick = jnp.where(other < half, kept[other % half], came[other % half])
        parts.append(pick.astype(jnp.float32))
    normed_grad = jnp.concatenate(parts, axis=0).T
    tokens = hidden[0].astype(jnp.float32)
    scale = lax.rsqrt(jnp.mean(tokens * tokens, axis=-1, keepdims=True) + eps_norm)
    weighed = normed_grad * gain[...]
    along = jnp.mean(weighed * tokens, axis=-1, keepdims=True)
    out[0] = grad[...] + scale * (weighed - tokens * (scale * scale * along))


def first_norm_back(me, kept, came, hidden_in, gain, grad):
    _, share, width = hidden_in.shape
    return pl.pallas_call(
        first_norm_back_kernel,
        grid_spec=pltpu.PrefetchScalarGridSpec(
            num_scalar_prefetch=1,
            grid=(1,),
            in_specs=[in_vmem()] * 5,
            out_specs=whole(hidden_in.shape),
        ),
        out_shape=jax.ShapeDtypeStruct(hidden_in.shape, jnp.float32),
        compiler_params=vmem(8),
        name="first_norm_back",
    )(me, kept, came, hidden_in, gain[None, :], grad)


def tile_pairs(length):
    blocks, reach = length // TILE, length // 2 // TILE
    return [(tb, sb) for tb in range(blocks) for sb in range(max(0, tb - reach), tb + 1)]


def slab_width(length):
    return length // 2 + TILE


def parity_lanes(rows, lanes, dtype=jnp.float32):
    lane = lax.broadcasted_iota(jnp.int32, (rows, lanes), 1)
    return (1 - 2 * (lane % 2)).astype(dtype)


def block(index):
    return slice(index * TILE, (index + 1) * TILE)


def segment_row(pieces):
    row = pieces.shape[1] - 8
    return jnp.concatenate(
        [pieces[i, row:, :].astype(jnp.float32) for i in range(pieces.shape[0])], axis=1
    )


def build_masks(ids, masks, length, targets_in_rows):
    row = lax.broadcasted_iota(jnp.int32, (TILE, TILE), 0)
    col = lax.broadcasted_iota(jnp.int32, (TILE, TILE), 1)
    in_lanes = [jnp.broadcast_to(ids[:1, block(b)], (TILE, TILE)) for b in range(length // TILE)]
    in_rows = [value.T for value in in_lanes]
    for index, (tb, sb) in enumerate(tile_pairs(length)):
        rows_of, lanes_of = (tb, sb) if targets_in_rows else (sb, tb)
        same = in_rows[rows_of] == in_lanes[lanes_of]
        if tb == sb:
            same = same & ((row >= col) if targets_in_rows else (col >= row))
        masks[index] = jnp.where(same, 1.0, 0.0).astype(jnp.bfloat16)


def lag_keep(ids, lag):
    lane = lax.broadcasted_iota(jnp.int32, ids.shape, 1)
    same = (pltpu.roll(ids, lag, 1) == ids) & (lane >= lag)
    return jnp.where(same, 1.0, 0.0)[:1]


def build_slab(taps, slab, width):
    rolled = pltpu.roll(jnp.broadcast_to(taps, (HALF, width)), 0, 1, stride=1, stride_axis=0)
    rolled = rolled.astype(jnp.bfloat16)
    slab[:HALF, :] = rolled
    slab[HALF:, HALF:] = rolled[:, : width - HALF]
    slab[HALF:, :HALF] = rolled[:, :HALF]


def start_maps(filters, pieces, lags, taps, masks, doubled):
    count, _, share = pieces.shape
    channels, length = lags.shape[1:]
    ids = segment_row(pieces)
    build_masks(ids, masks, length, False)
    taps[...] = filters[:, : taps.shape[1]].astype(jnp.float32)
    sign = parity_lanes(channels, share, jnp.bfloat16)
    for i in range(count):
        part = pieces[i, :channels, :]
        doubled[:channels, i * share : (i + 1) * share] = part
        doubled[channels:, i * share : (i + 1) * share] = part * sign
    inputs = doubled[:channels, :]
    lags[0] = inputs
    inputs = inputs.astype(jnp.float32)
    for j in range(1, AR):
        lags[j] = (pltpu.roll(inputs, j, 1) * lag_keep(ids, j)).astype(jnp.bfloat16)


def step_maps(first, place, maps, taps, slabs, masks, doubled):
    channels, length = maps.shape[2:]
    width = taps.shape[1]
    pairs = tile_pairs(length)
    parity = parity_lanes(channels, TILE)
    for k in range(slabs.shape[0]):
        slab = slabs.at[k]
        build_slab(taps[pl.ds(first + k, 1), :], slab, width)
        for tb in range(length // TILE):
            chosen = [(i, sb) for i, (t, sb) in enumerate(pairs) if t == tb]
            tiles = [slab[:, block(tb - sb)] * masks[i] for i, sb in chosen]
            low = chosen[0][1]
            both = product(
                doubled[:, low * TILE : (tb + 1) * TILE], jnp.concatenate(tiles, axis=0)
            )
            maps[0, place + k, :, block(tb)] = both[:channels].astype(jnp.bfloat16)
            maps[1, place + k, :, block(tb)] = (both[channels:] * parity).astype(jnp.bfloat16)


def maps_kernel(start, filters, pieces, maps, lags, taps, slabs, masks, doubled):
    start_maps(filters, pieces, lags, taps, masks, doubled)
    step_maps(start, 0, maps, taps, slabs, masks, doubled)


def mixed_kernel(
    me,
    filters,
    pieces,
    mixing_given,
    maps,
    lags,
    keep0,
    give0,
    keep1,
    give1,
    taps,
    slabs,
    masks,
    doubled,
    acc,
    mixing,
    arrived,
):
    _, _, model_width = mixing.shape
    count, _, share = pieces.shape
    filter_count, length = maps.shape[1], lags.shape[2]
    step = pl.program_id(0)

    copy = pltpu.make_async_copy(mixing_given, mixing, arrived)

    @pl.when(step == 0)
    def _():
        copy.start()
        start_maps(filters, pieces, lags, taps, masks, doubled)
        acc[...] = jnp.zeros_like(acc)

    step_maps(step * PER_STEP, step * PER_STEP, maps, taps, slabs, masks, doubled)

    @pl.when(step == 0)
    def _():
        copy.wait()

    def part(weights, values):
        return contract_first(weights.reshape(-1, model_width), values.reshape(-1, length))

    plus = pl.ds(step * PER_STEP, PER_STEP)
    minus = pl.ds(filter_count + step * PER_STEP, PER_STEP)
    total = part(mixing[plus], maps[0, plus]) + part(mixing[minus], maps[1, plus])
    for i in range(count):
        acc[i] += total[:, i * share : (i + 1) * share]

    @pl.when(step == pl.num_programs(0) - 1)
    def _():
        last = part(mixing[2 * filter_count :], lags[...])
        for i in range(count):
            acc[i] += last[:, i * share : (i + 1) * share]
        half = model_width // 2
        low, near = me[0] & 1, (me[0] >> 1) & 1
        for r in range(count // 4):
            for a in range(2):
                for other, (out0, out1) in enumerate(((keep0, keep1), (give0, give1))):
                    out0[r, a] = acc[r * 4 + a * 2 + (low ^ other), :half].astype(jnp.bfloat16)
                    out1[r, a] = acc[r * 4 + (near ^ other) * 2 + a, half:].astype(jnp.bfloat16)


def place_tokens(me, parts, out):
    low, near = me & 1, (me >> 1) & 1
    halves = len(parts) // 2
    rest = parts[0].shape[1]
    rows = out.shape[0] // (4 * rest * halves)
    for index, part in enumerate(parts):
        half, other = index // 2, index % 2
        for a in range(2):
            for r in range(rest):
                if half == 0:
                    owner = r * 4 + a * 2 + (low ^ other)
                else:
                    owner = r * 4 + (near ^ other) * 2 + a
                start = pl.multiple_of((owner * halves + half) * rows, rows)
                out[pl.ds(start, rows), :] = part[a, r, :rows, :]


def place_kernel(me, *refs):
    place_tokens(me[0], refs[:-1], refs[-1])


def place(me, parts):
    count = sum(math.prod(part.shape[:-1]) for part in parts)
    shape = (count, parts[0].shape[-1])
    return pl.pallas_call(
        place_kernel,
        grid_spec=pltpu.PrefetchScalarGridSpec(
            num_scalar_prefetch=1,
            grid=(1,),
            in_specs=[in_vmem()] * 4,
            out_specs=in_vmem(),
        ),
        out_shape=pltpu.VMEM(shape, jnp.bfloat16),
        compiler_params=vmem(8),
        name="place",
    )(me, *parts)


def spectral_back_kernel(start, filters, mixing, pieces, grads, *refs):
    *before, acc, taps, slabs, masks, both = refs
    _, channels, model_width = mixing.shape
    count = filters.shape[0]
    length, width = acc.shape[1], taps.shape[1]
    reach = length // 2
    pairs = tile_pairs(length)
    some = slabs.shape[0]
    rows = some * channels
    build_masks(segment_row(pieces), masks, length, True)
    source = lax.broadcasted_iota(jnp.int32, (width, width), 0)
    target = lax.broadcasted_iota(jnp.int32, (width, width), 1)
    flip = jnp.where(source + target == reach, 1.0, 0.0).astype(jnp.bfloat16)
    taps[...] = product(filters[:, :width], flip)
    sign = parity_lanes(rows, length, jnp.bfloat16)

    def by_map(first):
        weights = mixing[first : first + some].reshape(rows, model_width)
        return contract_last(weights, grads[...]).astype(jnp.bfloat16)

    both[:, :channels, :] = by_map(start).reshape(some, channels, length)
    both[:, channels:, :] = (by_map(count + start) * sign).reshape(some, channels, length)
    for k in range(some):
        build_slab(taps[start + k : start + k + 1, :], slabs.at[k], width)
    for sb in range(length // TILE):
        chosen = [(i, tb) for i, (tb, s) in enumerate(pairs) if s == sb]
        last = chosen[-1][1]
        total = before[0][:, block(sb)] if before else jnp.zeros((2 * channels, TILE), jnp.float32)
        for k in range(some):
            tiles = []
            for i, tb in chosen:
                place = reach - (tb - sb) * TILE
                tiles.append(slabs[k, :, place : place + TILE] * masks[i])
            total = total + product(
                both[k, :, sb * TILE : (last + 1) * TILE], jnp.concatenate(tiles, axis=0)
            )
        acc[:, block(sb)] = total


def lag_back_kernel(me, acc, mixing, grads, inputs, pieces, scales, kept, given, gain):
    _, channels, model_width = mixing.shape
    length = acc.shape[1]
    half, _, share = kept.shape
    ids = segment_row(pieces)
    lag_grad = contract_last(mixing[2 * K :].reshape(AR * channels, model_width), grads[...])
    total = acc[:channels] + parity_lanes(channels, length) * acc[channels:]
    for j in range(AR):
        term = lag_grad[j * channels : (j + 1) * channels]
        if j:
            term = pltpu.roll(term * lag_keep(ids, j), length - j, 1)
        total = total + term
    back = total.astype(jnp.bfloat16)
    for i in range(2 * half):
        part = back[:, i * share : (i + 1) * share]
        other = i ^ me[0]
        place = other >> 1

        @pl.when((other & 1) == 0)
        def _(part=part, place=place):
            kept[place] = part

        @pl.when((other & 1) == 1)
        def _(part=part, place=place):
            given[place] = part

    weighed = back.astype(jnp.float32) * inputs[0].astype(jnp.float32)
    by_lane = jnp.broadcast_to(jnp.sum(weighed, axis=1, keepdims=True), (channels, 128))
    row = lax.broadcasted_iota(jnp.int32, by_lane.shape, 0)
    lane = lax.broadcasted_iota(jnp.int32, by_lane.shape, 1)
    total = jnp.sum(jnp.where(row == lane, by_lane, 0.0), axis=0, keepdims=True)
    width = scales.shape[1]
    turned = jnp.broadcast_to(scales[...], (8, width))
    turned = pltpu.roll(turned, lax.rem(width - me[0] * channels, width), 1)
    gain[...] = jnp.broadcast_to(total, gain.shape) / turned[:, :128]


def toeplitz_scratch(length, count, slabs):
    width = slab_width(length)
    return [
        pltpu.VMEM((count, width), jnp.float32),
        pltpu.VMEM((slabs, TILE, width), jnp.bfloat16),
        pltpu.VMEM((len(tile_pairs(length)), TILE, TILE), jnp.bfloat16),
    ]


def maps_scratch(channels, length, count, slabs):
    return [
        *toeplitz_scratch(length, count, slabs),
        pltpu.VMEM((2 * channels, length), jnp.bfloat16),
    ]


def spectral_maps(pieces, filters, channels, start, count):
    length = filters.shape[1]
    return pl.pallas_call(
        functools.partial(maps_kernel, start),
        in_specs=[in_vmem()] * 2,
        out_specs=[in_vmem()] * 2,
        out_shape=[
            pltpu.VMEM((2, count, channels, length), jnp.bfloat16),
            pltpu.VMEM((AR, channels, length), jnp.bfloat16),
        ],
        scratch_shapes=maps_scratch(channels, length, filters.shape[0], count),
        compiler_params=vmem(12 + length // 128),
        cost_estimate=pl.CostEstimate(
            flops=6 * channels * count * length * length, transcendentals=0, bytes_accessed=4 << 20
        ),
        name="spectral_maps",
    )(filters, pieces)


def spectral_mixed(me, pieces, filters, mixing):
    owners, _, share = pieces.shape
    channels, model_width = mixing.shape[1:]
    count, length = filters.shape
    cut = (owners // 4, 2, model_width // 2, share)
    return pl.pallas_call(
        mixed_kernel,
        grid_spec=pltpu.PrefetchScalarGridSpec(
            num_scalar_prefetch=1,
            grid=(count // PER_STEP,),
            in_specs=[
                whole(filters.shape),
                in_vmem(),
                pl.BlockSpec(memory_space=pltpu.HBM),
            ],
            out_specs=[in_vmem()] * 6,
            scratch_shapes=[
                *maps_scratch(channels, length, count, PER_STEP),
                pltpu.VMEM((owners, model_width, share), jnp.float32),
                pltpu.VMEM(mixing.shape, jnp.bfloat16),
                pltpu.SemaphoreType.DMA,
            ],
        ),
        out_shape=[
            pltpu.VMEM((2, count, channels, length), jnp.bfloat16),
            pltpu.VMEM((AR, channels, length), jnp.bfloat16),
            *[pltpu.VMEM(cut, jnp.bfloat16)] * 4,
        ],
        compiler_params=vmem(12 + length // 128),
        name="spectral_mixed",
    )(me, in_hbm(filters), pieces, in_hbm(mixing))


def spectral_back(grads, mixing, filters, pieces, start, some, *before):
    channels = mixing.shape[1]
    count, length = filters.shape
    return pl.pallas_call(
        functools.partial(spectral_back_kernel, start),
        in_specs=[in_vmem() for _ in range(4 + len(before))],
        out_specs=in_vmem(),
        scratch_shapes=[
            *toeplitz_scratch(length, count, some),
            pltpu.VMEM((some, 2 * channels, length), jnp.bfloat16),
        ],
        out_shape=pltpu.VMEM((2 * channels, length), jnp.float32),
        compiler_params=vmem(12 + length // 128),
        name="spectral_back",
    )(filters, mixing, pieces, grads, *before)


def lag_back(me, acc, mixing, grads, lags, pieces, gain):
    channels = mixing.shape[1]
    owners, _, share = pieces.shape
    sent = pltpu.VMEM((owners // 2, channels, share), jnp.bfloat16)
    return pl.pallas_call(
        lag_back_kernel,
        grid_spec=pltpu.PrefetchScalarGridSpec(
            num_scalar_prefetch=1,
            grid=(1,),
            in_specs=[in_vmem()] * 6,
            out_specs=[in_vmem()] * 3,
        ),
        out_shape=[sent, sent, pltpu.VMEM((8, 128), jnp.float32)],
        compiler_params=vmem(12),
        name="lag_back",
    )(me, acc, mixing, grads, lags, pieces, gain[None, :])


def gelu_parts(gate_value, upper_value, hidden_grad):
    slope = math.sqrt(2 / math.pi)
    square = gate_value * gate_value
    tanh = jnp.tanh(slope * gate_value * (1.0 + 0.044715 * square))
    rise = 0.5 * (1.0 + tanh)
    gelu = gate_value * rise
    bend = 0.5 * slope * (1.0 - tanh * tanh) * (1.0 + 3 * 0.044715 * square)
    return (
        gelu * upper_value,
        hidden_grad * upper_value * (rise + gate_value * bend),
        hidden_grad * gelu,
    )


def feed_forward_kernel(
    bit, held, got, hidden_in, gain, cotangent, gate, up, down, output, normed_out, grad, grad_low
):
    share, width = grad.shape
    mixed = held[bit[0]].astype(jnp.float32) + got[...].astype(jnp.float32)
    resid = hidden_in[0].astype(jnp.float32) + mixed.T
    scale = lax.rsqrt(jnp.mean(resid * resid, axis=-1, keepdims=True) + eps_norm)
    normed = (resid * scale * gain[...]).astype(jnp.bfloat16)
    value, back = resid, jnp.zeros_like(resid)
    units = gate.shape[1] // FEED_STEPS
    for step in range(FEED_STEPS):
        own = slice(step * units, (step + 1) * units)
        gate_value = product(normed, gate[:, own])
        upper_value = product(normed, up[:, own])
        hidden_grad = contract_last(cotangent[0], down[own, :])
        hidden, gate_back, upper_back = gelu_parts(gate_value, upper_value, hidden_grad)
        value = value + product(hidden.astype(jnp.bfloat16), down[own, :])
        back = back + contract_last(gate_back.astype(jnp.bfloat16), gate[:, own])
        back = back + contract_last(upper_back.astype(jnp.bfloat16), up[:, own])
    output[0] = value.astype(jnp.bfloat16)
    weighed = back * gain[...]
    along = jnp.mean(weighed * resid, axis=-1, keepdims=True)
    total = scale * (weighed - resid * (scale * scale * along))
    total = cotangent[0].astype(jnp.float32) + total
    grad[...] = total
    grad_low[...] = total.astype(jnp.bfloat16)
    gains = jnp.sum(back * resid * scale, axis=0, keepdims=True)
    high = jnp.broadcast_to(gains, (16, width)).astype(jnp.bfloat16)
    low = (gains - high.astype(jnp.float32)).astype(jnp.bfloat16)
    row = lax.broadcasted_iota(jnp.int32, low.shape, 0)
    normed_out[:share, :] = normed
    normed_out[share:, :] = jnp.where(row < 8, high, low)


def feed_forward(bit, held, got, hidden_in, gain, cotangent, w_gate, w_up, w_down):
    _, share, width = hidden_in.shape
    return pl.pallas_call(
        feed_forward_kernel,
        grid_spec=pltpu.PrefetchScalarGridSpec(
            num_scalar_prefetch=1,
            grid=(1,),
            in_specs=[in_vmem()] * 8,
            out_specs=[whole(hidden_in.shape), *[in_vmem()] * 3],
        ),
        out_shape=[
            jax.ShapeDtypeStruct(hidden_in.shape, jnp.bfloat16),
            pltpu.VMEM((share + 16, width), jnp.bfloat16),
            pltpu.VMEM((share, width), jnp.float32),
            pltpu.VMEM((share, width), jnp.bfloat16),
        ],
        compiler_params=vmem(16),
        name="feed_forward",
    )(bit, held, got, hidden_in, gain[None, :], cotangent, w_gate, w_up, w_down)


CHUNK = 12


def own_mixing_grad_kernel(maps, lags, grads, out, lag_out):
    def chunk(index, _):
        own = pl.ds(index * CHUNK, CHUNK)
        for which in range(2):
            values = maps[which, own]
            total = product(values.reshape(-1, values.shape[-1]), grads[...])
            out[which, own] = total.astype(out.dtype).reshape(CHUNK, *out.shape[2:])

    lax.fori_loop(0, maps.shape[1] // CHUNK, chunk, None)
    values = lags[...].reshape(-1, lags.shape[-1])
    lag_out[...] = product(values, grads[...]).astype(out.dtype).reshape(lag_out.shape)


def own_mixing_grad(maps, lags, grads):
    _, count, channels, _ = maps.shape
    width = grads.shape[1]
    return pl.pallas_call(
        own_mixing_grad_kernel,
        in_specs=[in_vmem()] * 3,
        out_specs=[in_vmem()] * 2,
        out_shape=[
            pltpu.VMEM((2, count, channels, width), jnp.bfloat16),
            pltpu.VMEM((AR, channels, width), jnp.bfloat16),
        ],
        compiler_params=vmem(16),
        name="own_mixing_grad",
    )(maps, lags, grads)


def mixing_grad_kernel(which, maps0, maps1, lags, grads, own, own_lags, out):
    def total(values, mine):
        values = product(values.reshape(-1, values.shape[-1]), grads[...])
        return (values + mine.reshape(values.shape).astype(jnp.float32)).astype(out.dtype)

    channels = lags.shape[1]
    done = 0
    for maps in (maps0, maps1):

        def chunk(index, _, maps=maps, done=done):
            part, place = (pl.ds(start + index * CHUNK, CHUNK) for start in (0, done))
            rows = CHUNK * channels
            start = pl.multiple_of(done * channels + index * rows, rows)
            out[pl.ds(start, rows), :] = total(maps[which, part], own[which, place])

        lax.fori_loop(0, maps.shape[1] // CHUNK, chunk, None)
        done += maps.shape[1]
    if which:
        out[done * channels :, :] = total(lags[...], own_lags[...])


def mixing_grad(which, maps, lags, grads, own, own_lags):
    channels = lags.shape[1]
    count = own.shape[1]
    shape = ((count + which * AR) * channels, grads.shape[1])
    return pl.pallas_call(
        functools.partial(mixing_grad_kernel, which),
        in_specs=[in_vmem()] * 6,
        out_specs=in_vmem(),
        out_shape=pltpu.VMEM(shape, jnp.bfloat16),
        compiler_params=vmem(16),
        name="mixing_grad",
    )(*maps, lags, grads, own, own_lags)


def finish_mixing_kernel(part, got, *refs):
    out = refs[-1]
    rows = out.shape[0] * out.shape[1]
    own = pl.ds(pl.multiple_of(pl.program_id(0) * rows, rows), rows)
    out[...] = (part[own, :].astype(jnp.float32) + got[own, :].astype(jnp.float32)).reshape(out.shape)


def finish_mixing(part, got, first, total, into=None):
    channels = total[1]
    count = part.shape[0] // channels
    steps = 3
    size = count // steps
    given = [] if into is None else [into]
    return pl.pallas_call(
        finish_mixing_kernel,
        grid=(steps,),
        in_specs=[in_vmem(), in_vmem(), *[pl.BlockSpec(memory_space=pl.ANY) for _ in given]],
        out_specs=pl.BlockSpec(
            tuple(map(pl.Element, (size, *total[1:]))), lambda k: (first + k * size, 0, 0)
        ),
        out_shape=jax.ShapeDtypeStruct(total, jnp.float32),
        input_output_aliases={2: 0} if given else {},
        compiler_params=vmem(16),
        name="finish_mixing",
    )(part, got, *given)


def unit_rows(width, units):
    blocks = width // units // 2
    return [width + units * i for i in range(blocks)], width + units * blocks + 16


def unit_grads_kernel(channels, me, *refs):
    *parts, gate, up, down, first_gain, out, normed, cotangent = refs
    place_tokens(me[0], parts[:4], normed)
    place_tokens(me[0], parts[4:], cotangent)
    width, units = gate.shape[0], out.shape[2]
    mine = pl.ds(pl.multiple_of(me[0] * units, units), units)
    hidden_grad = contract_last(cotangent[...], down[mine, :])
    gate_value = product(normed[...], gate[:, mine])
    upper_value = product(normed[...], up[:, mine])
    hidden, gate_back, upper_back = gelu_parts(gate_value, upper_value, hidden_grad)
    gate_part = contract_first(normed[...], gate_back.astype(jnp.bfloat16))
    up_part = contract_first(normed[...], upper_back.astype(jnp.bfloat16))
    down_part = contract_first(hidden.astype(jnp.bfloat16), cotangent[...]).astype(jnp.bfloat16)
    starts, size = unit_rows(width, units)
    out[0, :width] = gate_part.astype(jnp.bfloat16)
    out[1, :width] = up_part.astype(jnp.bfloat16)
    for i in range(2 * len(starts)):
        half, start = i // len(starts), starts[i % len(starts)]
        out[half, start : start + units] = down_part[:, i * units : (i + 1) * units]
    second = jnp.zeros((16, width), jnp.float32)
    for part in parts[2:4]:
        for a in range(2):
            for r in range(part.shape[1]):
                second = second + part[a, r, -16:, :].astype(jnp.float32)
    second = second[:8] + second[8:]
    second = pltpu.roll(second, lax.rem(width - me[0] * channels, width), 1)
    out[0, size - 16 :] = jnp.zeros((16, units), jnp.bfloat16)
    out[1, size - 16 :] = jnp.zeros((16, units), jnp.bfloat16)
    lanes = first_gain.shape[1]
    gains = jnp.concatenate([second[:, :lanes], first_gain[...]], axis=0)
    out[0, size - 16 :, :lanes] = gains.astype(jnp.bfloat16)


def unit_grads(me, normed_parts, cotangent_parts, w_gate, w_up, w_down, first_gain):
    width, hidden = w_gate.shape
    chans = lax.axis_size("chan")
    units = hidden // chans
    parts = [*normed_parts, *cotangent_parts]
    tokens = sum(math.prod(part.shape[:-1]) for part in cotangent_parts)
    shape = (2, unit_rows(width, units)[1], units)
    return pl.pallas_call(
        functools.partial(unit_grads_kernel, width // chans),
        grid_spec=pltpu.PrefetchScalarGridSpec(
            num_scalar_prefetch=1,
            grid=(1,),
            in_specs=[
                *[in_vmem() for _ in parts],
                *[in_vmem()] * 4,
            ],
            out_specs=in_vmem(),
            scratch_shapes=[pltpu.VMEM((tokens, width), jnp.bfloat16)] * 2,
        ),
        out_shape=pltpu.VMEM(shape, jnp.bfloat16),
        compiler_params=vmem(24),
        name="unit_grads",
    )(me, *parts, w_gate, w_up, w_down, first_gain)


def finish_units_kernel(core, mine, other, gate, up, down, gains):
    width, units = gate.shape
    starts, size = unit_rows(width, units)
    for which, (low, high) in enumerate(((mine, other), (other, mine))):

        @pl.when(core[0] == which)
        def _(low=low, high=high):
            gate[...] = low[:width].astype(jnp.float32)
            up[...] = high[:width].astype(jnp.float32)
            for i in range(2 * len(starts)):
                source, start = (low, high)[i // len(starts)], starts[i % len(starts)]
                part = source[start : start + units].astype(jnp.float32)
                down[:, i * units : (i + 1) * units] = part
            gains[...] = low[size - 16 :].astype(jnp.float32)


def finish_units(core, mine, other, width):
    units = mine.shape[1]
    shapes = [(width, units), (width, units), (units, width), (16, units)]
    return pl.pallas_call(
        finish_units_kernel,
        grid_spec=pltpu.PrefetchScalarGridSpec(
            num_scalar_prefetch=1,
            grid=(1,),
            in_specs=[in_vmem()] * 2,
            out_specs=[whole(shape) for shape in shapes],
        ),
        out_shape=[jax.ShapeDtypeStruct(shape, jnp.float32) for shape in shapes],
        compiler_params=vmem(16),
        name="finish_units",
    )(core, mine, other)


def swap(values, axis, mask):
    count = lax.axis_size(axis)
    return lax.ppermute(values, axis, [(i, i ^ mask) for i in range(count)])


def bits_of(axis):
    return [1 << b for b in range(lax.axis_size(axis).bit_length() - 1)]


def entry(values, index, dim):
    return lax.dynamic_slice_in_dim(values, index, 1, dim, allow_negative_indices=False)


def join(mine, other, high, dim):
    return jnp.where(
        high, jnp.concatenate([other, mine], dim), jnp.concatenate([mine, other], dim)
    )


def tie(*values):
    return lax.optimization_barrier(values)


def gather_round(held, mask, bits, came=None):
    came = swap(held, "chan", mask) if came is None else came
    return join(held[None], came[None], bits[mask][2], 0)


class Gather:
    def __init__(self, values, halves, bits):
        masks = bits_of("chan")
        self.bits = bits
        self.shape = values.shape
        self.common = masks[2:]
        self.orders = [(masks[1], masks[0]), (masks[0], masks[1])][:halves]
        self.held = values[None]

    def first(self, came=None):
        for mask in self.common:
            self.held = gather_round(self.held, mask, self.bits, came).reshape(-1, *self.shape)
            came = None
        return self.held

    def second(self):
        self.halves = [self.held]
        if len(self.orders) == 2:
            half = self.shape[0] // 32 * 16
            self.halves = [self.held[:, :half], self.held[:, half:]]
        self.halves = [
            gather_round(h, order[0], self.bits)
            for h, order in zip(self.halves, self.orders, strict=True)
        ]
        return self.halves

    def third(self):
        self.others = [
            swap(h, "chan", order[1]) for h, order in zip(self.halves, self.orders, strict=True)
        ]
        return self.others

    def parts(self):
        return [part for pair in zip(self.halves, self.others, strict=True) for part in pair]


def add(left, right):
    return left.astype(jnp.float32) + right.astype(jnp.float32)


def own_entry(values, mask, dim, bits):
    return add(*exchange(values, mask, dim, bits)).squeeze(dim)


def exchange_rest(kept, came):
    count = 2 * kept.shape[0]
    held = jnp.stack([kept, came], axis=1).reshape(count, *kept.shape[1:])
    for mask in bits_of("chan")[1:]:
        split = held.reshape(-1, 2, mask, *held.shape[1:])
        kept, came = split[:, 0], swap(split[:, 1], "chan", mask)
        held = jnp.stack([kept, came], axis=1).reshape(held.shape)
    return kept.reshape(count // 2, *held.shape[1:]), came.reshape(count // 2, *held.shape[1:])


def exchange(values, mask, dim, bits):
    keep, give = (entry(values, bit, dim) for bit in bits[mask][:2])
    return keep, swap(give, "chan", mask)


def scatter_tokens(keep0, give0, keep1, give1, bits, beside):
    masks = bits_of("chan")
    got0, got1 = swap(give0, "chan", masks[0]), swap(give1, "chan", masks[1])
    half0 = add(keep0, got0).astype(jnp.bfloat16)
    half1 = add(keep1, got1).astype(jnp.bfloat16)
    half0, half1 = beside(half0, half1)
    half0 = own_entry(half0, masks[1], 1, bits)
    half1 = own_entry(half1, masks[0], 1, bits)
    held = jnp.concatenate([half0, half1], axis=1)
    for mask in masks[:2:-1]:
        held = held.astype(jnp.bfloat16).reshape(2, -1, *held.shape[1:])
        held = own_entry(held, mask, 0, bits)
    return held.astype(jnp.bfloat16)


def shards(
    hidden_in, segments, filters, gain_one, mixing, gain_two, w_gate, w_up, w_down, out_grad
):
    chans = lax.axis_size("chan")
    me = lax.axis_index("chan").astype(jnp.int32)
    at = me.reshape(1)
    _, share, width = hidden_in.shape
    channels = width // chans
    core = lax.axis_index("rows").astype(jnp.int32) & 1
    other_core = 1 - core
    bits = [(me >> b) & 1 for b in range(len(bits_of("chan")))]
    bits = [value for bit in bits for value in (bit, bit ^ 1, bit != 0)]
    hidden_in, at, core, other_core, *bits = tie(hidden_in, at, core, other_core, *bits)
    bits = {mask: bits[3 * i : 3 * i + 3] for i, mask in enumerate(bits_of("chan"))}
    pieces = lax.all_to_all(
        first_norm(at, hidden_in, gain_one, segments, chans),
        "chan",
        split_axis=0,
        concat_axis=0,
    )
    pieces, cotangent = tie(pieces, out_grad)
    cotangent_gather = Gather(cotangent[0], 2, bits)
    came = swap(cotangent_gather.held, "chan", 4)
    maps, lags, *cut = spectral_mixed(at, pieces, filters, mixing)
    pieces, lags, came = tie(pieces, lags, came)
    cotangent_gather.first(came)
    peer_pieces = swap(pieces, "rows", 2)

    def beside(*values):
        *values, cotangent_gather.held = tie(*values, cotangent_gather.held)
        cotangent_gather.second()
        return values

    held = scatter_tokens(*cut, bits, beside)
    held, peer_pieces, *cotangent_gather.halves = tie(
        held, peer_pieces, *cotangent_gather.halves
    )
    got = exchange(held, 4, 0, bits)[1][0]
    first_maps, peer_lags = spectral_maps(peer_pieces, filters, channels, 0, K // 2)
    held, got, first_maps = tie(held, got, first_maps)
    cotangent_gather.third()
    output, normed_two, resid_grad, resid_low = feed_forward(
        bits[4][0].reshape(1), held, got, hidden_in, gain_two, out_grad, w_gate, w_up, w_down
    )
    grad_gather = Gather(resid_low, 2, bits)
    first, *cotangent_gather.others = tie(grad_gather.first(), *cotangent_gather.others)
    peer_pieces, resid_grad = tie(peer_pieces, resid_grad)
    second_maps, _ = spectral_maps(peer_pieces, filters, channels, K // 2, K // 2)
    grad_gather.held, second_maps = tie(first, second_maps)
    peer_maps = (first_maps, second_maps)
    grad_gather.second()
    normed_two, *grad_gather.halves = tie(normed_two, *grad_gather.halves)
    grad_gather.third()
    normed_gather = Gather(normed_two, 2, bits)
    normed_gather.first()
    full_grad = place(at, grad_gather.parts())
    peer_grad = swap(full_grad, "rows", 2)
    normed_gather.second()
    acc = spectral_back(full_grad, mixing, filters, pieces, 0, K // 2)
    acc, *normed_gather.halves = tie(acc, *normed_gather.halves)
    normed_gather.third()
    acc = spectral_back(full_grad, mixing, filters, pieces, K // 2, K // 2, acc)
    back, give, first_local = lag_back(at, acc, mixing, full_grad, lags, pieces, gain_one)
    came = swap(give, "chan", 1)
    first_local, *normed_parts = tie(first_local, *normed_gather.parts())
    unit_parts = unit_grads(
        at, normed_parts, cotangent_gather.parts(), w_gate, w_up, w_down, first_local
    )
    unit_parts, full_grad, back, came = tie(unit_parts, full_grad, back, came)
    own, own_lags = own_mixing_grad(maps, lags, full_grad)
    back, came = exchange_rest(back, came)
    unit_given = swap(entry(unit_parts, other_core, 0)[0], "rows", 1)
    unit_half = add(entry(unit_parts, core, 0)[0], unit_given).astype(jnp.bfloat16)
    own_lags, unit_half, peer_grad = tie(own_lags, unit_half, peer_grad)
    unit_other = swap(unit_half, "rows", 2)
    first_part = mixing_grad(0, peer_maps, peer_lags, peer_grad, own, own_lags)
    first_part, peer_grad = tie(first_part, peer_grad)
    second_part = mixing_grad(1, peer_maps, peer_lags, peer_grad, own, own_lags)
    second_part, came, unit_other = tie(second_part, came, unit_other)
    input_total = first_norm_back(at, back, came, hidden_in, gain_one, resid_grad)
    unit_half = add(unit_half, unit_other).astype(jnp.bfloat16)
    for mask in bits_of("rows")[2:]:
        unit_half = add(unit_half, swap(unit_half, "rows", mask)).astype(jnp.bfloat16)
    unit_other = swap(unit_half, "rows", 1)
    mixing_sum = None
    for part, first in ((first_part, 0), (second_part, K)):
        masks = [1, *bits_of("rows")[2:]]
        for mask in masks[:-1]:
            part = add(part, swap(part, "rows", mask)).astype(jnp.bfloat16)
        got = swap(part, "rows", masks[-1])
        mixing_sum = finish_mixing(part, got, first, mixing.shape, mixing_sum)
        if not first:
            mixing_sum, unit_half = tie(mixing_sum, unit_half)
    gate_sum, up_sum, down_sum, gains = finish_units(
        core.reshape(1), unit_half, unit_other, width
    )
    return (
        output,
        input_total,
        mixing_sum,
        gate_sum,
        up_sum,
        down_sum,
        gains[8, :channels],
        gains[0, :channels],
    )


def solution(mesh):
    in_specs = (
        P("rows", "chan", None),
        P("rows", None),
        P(),
        P(),
        P(None, "chan", None),
        P(),
        P(),
        P(),
        P(),
        P("rows", "chan", None),
    )
    out_specs = (
        P("rows", "chan", None),
        P("rows", "chan", None),
        P(None, "chan", None),
        P(None, "chan"),
        P(None, "chan"),
        P("chan", None),
        P("chan"),
        P("chan"),
    )
    return jax.shard_map(shards, mesh=mesh, in_specs=in_specs, out_specs=out_specs, check_vma=False)
```
